256 devices in a mesh: tile: 64 (over z, x, y_hi), chan: 4 (over y_lo, core).
Axes of the slice: x: 4, y: 4 (y_hi: 2, y_lo: 2; y = y_hi * 2 + y_lo), z: 8, core: 2. Of those that a mesh axis runs over, the one named last changes fastest.
Arguments:
- features: bfloat16 [512, 64, 4096], P('tile', 'chan'), may hold values from -6 to 6
- conv_weight: bfloat16 [64, 576], P('chan'), may hold values from -0.25 to 0.25
- conv_bias: float32 [64], P('chan'), may hold values from -3 to 3
- down_weight: bfloat16 [64, 256], P(None, 'chan'), may hold values from -0.375 to 0.375
- cotangent: bfloat16 [128, 64, 4096], P('tile', 'chan'), may hold values from -0.0078125 to 0.0078125
- edge_links: int32 [512, 4], P('tile'), may hold values from 0 to 511, as said below
- edge_turns: int32 [512, 4], P('tile'), may hold values from 0 to 3
- corner_links: int32 [512, 4], P('tile'), may hold values from -1 to 511, as said below
- corner_turns: int32 [512, 4], P('tile'), may hold values from 0 to 3
- child_slot: int32 [512], P('tile'), may hold values from 0 to 511, as said below
Outputs:
- coarse: bfloat16 [128, 64, 4096], P('tile', 'chan')
- grad_conv: float32 [64, 576], P('chan')
- grad_bias: float32 [64], P('chan')
- grad_down: float32 [64, 256], P(None, 'chan')
The draws below stay inside these ranges and needn't reach their ends.
Inputs may be any that keep to these rules, and one draw needn't show every extreme that they name: `edge_links`: edge k: 0 north, 1 west, 2 south, 3 east. `corner_links`: corner k: 0 north-west, 1 south-west, 2 south-east, 3 north-east; -1 where no tile touches that corner. `child_slot`: a permutation of 0 to 511; coarse tile k lies on index k // 2 of tile; of the 8 fine tiles of one index of tile, at most 1 have their coarse tiles on any one index of tile, and that many do for some pair.
All inputs are finite; a program needn't handle non-finite values.
Results may differ from the reference program's by a relative error of at most 0.0055.
Values may be sent and summed in bfloat16 or wider, within the bound.
No kernel may reach another device: no remote copies, remote signals or barrier semaphores. Data moves between devices by JAX's collectives and lax.ppermute only.
A program may use at most 64 MiB of HBM per device.

```python
import jax
import jax.numpy as jnp
from jax import lax

C = 64
S = 64
TILE_DEV = 8
TILES = 512
COARSE = 128
N_TILE = 64


def link_table(key, offsets, with_gaps):
    keys = jax.random.split(key, 4)
    position = jnp.arange(TILES, dtype=jnp.int32)[:, None]
    jitter = jax.random.randint(keys[0], (TILES, 4), -2, 3)
    local_links = (position + jnp.array(offsets, jnp.int32)[None, :] + jitter) % TILES
    far_links = jax.random.randint(keys[1], (TILES, 4), 0, TILES)
    far_pick = jax.random.randint(keys[2], (TILES, 4), 0, 8) == 0
    links = jnp.where(far_pick, far_links, local_links)
    if with_gaps:
        gap_pick = jax.random.randint(keys[3], (TILES, 4), 0, 16) == 0
        links = jnp.where(gap_pick, -1, links)
    return links.astype(jnp.int32)


def draw_edge_links(key, part):
    return link_table(jax.random.fold_in(key, 11), [-16, -1, 16, 1], False)


def draw_corner_links(key, part):
    return link_table(jax.random.fold_in(key, 23), [-17, 15, 17, -15], True)


def draw_child_slot(key, part):
    keys = jax.random.split(jax.random.fold_in(key, 37), 4)
    group_count = min(TILE_DEV, N_TILE)
    first_perm = jax.random.permutation(keys[0], N_TILE)
    second_perm = jax.random.permutation(keys[1], N_TILE)
    offsets = jax.random.permutation(keys[2], N_TILE)[:group_count]
    local_perm = jax.random.permutation(keys[3], TILE_DEV)
    tiles_all = jnp.arange(TILES, dtype=jnp.int32)
    device = tiles_all // TILE_DEV
    within = tiles_all % TILE_DEV
    owner_index = second_perm[(first_perm[device] + offsets[within % group_count]) % N_TILE]
    return (owner_index * TILE_DEV + local_perm[within]).astype(jnp.int32)


def plant(result, key, smallest, top_value):
    longest = result.shape.index(max(result.shape))
    spots = []
    for shift in (0, 1):
        where = [jax.random.randint(jax.random.fold_in(key, axis), (), 0, length) for axis, length in enumerate(result.shape)]
        where[longest] = (where[longest] + shift) % result.shape[longest]
        spots.append(tuple(where))
    return result.at[spots[0]].set(smallest).at[spots[1]].set(top_value)


def block_levels(rng, extent, shards, smallest, top_value):
    level = 1.0
    for dim, blocks in shards:
        heights = jax.random.uniform(jax.random.fold_in(jax.random.fold_in(rng, 6), dim), (blocks,), jnp.float32, smallest / len(shards), top_value / len(shards))
        level = level * jnp.repeat(jnp.exp(heights), extent[dim] // blocks).reshape((-1,) + (1,) * (len(extent) - 1 - dim))
    return level


def bell_draw(own_key, shape, scale, bound, cuts=(), kind=jnp.bfloat16):
    entries = scale * jax.random.normal(own_key, shape, jnp.float32)
    if cuts:
        entries = entries * block_levels(own_key, shape, cuts, -0.22, 0.18)
    return jnp.clip(entries, -bound, bound).astype(kind)


def setup_inputs(seed: int = 0) -> dict:
    key_of = jax.random.split(jax.random.key(seed), 11)
    return {
        "features": bell_draw(key_of[0], (TILES, C, S * S), 1.0, 6.0, ((0, 64), (1, 4))),
        "conv_weight": bell_draw(key_of[1], (C, C * 9), (C * 9) ** -0.5, 0.25, ((0, 4),)),
        "conv_bias": bell_draw(key_of[2], (C,), 0.5, 3.0, ((0, 4),), jnp.float32),
        "down_weight": bell_draw(key_of[3], (C, C * 4), (C * 4) ** -0.5, 0.375, ((1, 4),)),
        "cotangent": bell_draw(key_of[4], (COARSE, C, S * S), (COARSE * S * S) ** -0.5, 0.0078125, ((0, 64), (1, 4))),
        "edge_links": draw_edge_links(jax.random.fold_in(key_of[10], 71), 0),
        "edge_turns": plant(jax.random.randint(key_of[6], (TILES, 4), 0, 4), jax.random.fold_in(key_of[6], 1), 0, 3).astype(jnp.int32),
        "corner_links": draw_corner_links(jax.random.fold_in(key_of[10], 71), 0),
        "corner_turns": plant(jax.random.randint(key_of[8], (TILES, 4), 0, 4), jax.random.fold_in(key_of[8], 1), 0, 3).astype(jnp.int32),
        "child_slot": draw_child_slot(jax.random.fold_in(key_of[10], 71), 0),
    }


def edge_parts(tile_grid):
    side_len = tile_grid.shape[-1]
    edge_row = side_len - 1
    rim_strips = jnp.stack([tile_grid[:, :, 0, ::-1], tile_grid[:, :, :, 0], tile_grid[:, :, edge_row, :], tile_grid[:, :, ::-1, edge_row]], axis=1)
    corners = jnp.stack([tile_grid[:, :, 0, 0], tile_grid[:, :, edge_row, 0], tile_grid[:, :, edge_row, edge_row], tile_grid[:, :, 0, edge_row]], axis=1)
    return rim_strips, corners


def pad_tiles(tile_grid, every_rim, every_corner, edge_links, edge_turns, corner_links, corner_turns):
    side_index = jnp.arange(4, dtype=jnp.int32)[None, :]
    chosen = (side_index + 2 + edge_turns) % 4
    strips = every_rim[edge_links, chosen]
    corner_pick = (side_index + 2 + corner_turns) % 4
    corner_vals = every_corner[jnp.maximum(corner_links, 0), corner_pick]
    corner_vals = jnp.where((corner_links >= 0)[:, :, None], corner_vals, jnp.zeros_like(corner_vals))
    north_row = strips[:, 0]
    west_col = strips[:, 1, :, ::-1]
    south_row = strips[:, 2, :, ::-1]
    east_col = strips[:, 3]
    upper_row = jnp.concatenate([corner_vals[:, 0, :, None], north_row, corner_vals[:, 3, :, None]], axis=-1)
    bottom = jnp.concatenate([corner_vals[:, 1, :, None], south_row, corner_vals[:, 2, :, None]], axis=-1)
    middle = jnp.concatenate([west_col[:, :, :, None], tile_grid, east_col[:, :, :, None]], axis=-1)
    return jnp.concatenate([upper_row[:, :, None, :], middle, bottom[:, :, None, :]], axis=2)


def to_patches(tile_field):
    tile_count, channel_count, side_len = tile_field.shape[0], tile_field.shape[1], tile_field.shape[2]
    half_side = side_len // 2
    blocks = tile_field.reshape(tile_count, channel_count, half_side, 2, half_side, 2).transpose(0, 1, 3, 5, 2, 4)
    return blocks.reshape(tile_count, channel_count * 4, half_side * half_side)


def from_patches(patches, channel_count, side_len):
    tile_count = patches.shape[0]
    half_side = side_len // 2
    blocks = patches.reshape(tile_count, channel_count, 2, 2, half_side, half_side).transpose(0, 1, 4, 2, 5, 3)
    return blocks.reshape(tile_count, channel_count, side_len, side_len)


def join_quarters(by_slot, side_len):
    half_side = side_len // 2
    slot_count, channel_count = by_slot.shape[0], by_slot.shape[1]
    blocks = by_slot.reshape(slot_count // 4, 2, 2, channel_count, half_side, half_side).transpose(0, 3, 1, 4, 2, 5)
    return blocks.reshape(slot_count // 4, channel_count, side_len * side_len)


def split_coarse(coarse_field, side_len):
    half_side = side_len // 2
    tile_count, channel_count = coarse_field.shape[0], coarse_field.shape[1]
    blocks = coarse_field.reshape(tile_count, channel_count, 2, half_side, 2, half_side).transpose(0, 2, 4, 1, 3, 5)
    return blocks.reshape(tile_count * 4, channel_count, half_side * half_side)


def silu_slope(pre_act):
    squashed = jax.nn.sigmoid(pre_act)
    return squashed * (1.0 + pre_act * (1.0 - squashed))


def convolve(padded, kernel):
    filters = kernel.reshape(kernel.shape[0], -1, 3, 3)
    return lax.conv_general_dilated(padded, filters, (1, 1), "VALID", dimension_numbers=("NCHW", "OIHW", "NCHW"))


def reference(features, conv_weight, conv_bias, down_weight, cotangent, edge_links, edge_turns, corner_links, corner_turns, child_slot):
    tile_grid = features.reshape(TILES, C, S, S)
    rim_strips, corners = edge_parts(tile_grid)
    fine_cot = split_coarse(cotangent, S)[child_slot]
    kernel = conv_weight.astype(jnp.float32)
    down_float = down_weight.astype(jnp.float32)

    def block_step(totals, block_index):
        grad_conv, grad_bias, grad_down = totals
        first_tile = (block_index * TILE_DEV).astype(jnp.int32)
        tiles_here = lax.dynamic_slice_in_dim(tile_grid, first_tile, TILE_DEV, 0)
        links_here = lax.dynamic_slice_in_dim(edge_links, first_tile, TILE_DEV, 0)
        turns_here = lax.dynamic_slice_in_dim(edge_turns, first_tile, TILE_DEV, 0)
        clinks_here = lax.dynamic_slice_in_dim(corner_links, first_tile, TILE_DEV, 0)
        cturns_here = lax.dynamic_slice_in_dim(corner_turns, first_tile, TILE_DEV, 0)
        padded = pad_tiles(tiles_here, rim_strips, corners, links_here, turns_here, clinks_here, cturns_here).astype(jnp.float32)
        pre_act = convolve(padded, kernel) + conv_bias[None, :, None, None]
        hidden = jax.nn.silu(pre_act).astype(jnp.bfloat16)
        hidden = lax.optimization_barrier(hidden)
        patches = to_patches(hidden).astype(jnp.float32)
        quarter = jnp.einsum("ok,tkq->toq", down_float, patches).astype(jnp.bfloat16)
        cot_here = lax.dynamic_slice_in_dim(fine_cot, first_tile, TILE_DEV, 0).astype(jnp.float32)
        grad_down = grad_down + jnp.einsum("toq,tkq->ok", cot_here, patches)
        grad_hidden = from_patches(jnp.einsum("ok,toq->tkq", down_float, cot_here), C, S)
        grad_pre = (grad_hidden * silu_slope(pre_act)).astype(jnp.bfloat16)
        grad_pre = lax.optimization_barrier(grad_pre).astype(jnp.float32)
        grad_bias = grad_bias + jnp.sum(grad_pre, axis=(0, 2, 3))
        products = []
        for row_shift in range(3):
            for col_shift in range(3):
                window = padded[:, :, row_shift:row_shift + S, col_shift:col_shift + S]
                products.append(jnp.einsum("toyx,tiyx->oi", grad_pre, window))
        grad_conv = grad_conv + jnp.stack(products, axis=-1).reshape(C, C * 9)
        return (grad_conv, grad_bias, grad_down), quarter

    initial = (jnp.zeros((C, C * 9), jnp.float32), jnp.zeros((C,), jnp.float32), jnp.zeros((C, C * 4), jnp.float32))
    totals, quarters = lax.scan(block_step, initial, jnp.arange(N_TILE, dtype=jnp.int32))
    quarters = quarters.reshape(TILES, C, (S // 2) * (S // 2))
    ordered = jnp.zeros_like(quarters).at[child_slot].set(quarters)
    coarse = join_quarters(ordered, S)
    return (coarse, totals[0], totals[1], totals[2])
```

```python
import jax
import jax.numpy as jnp
from jax import lax
from jax.experimental import pallas as pl
from jax.experimental.pallas import tpu as pltpu
from jax.sharding import PartitionSpec as P

BF = jnp.bfloat16
F32 = jnp.float32
NODES = 64
MSG = (NODES * 8, 384)


def iota(shape, dim):
    return lax.broadcasted_iota(jnp.int32, shape, dim)


def ones_where(mask):
    return jnp.where(mask, 1.0, 0.0).astype(BF)


def keep(mask, x):
    return jnp.where(mask, x, 0.0).astype(BF)


def mm(a, b):
    return jnp.dot(a, b, preferred_element_type=F32)


def mm_nt(a, b):
    return lax.dot_general(a, b, (((1,), (1,)), ((), ())), preferred_element_type=F32)


def halves(x):
    high = x.astype(BF)
    return high, (x - high.astype(F32)).astype(BF)


def call(body, out_shape, grid, in_specs, out_specs, scratch=(), flops=0, moved=0):
    return pl.pallas_call(
        body,
        out_shape=out_shape,
        grid=grid,
        in_specs=in_specs,
        out_specs=out_specs,
        scratch_shapes=scratch,
        compiler_params=pltpu.CompilerParams(vmem_limit_bytes=48 << 20),
        cost_estimate=pl.CostEstimate(flops=flops, bytes_accessed=moved, transcendentals=0),
    )


def whole(shape):
    return pl.BlockSpec(shape, lambda i: (0,) * len(shape))


def send_body(feat_ref, cot_ref, small_ref, out_ref):
    step = pl.program_id(0)
    cot = cot_ref[...]
    stack = jnp.concatenate([cot[:, q * 256 : q * 256 + 256] for q in range(16)], axis=0)
    row = iota((128, 512), 0) + step * 128
    col = iota((128, 512), 1)
    k, g, a, qr, hf = row >> 5, (row >> 3) & 3, (row >> 2) & 1, (row >> 1) & 1, row & 1
    source = (qr << 8) | (g << 6) | (hf << 5) | (a << 4) | k
    out_ref[:, 0:256] = mm(ones_where(col == source), stack).astype(BF)

    first = feat_ref[:, 0:128]
    last = feat_ref[:, 3968:4096]
    p = iota((16, 128), 0) + step * 16
    lane = iota((16, 128), 1)
    rim_n = mm_nt(ones_where(lane == 63 - p), first)
    rim_s = mm_nt(ones_where(lane == 64 + p), last)
    pc = iota((32, 4096), 0)
    px = iota((32, 4096), 1)
    pos = (pc & 15) + step * 16
    want = jnp.where(pc < 16, pos * 64, (63 - pos) * 64 + 63)
    rim_we = mm_nt(ones_where(px == want), feat_ref[...])
    cr = iota((16, 128), 0)
    corners = mm_nt(
        ones_where(((cr == 0) & (lane == 0)) | ((cr == 3) & (lane == 63))), first
    ) + mm_nt(ones_where(((cr == 1) & (lane == 64)) | ((cr == 2) & (lane == 127))), last)
    tc = iota((128, 128), 0)
    to = iota((128, 128), 1)
    by_chan = jnp.zeros((16, 128), F32)
    for c in range(4):
        spread = jnp.broadcast_to(corners[c : c + 1, :], (16, 128))
        by_chan = by_chan + mm(keep((lane & 15) == cr, spread), ones_where(to == (tc >> 4) * 4 + c))
    parts = [rim_n, rim_we[0:16], rim_s, rim_we[16:32], by_chan]
    stack = jnp.concatenate([x.astype(BF) for x in parts] + [small_ref[...]], axis=0)
    r, node = tc & 7, tc >> 3
    source = jnp.where(r < 5, r * 16 + node, jnp.where(r == 5, 80, jnp.where(r == 6, 81 + step, -1)))
    out_ref[:, 256:384] = mm(ones_where(to == source), stack).astype(BF)


def pick_body(msg_ref, out_ref, slot_ref):
    step = pl.program_id(0)
    cot = msg_ref[:, 0:256]
    misc = msg_ref[:, 256:384]
    row = iota((128, 512), 0) + step * 128
    col = iota((128, 512), 1)
    lane = iota((128, 128), 1)
    sub = iota((128, 128), 0)
    base = (row >> 3) << 3
    both = mm(ones_where((col == base + 5) | (col == base + 6)), misc)
    fields = mm(keep((lane & 7) == (sub & 7), both), ones_where((sub >> 3) == lane))
    flip = fields.T
    slot_ref[...] = jnp.broadcast_to(flip[12:13, :] * 8.0 + flip[13:14, :], (8, 128))
    num = fields.astype(jnp.int32)

    def field(f):
        return num[:, f : f + 1]

    slot_row = field(12) * 8 + ((field(13) >> 1) << 1)
    lane2 = iota((128, 256), 1)
    fold_r = iota((256, 128), 0)
    fold_c = iota((256, 128), 1)
    fold = ones_where(((fold_r >> 6) == (fold_c >> 5)) & ((fold_r & 31) == (fold_c & 31)))
    mine = ((lane2 >> 5) & 1) == (field(13) & 1)
    for hf in range(2):
        got = mm(ones_where(col == slot_row + hf), cot)
        out_ref[:, hf * 128 : hf * 128 + 128] = mm(keep(mine, got), fold).astype(BF)
    total = jnp.zeros((128, 128), F32)
    for k in range(4):
        got = mm(ones_where(col == field(k) * 8 + field(4 + k)), misc)
        place = ones_where(lane == k * 16 + (sub & 15))
        total = total + mm(keep((lane >> 4) == field(8 + k), got), place)
    got = mm(ones_where(col == field(14) * 8 + 4), misc)
    total = total + mm(keep(lane == field(15), got), ones_where(lane == 64))
    out_ref[:, 256:384] = total.astype(BF)


def regroup_body(msg_ref, out_ref):
    step = pl.program_id(0)
    row = iota((128, 512), 0)
    col = iota((128, 512), 1)
    pair, g, k, p = row >> 6, (row >> 4) & 3, row & 15, row & 63
    tile = (step << 1) | pair
    out_ref[:, 0:256] = mm(ones_where(col == ((k << 5) | (g << 3) | tile)), msg_ref[:, 0:256]).astype(BF)
    out_ref[:, 256:384] = mm(ones_where(col == ((p << 3) | tile)), msg_ref[:, 256:384]).astype(BF)


def level_body(feat_ref, msg_ref, w_ref, bias_ref, down_ref, down_t_ref, out_ref, win_ref, gc_ref, gd_ref, gb_ref):
    step = pl.program_id(0)
    x = jnp.concatenate([feat_ref[c, 0] for c in range(4)], axis=0)
    stack = jnp.concatenate([x[:, q * 512 : q * 512 + 512] for q in range(8)], axis=0)
    l_in = iota((512, 512), 0)
    l_out = iota((512, 512), 1)
    to = (
        (((l_in >> 6) & 1) << 8)
        | ((l_in & 1) << 7)
        | ((l_in >> 7) << 5)
        | ((l_in >> 1) & 31)
    )
    split = mm(stack, ones_where(l_out == to))

    def plane(a, b):
        s = (a * 2 + b) * 128
        return jnp.concatenate([split[q * 64 : q * 64 + 64, s : s + 128] for q in range(8)], axis=1)

    rim = [msg_ref[c, 0, :, 256:384].astype(F32) for c in range(4)]
    flip = [r.T.astype(BF) for r in rim]

    def strip(k):
        return jnp.concatenate([f[k * 16 : k * 16 + 16, :] for f in flip], axis=0)

    def corner(k):
        return jnp.concatenate([r[k * 16 : k * 16 + 16, 64:65] for r in rim], axis=0)

    lane = iota((64, 1024), 1)
    v = lane & 31
    pos = iota((64, 1024), 0)
    cols = []
    for a in range(2):
        y = ((lane >> 5) << 1) + a
        side = mm(strip(1), ones_where((v == 0) & (y == 63 - pos))) + mm(
            strip(3), ones_where((v == 31) & (y == pos))
        )
        even, odd = plane(a, 0), plane(a, 1)
        cols.append(
            [
                jnp.where(v == 0, side, pltpu.roll(odd, 1, axis=1)),
                even,
                odd,
                jnp.where(v == 31, side, pltpu.roll(even, 1023, axis=1)),
            ]
        )
    lane_e = iota((64, 512), 1)
    pos_e = iota((64, 512), 0)
    inner = lane_e & 127
    at = ((inner & 31) << 1) + (lane_e >> 7)
    ends = mm(strip(0), ones_where((inner < 32) & (pos_e == at - 1))) + mm(
        strip(2), ones_where((inner >= 96) & (pos_e == 64 - at))
    )
    for spot, k in ((0, 0), (96, 1), (384 + 31, 3), (384 + 127, 2)):
        ends = jnp.where(lane_e == spot, corner(k), ends)
    blank = jnp.zeros((64, 896), F32)
    for cx in range(4):
        end = ends[:, cx * 128 : cx * 128 + 128]
        top = jnp.where(lane < 32, jnp.concatenate([end, blank], axis=1), pltpu.roll(cols[1][cx], 32, axis=1))
        low = jnp.where(lane >= 992, jnp.concatenate([blank, end], axis=1), pltpu.roll(cols[0][cx], 992, axis=1))
        for ry, w in enumerate((top, cols[0][cx], cols[1][cx], low)):
            at_row = (ry * 4 + cx) * 64
            win_ref[at_row : at_row + 64, :] = w.astype(BF)

    pre = mm(w_ref[...], win_ref[...]) + bias_ref[...]
    sig = 1.0 / (1.0 + jnp.exp(-pre))
    hidden = (pre * sig).astype(BF)
    quarter = mm(down_ref[...], hidden).astype(BF)
    for c in range(4):
        out_ref[c, pl.ds(pl.multiple_of(step * 16, 16), 16), :] = quarter[c * 16 : c * 16 + 16, :]
    back = jnp.concatenate(
        [
            jnp.concatenate([msg_ref[c, 0, g * 16 : g * 16 + 16, 0:256] for c in range(4)], axis=0)
            for g in range(4)
        ],
        axis=1,
    )
    grad_hidden = mm(down_t_ref[...], back)
    grad_pre = (grad_hidden * (sig * (1.0 + pre * (1.0 - sig)))).astype(BF)

    @pl.when(step == 0)
    def _():
        gc_ref[...] = jnp.zeros_like(gc_ref)
        gd_ref[...] = jnp.zeros_like(gd_ref)
        gb_ref[...] = jnp.zeros_like(gb_ref)

    gb_ref[...] += jnp.broadcast_to(jnp.sum(grad_pre.astype(F32), axis=1, keepdims=True), (256, 128))
    gd_ref[...] += mm_nt(back, hidden)
    gc_ref[...] += mm_nt(win_ref[...], grad_pre)

    @pl.when(step == 1)
    def _():
        rows = []
        for dy in range(3):
            for cx in range(4):
                r0, r1 = (dy * 4 + cx) * 64, ((dy + 1) * 4 + cx) * 64
                rows.append(gc_ref[r0 : r0 + 64, 0:128] + gc_ref[r1 : r1 + 64, 128:256])
        taps = []
        for dy in range(3):
            for dx in range(3):
                taps.append(rows[dy * 4 + dx] + pltpu.roll(rows[dy * 4 + dx + 1], 64, axis=1))
        taps.append(jnp.zeros((64, 128), F32))
        conv = jnp.concatenate(taps, axis=0)
        conv = jnp.concatenate([conv[q * 128 : q * 128 + 128, :].T for q in range(5)], axis=1)[0:64, :]
        kk = iota((640, 1024), 0)
        cc = iota((640, 1024), 1)
        i, tap = kk & 63, kk >> 6
        place = ones_where((cc == ((i >> 4) << 8) + (i & 15) * 9 + tap) & (tap < 9))
        conv = [mm(h, place) for h in halves(conv)]
        kk = iota((256, 1024), 0)
        cc = iota((256, 1024), 1)
        i, ab = kk & 63, kk >> 6
        place = ones_where(cc == ((i >> 4) << 8) + 144 + (i & 15) * 4 + ab)
        down = [mm(h, place) for h in halves(gd_ref[...])]
        gb = gb_ref[0:64, :] + gb_ref[64:128, :] + gb_ref[128:192, :] + gb_ref[192:256, :]
        bias = [h.astype(F32)[:, 0:1] for h in halves(gb)]
        lane16 = iota((16, 1024), 1)
        for part in range(2):
            for c in range(4):
                d = jnp.concatenate(
                    [down[part][s * 16 : s * 16 + 16, c * 256 : c * 256 + 256] for s in range(4)], axis=1
                )
                both = conv[part][c * 16 : c * 16 + 16, :] + d
                both = jnp.where(lane16 == 208, bias[part][c * 16 : c * 16 + 16, :], both)
                out_ref[c, 32 + part * 16 : 48 + part * 16, :] = both.astype(BF)


def spread_body(msg_ref, out_ref):
    step = pl.program_id(0)
    stack = jnp.concatenate(
        [msg_ref[c, 0:32, g * 256 : g * 256 + 256] for g in range(4) for c in range(4)], axis=0
    )
    row = iota((128, 512), 0) + step * 128
    col = iota((128, 512), 1)
    source = (((row >> 3) & 3) << 7) | (((row >> 1) & 3) << 5) | ((row & 1) << 4) | (row >> 5)
    out_ref[:, 0:256] = mm(ones_where(col == source), stack).astype(BF)
    total = jnp.zeros((16, 1024), F32)
    for c in range(4):
        total = total + (msg_ref[c, 32:48, :].astype(F32) + msg_ref[c, 48:64, :].astype(F32))
    parts = [
        h[:, s * 256 + o : s * 256 + o + 128] for h in halves(total) for o in (0, 128) for s in range(4)
    ]
    stack = jnp.concatenate(parts, axis=0)
    row = iota((128, 256), 0) + step * 128
    col = iota((128, 256), 1)
    r, p = row & 7, row >> 3
    out_ref[:, 256:384] = mm(ones_where((col == (r << 6) + p) & (r < 4)), stack).astype(BF)


def place_body(msg_ref, slot_ref, out_ref):
    step = pl.program_id(0)
    quarter = msg_ref[:, 0:256]
    slot = slot_ref[0:1, :].astype(jnp.int32)
    row = iota((128, 512), 0) + step * 128
    lane = iota((128, 256), 1)
    half = iota((128, 256), 0) & 1
    li = iota((256, 256), 0)
    lo = iota((256, 256), 1)
    same = ((lo >> 6) == ((li >> 5) & 3)) & ((lo & 31) == (li & 31))
    total = jnp.zeros((128, 256), F32)
    for qc in range(2):
        got = mm(ones_where(slot == ((row >> 1) << 1) + qc), quarter)
        total = total + mm(keep((lane >> 7) == half, got), ones_where(same & (((lo >> 5) & 1) == qc)))
    out_ref[:, 0:256] = total.astype(BF)
    r = iota((16, 512), 0)
    src = iota((16, 512), 1) & 7
    summed = mm(ones_where((src < 4) & ((src & 1) == (r & 1)) & (r < 4)), msg_ref[:, 256:384])
    high, low = halves(summed)
    both = jnp.where(iota((16, 128), 0) < 2, high.astype(F32), low.astype(F32)).astype(BF)
    r = iota((128, 16), 0) & 7
    c = iota((128, 16), 1)
    out_ref[:, 256:384] = mm(ones_where((r == c) & (r < 4)), both).astype(BF)


def finish_body(msg_ref, coarse_ref, conv_ref, down_ref, bias_ref):
    step = pl.program_id(0)
    row = iota((128, 512), 0) + step * 128
    col = iota((128, 512), 1)
    qr, g, hf, a, k = row >> 8, (row >> 6) & 3, (row >> 5) & 1, (row >> 4) & 1, row & 15
    source = (k << 5) | (g << 3) | (a << 2) | (qr << 1) | hf
    got = mm(ones_where(col == source), msg_ref[:, 0:256]).astype(BF)
    coarse_ref[...] = jnp.concatenate([got[q * 32 : q * 32 + 32, :] for q in range(4)], axis=1)

    @pl.when(step == 0)
    def _():
        row = iota((256, 512), 0)
        col = iota((256, 512), 1)
        got = mm(ones_where(col == ((row & 63) << 3) + (row >> 6)), msg_ref[:, 256:384])
        near = iota((1024, 576), 0)
        at = iota((1024, 576), 1)
        place = ones_where((at == (near >> 8) * 144 + (near & 255)) & ((near & 255) < 144))
        sub = iota((128, 128), 0)
        lane = iota((128, 128), 1)
        shift = ones_where((sub == lane + 16) & (lane < 64))
        conv = jnp.zeros((16, 576), F32)
        down = jnp.zeros((64, 128), F32)
        for h in range(2):
            low, high = got[h * 128 : h * 128 + 64, :], got[h * 128 + 64 : h * 128 + 128, :]
            wide = jnp.concatenate(
                [x[s * 16 : s * 16 + 16, :] for s in range(4) for x in (low, high)], axis=1
            )
            conv = conv + mm(wide.astype(BF), place)
            down = down + mm(high.astype(BF), shift)
        conv_ref[...] = conv
        down_ref[...] = down[:, 0:64]
        bias_ref[...] = got[64:80, 80:81] + got[192:208, 80:81]


def index_rows(edge_links, edge_turns, corner_links, corner_turns, child_slot):
    side = jnp.arange(4, dtype=jnp.int32)[None, :]
    slot = child_slot[None, :]
    edge = jnp.concatenate(
        [
            (edge_links >> 3).T,
            ((side + 2 + edge_turns) & 3).T,
            (edge_links & 7).T,
            slot >> 3,
            slot & 7,
            jnp.zeros((2, 8), jnp.int32),
        ],
        axis=0,
    ).reshape(1, 128)
    node = jnp.where(corner_links < 0, 127, corner_links >> 3).T
    pixel = ((corner_links & 7) * 4 + ((side + 2 + corner_turns) & 3)).T
    corner = jnp.concatenate([jnp.zeros((4, 112), jnp.int32), node, pixel], axis=1)
    return jnp.concatenate([edge, corner, jnp.zeros((43, 128), jnp.int32)], axis=0).astype(BF)


def gather_weights(conv_weight, conv_bias, down_weight):
    b0 = conv_bias.astype(BF)
    rest = conv_bias - b0.astype(F32)
    b1 = rest.astype(BF)
    b2 = (rest - b1.astype(F32)).astype(BF)
    packed = jnp.concatenate(
        [conv_weight, down_weight.reshape(16, 256), jnp.stack([b0, b1, b2], axis=1), jnp.zeros((16, 61), BF)],
        axis=1,
    )
    every = lax.all_gather(packed, "chan", axis=0, tiled=True)
    taps = every[:, :576].reshape(64, 64, 3, 3).transpose(0, 2, 3, 1)
    weights = jnp.concatenate(
        [
            jnp.pad(taps, ((0, 0), (a, 1 - a), (b, 1 - b), (0, 0))).reshape(64, 1024)
            for a in range(2)
            for b in range(2)
        ],
        axis=0,
    )
    down = every[:, 576:832].reshape(4, 64, 16, 4).transpose(1, 3, 0, 2).reshape(64, 256)
    bias = every[:, 832:835].astype(F32)
    bias = (bias[:, 0] + bias[:, 1]) + bias[:, 2]
    return weights, down, jnp.concatenate([bias] * 4)[:, None]


def on_device(
    features,
    conv_weight,
    conv_bias,
    down_weight,
    cotangent,
    edge_links,
    edge_turns,
    corner_links,
    corner_turns,
    child_slot,
):
    msg_spec = whole(MSG)
    block = pl.BlockSpec((128, 384), lambda i: (i, 0))
    msg = jax.ShapeDtypeStruct(MSG, BF)

    def to_nodes(x):
        return lax.all_to_all(x.reshape(64, 8, 384), "tile", 0, 0, tiled=True).reshape(MSG)

    small = index_rows(edge_links, edge_turns, corner_links, corner_turns, child_slot)
    pieces = call(
        send_body,
        msg,
        (4,),
        [whole((128, 4096)), whole((32, 4096)), whole((48, 128))],
        block,
        flops=10**9,
        moved=2 * 10**6,
    )(features.reshape(128, 4096), cotangent.reshape(32, 4096), small)
    pieces = to_nodes(pieces)
    tiles = lax.all_to_all(features.reshape(4, 2, 16, 4096), "chan", 0, 0, tiled=True)
    weights, down, bias = gather_weights(conv_weight, conv_bias, down_weight)
    picked, slots = call(
        pick_body,
        (msg, jax.ShapeDtypeStruct((8, 512), F32)),
        (4,),
        [msg_spec],
        (block, pl.BlockSpec((8, 128), lambda i: (0, i))),
        flops=10**9,
        moved=10**6,
    )(pieces)
    picked = to_nodes(picked)
    picked = call(regroup_body, msg, (4,), [msg_spec], block, flops=4 * 10**8, moved=10**6)(picked)
    picked = lax.all_to_all(picked.reshape(4, 128, 384), "chan", 0, 0, tiled=True)
    local = call(
        level_body,
        jax.ShapeDtypeStruct((4, 64, 1024), BF),
        (2,),
        [
            pl.BlockSpec((4, 1, 16, 4096), lambda i: (0, i, 0, 0)),
            pl.BlockSpec((4, 1, 64, 384), lambda i: (0, i, 0, 0)),
            whole((256, 1024)),
            whole((256, 1)),
            whole((64, 256)),
            whole((256, 64)),
        ],
        whole((4, 64, 1024)),
        (
            pltpu.VMEM((1024, 1024), BF),
            pltpu.VMEM((1024, 256), F32),
            pltpu.VMEM((64, 256), F32),
            pltpu.VMEM((256, 128), F32),
        ),
        flops=4 * 10**9,
        moved=4 * 10**6,
    )(tiles, picked.reshape(4, 2, 64, 384), weights, bias, down, down.T)
    local = lax.all_to_all(local, "chan", 0, 0, tiled=True)
    out = call(spread_body, msg, (4,), [whole((4, 64, 1024))], block, flops=4 * 10**8, moved=10**6)(local)
    out = to_nodes(out)
    out = call(place_body, msg, (4,), [msg_spec, whole((8, 512))], block, flops=5 * 10**8, moved=10**6)(
        out, slots
    )
    out = to_nodes(out)
    coarse, grad_conv, grad_down, grad_bias = call(
        finish_body,
        (
            jax.ShapeDtypeStruct((32, 4096), BF),
            jax.ShapeDtypeStruct((16, 576), F32),
            jax.ShapeDtypeStruct((64, 64), F32),
            jax.ShapeDtypeStruct((16, 1), F32),
        ),
        (4,),
        [msg_spec],
        (
            pl.BlockSpec((32, 1024), lambda i: (0, i)),
            whole((16, 576)),
            whole((64, 64)),
            whole((16, 1)),
        ),
        flops=4 * 10**8,
        moved=10**6,
    )(out)
    return (coarse.reshape(2, 16, 4096), grad_conv, grad_bias.reshape(16), grad_down)


def solution(mesh):
    in_specs = (
        P("tile", "chan", None),
        P("chan", None),
        P("chan"),
        P(None, "chan"),
        P("tile", "chan", None),
        P("tile", None),
        P("tile", None),
        P("tile", None),
        P("tile", None),
        P("tile"),
    )
    out_specs = (P("tile", "chan", None), P("chan", None), P("chan"), P(None, "chan"))
    return jax.shard_map(
        on_device, mesh=mesh, in_specs=in_specs, out_specs=out_specs, check_vma=False
    )
```

```python
import jax
import jax.numpy as jnp
from jax import lax
from jax.experimental import pallas as pl
from jax.experimental.pallas import tpu as pltpu
from jax.sharding import PartitionSpec as P

BF = jnp.bfloat16
F32 = jnp.float32
NODES = 64
MSG = (NODES * 8, 384)


def iota(shape, dim):
    return lax.broadcasted_iota(jnp.int32, shape, dim)


def down_col(n, start=0):
    return iota((n, 1), 0) + start


def lane_row(n):
    return iota((1, n), 1)


def ones_where(mask):
    return jnp.where(mask, 1.0, 0.0).astype(BF)


def keep(mask, x):
    return jnp.where(mask, x, 0.0).astype(BF)


def mm(a, b):
    return jnp.dot(a, b, preferred_element_type=F32)


def mm_nt(a, b):
    return lax.dot_general(a, b, (((1,), (1,)), ((), ())), preferred_element_type=F32)


def halves(x):
    high = x.astype(BF)
    return high, (x - high.astype(F32)).astype(BF)


def call(body, out_shape, grid, in_specs, out_specs, scratch=(), flops=0, moved=0):
    return pl.pallas_call(
        body,
        out_shape=out_shape,
        grid=grid,
        in_specs=in_specs,
        out_specs=out_specs,
        scratch_shapes=scratch,
        compiler_params=pltpu.CompilerParams(vmem_limit_bytes=48 << 20),
        cost_estimate=pl.CostEstimate(flops=flops, bytes_accessed=moved, transcendentals=0),
    )


def whole(shape):
    return pl.BlockSpec(shape, lambda *i: (0,) * len(shape))


def send_body(me_ref, feat_ref, cot_ref, el_ref, et_ref, cl_ref, ct_ref, slot_ref, out_ref, *peer_refs):
    step = pl.program_id(0)
    for d in range(1, 4):

        @pl.when(step == d)
        def _():
            peer = me_ref[0] ^ d
            peer_refs[d - 1][...] = feat_ref[pl.ds(pl.multiple_of(peer * 32, 32), 32), :]

    cot = cot_ref[...]
    stack = jnp.concatenate([cot[:, q * 256 : q * 256 + 256] for q in range(16)], axis=0)
    row = down_col(128, step * 128)
    k, g, a, qr, hf = row >> 5, (row >> 3) & 3, (row >> 2) & 1, (row >> 1) & 1, row & 1
    source = (qr << 8) | (g << 6) | (hf << 5) | (a << 4) | k
    out_ref[:, 0:256] = mm(ones_where(lane_row(512) == source), stack).astype(BF)

    first = feat_ref[:, 0:128]
    last = feat_ref[:, 3968:4096]
    p = down_col(16, step * 16)
    lane = lane_row(128)
    rim_n = mm_nt(ones_where(lane == 63 - p), first)
    rim_s = mm_nt(ones_where(lane == 64 + p), last)
    pc = down_col(32)
    pos = (pc & 15) + step * 16
    want = jnp.where(pc < 16, pos * 64, (63 - pos) * 64 + 63)
    rim_we = mm_nt(ones_where(lane_row(4096) == want), feat_ref[...])
    cr = down_col(16)
    at_first = jnp.where(cr == 0, 0, jnp.where(cr == 3, 63, -1))
    at_last = jnp.where(cr == 1, 64, jnp.where(cr == 2, 127, -1))
    corners = mm_nt(ones_where(lane == at_first), first) + mm_nt(ones_where(lane == at_last), last)
    tc = down_col(128)
    by_chan = jnp.zeros((16, 128), F32)
    for c in range(4):
        spread = jnp.broadcast_to(corners[c : c + 1, :], (16, 128))
        by_chan = by_chan + mm(keep((lane & 15) == cr, spread), ones_where(lane == (tc >> 4) * 4 + c))

    def over_lanes(x):
        rows = jnp.zeros((x.shape[0], 128), jnp.int32)
        for t in range(8):
            rows = jnp.where((lane & 7) == t, x[:, t : t + 1], rows)
        return rows

    def in_row(x, first_field):
        rows = over_lanes(x)
        side = iota(rows.shape, 0)
        mine = (iota(rows.shape, 1) >> 3) == side + first_field
        return jnp.sum(jnp.where(mine, rows, 0).astype(F32), axis=0, keepdims=True)

    side = iota((4, 8), 0)
    el, cl, slot = el_ref[...], cl_ref[...], slot_ref[...]
    edge = in_row(el >> 3, 0) + in_row((side + 2 + et_ref[...]) & 3, 4) + in_row(el & 7, 8)
    edge = edge + in_row(slot >> 3, 12) + in_row(slot & 7, 13)
    node = over_lanes(jnp.where(cl < 0, 127, cl >> 3)).astype(F32)
    pixel = over_lanes((cl & 7) * 4 + ((side + 2 + ct_ref[...]) & 3)).astype(F32)
    field = lane >> 3
    sub = down_col(16)
    small = jnp.where(sub == 0, edge, 0.0)
    for part in range(4):
        line = jnp.where(field == 14, node[part : part + 1, :], 0.0)
        line = jnp.where(field == 15, pixel[part : part + 1, :], line)
        small = small + jnp.where(sub == part + 1, line, 0.0)
    parts = [rim_n, rim_we[0:16], rim_s, rim_we[16:32], by_chan, small, jnp.zeros((32, 128), F32)]
    stack = jnp.concatenate([x.astype(BF) for x in parts], axis=0)
    r, node = tc & 7, tc >> 3
    source = jnp.where(r < 5, r * 16 + node, jnp.where(r == 5, 80, jnp.where(r == 6, 81 + step, -1)))
    out_ref[:, 256:384] = mm(ones_where(lane == source), stack).astype(BF)


def pick_body(msg_ref, out_ref, slot_ref):
    step = pl.program_id(0)
    cot = msg_ref[:, 0:256]
    misc = msg_ref[:, 256:384]
    col = lane_row(512)
    lane = lane_row(128)
    sub = down_col(128)
    base = ((sub + step * 128) >> 3) << 3
    both = mm(ones_where((col == base + 5) | (col == base + 6)), misc)
    fields = mm(keep((lane & 7) == (sub & 7), both), ones_where((sub >> 3) == lane))
    flip = fields.T
    slot_ref[...] = jnp.broadcast_to(flip[12:13, :] * 8.0 + flip[13:14, :], (8, 128))
    num = fields.astype(jnp.int32)

    def field(f):
        return num[:, f : f + 1]

    slot_row = field(12) * 8 + ((field(13) >> 1) << 1)
    lane2 = lane_row(256)
    fold_r = down_col(256)
    fold = ones_where(lane == (((fold_r >> 6) << 5) | (fold_r & 31)))
    mine = ((lane2 >> 5) & 1) == (field(13) & 1)
    for hf in range(2):
        got = mm(ones_where(col == slot_row + hf), cot)
        out_ref[:, hf * 128 : hf * 128 + 128] = mm(keep(mine, got), fold).astype(BF)
    total = jnp.zeros((128, 128), F32)
    for k in range(4):
        got = mm(ones_where(col == field(k) * 8 + field(4 + k)), misc)
        place = ones_where(lane == k * 16 + (sub & 15))
        total = total + mm(keep((lane >> 4) == field(8 + k), got), place)
    got = mm(ones_where(col == field(14) * 8 + 4), misc)
    total = total + mm(keep(lane == field(15), got), ones_where(jnp.broadcast_to(lane == 64, (128, 128))))
    out_ref[:, 256:384] = total.astype(BF)


def regroup_body(me_ref, msg_ref, conv_ref, bias_ref, down_ref, *out_refs):
    row = down_col(128)
    col = lane_row(512)
    pair, g, k, p = row >> 6, (row >> 4) & 3, row & 15, row & 63
    zero = jnp.zeros((64, 64), BF)
    lane = lane_row(128)
    bias = jnp.where(lane_row(16) == down_col(16), bias_ref[...], 0.0)
    bias = jnp.sum(bias, axis=1, keepdims=True)
    b0 = bias.astype(BF).astype(F32)
    b1 = (bias - b0).astype(BF).astype(F32)
    b2 = (bias - b0) - b1
    bias = jnp.where(lane == 0, b0, jnp.where(lane == 1, b1, jnp.where(lane == 2, b2, 0.0))).astype(BF)
    for d in range(4):
        out_ref = out_refs[d]
        tile = ((me_ref[0] ^ d) << 1) | pair
        out_ref[0:128, 0:256] = mm(
            ones_where(col == ((k << 5) | (g << 3) | tile)), msg_ref[:, 0:256]
        ).astype(BF)
        out_ref[0:128, 256:384] = mm(ones_where(col == ((p << 3) | tile)), msg_ref[:, 256:384]).astype(BF)
        out_ref[128:192, 0:128] = jnp.concatenate([down_ref[...], zero], axis=1)
        out_ref[128:144, 128:384] = conv_ref[:, 0:256]
        out_ref[144:160, 128:384] = conv_ref[:, 256:512]
        out_ref[160:176, 128:256] = jnp.concatenate([conv_ref[:, 512:576], zero[0:16]], axis=1)
        out_ref[160:176, 256:384] = bias
        out_ref[176:192, 128:384] = jnp.zeros((16, 256), BF)


def lay_weights(raw_ref, w_ref, down_ref, down_t_ref, bias_ref):
    raw = jnp.concatenate(
        [
            jnp.concatenate([raw_ref[c, 128 + q * 16 : 144 + q * 16, 128 : 128 + n] for c in range(4)], axis=0)
            for q, n in ((0, 256), (1, 256), (2, 128))
        ],
        axis=1,
    )
    e = iota((640, 1), 0)
    i = (e * 7282) >> 16
    tap = e - i * 9
    dy = (tap * 86) >> 8
    to = jnp.where(e < 576, dy * 256 + (tap - dy * 3) * 64 + i, -9999)
    col = lane_row(1536)
    shifted = mm(raw, ones_where(jnp.where(col < 768, col, col - 832) == to)).astype(BF)
    zero = jnp.zeros((64, 256), BF)
    for a in range(2):
        for b in range(2):
            part = shifted[:, b * 768 : b * 768 + 768]
            row = (a * 2 + b) * 64
            w_ref[row : row + 64, :] = jnp.concatenate([zero, part] if a else [part, zero], axis=1)
    down = jnp.zeros((64, 256), F32)
    down_t = jnp.zeros((256, 64), F32)
    for c in range(4):
        mine = raw_ref[c, 128:192, 0:128]
        l = down_col(128)
        to = jnp.where(l < 64, (l & 3) * 64 + c * 16 + (l >> 2), -1)
        down = down + mm(mine, ones_where(lane_row(256) == to))
        l = lane_row(128)
        to = jnp.where(l < 64, (l & 3) * 64 + c * 16 + (l >> 2), -1)
        down_t = down_t + mm_nt(ones_where(down_col(256) == to), mine)
    down_ref[...] = down.astype(BF)
    down_t_ref[...] = down_t.astype(BF)
    bias = jnp.concatenate([raw_ref[c, 160:176, 256:259].astype(F32) for c in range(4)], axis=0)
    bias = (bias[:, 0:1] + bias[:, 1:2]) + bias[:, 2:3]
    bias_ref[...] = jnp.broadcast_to(jnp.concatenate([bias] * 4, axis=0), (256, 128))


def level_body(me_ref, *refs):
    feat_refs, in_refs, out_refs = refs[0:4], refs[4:8], refs[8:12]
    x_ref, msg_ref, sum_ref, win_ref, gc_ref, gd_ref, gb_ref, w_ref, down_ref, down_t_ref, bias_ref = refs[12:]
    step = pl.program_id(0)
    me = me_ref[0]

    @pl.when(step == 0)
    def _():
        for d in range(4):
            msg_ref[me ^ d] = in_refs[d][...]
        lay_weights(msg_ref, w_ref, down_ref, down_t_ref, bias_ref)

    for d in range(4):
        x_ref[me ^ d] = feat_refs[d][0]
    half = pl.multiple_of(step * 64, 64)
    x = jnp.concatenate([x_ref[c] for c in range(4)], axis=0)
    stack = jnp.concatenate([x[:, q * 512 : q * 512 + 512] for q in range(8)], axis=0)
    l_in = down_col(512)
    to = (
        (((l_in >> 6) & 1) << 8)
        | ((l_in & 1) << 7)
        | ((l_in >> 7) << 5)
        | ((l_in >> 1) & 31)
    )
    split = mm(stack, ones_where(lane_row(512) == to))

    def plane(a, b):
        s = (a * 2 + b) * 128
        return jnp.concatenate([split[q * 64 : q * 64 + 64, s : s + 128] for q in range(8)], axis=1)

    rim = [msg_ref[c, pl.ds(half, 64), 256:384].astype(F32) for c in range(4)]
    flip = [r.T.astype(BF) for r in rim]

    def strip(k):
        return jnp.concatenate([f[k * 16 : k * 16 + 16, :] for f in flip], axis=0)

    def corner(k):
        return jnp.concatenate([r[k * 16 : k * 16 + 16, 64:65] for r in rim], axis=0)

    lane = lane_row(1024)
    v = lane & 31
    pos = down_col(64)
    cols = []
    for a in range(2):
        y = ((lane >> 5) << 1) + a
        west = jnp.where(v == 0, 63 - y, -1)
        east = jnp.where(v == 31, y, -1)
        side = mm(strip(1), ones_where(west == pos)) + mm(strip(3), ones_where(east == pos))
        even, odd = plane(a, 0), plane(a, 1)
        cols.append(
            [
                jnp.where(v == 0, side, pltpu.roll(odd, 1, axis=1)),
                even,
                odd,
                jnp.where(v == 31, side, pltpu.roll(even, 1023, axis=1)),
            ]
        )
    lane_e = lane_row(512)
    inner = lane_e & 127
    at = ((inner & 31) << 1) + (lane_e >> 7)
    north = jnp.where(inner < 32, at - 1, -1)
    south = jnp.where(inner >= 96, 64 - at, -1)
    ends = mm(strip(0), ones_where(north == pos)) + mm(strip(2), ones_where(south == pos))
    for spot, k in ((0, 0), (96, 1), (384 + 31, 3), (384 + 127, 2)):
        ends = jnp.where(lane_e == spot, corner(k), ends)
    blank = jnp.zeros((64, 896), F32)
    for cx in range(4):
        end = ends[:, cx * 128 : cx * 128 + 128]
        top = jnp.where(lane < 32, jnp.concatenate([end, blank], axis=1), pltpu.roll(cols[1][cx], 32, axis=1))
        low = jnp.where(lane >= 992, jnp.concatenate([blank, end], axis=1), pltpu.roll(cols[0][cx], 992, axis=1))
        for ry, w in enumerate((top, cols[0][cx], cols[1][cx], low)):
            at_row = (ry * 4 + cx) * 64
            win_ref[at_row : at_row + 64, :] = w.astype(BF)

    pre = mm(w_ref[...], win_ref[...]) + bias_ref[:, 0:1]
    sig = 1.0 / (1.0 + jnp.exp(-pre))
    hidden = (pre * sig).astype(BF)
    quarter = mm(down_ref[...], hidden).astype(BF)
    for c in range(4):
        sum_ref[c, pl.ds(pl.multiple_of(step * 16, 16), 16), :] = quarter[c * 16 : c * 16 + 16, :]
    back = jnp.concatenate(
        [
            jnp.concatenate(
                [msg_ref[c, pl.ds(half + g * 16, 16), 0:256] for c in range(4)], axis=0
            )
            for g in range(4)
        ],
        axis=1,
    )
    grad_hidden = mm(down_t_ref[...], back)
    grad_pre = (grad_hidden * (sig * (1.0 + pre * (1.0 - sig)))).astype(BF)

    @pl.when(step == 0)
    def _():
        gc_ref[...] = jnp.zeros_like(gc_ref)
        gd_ref[...] = jnp.zeros_like(gd_ref)
        gb_ref[...] = jnp.zeros_like(gb_ref)

    gb_ref[...] += jnp.broadcast_to(jnp.sum(grad_pre.astype(F32), axis=1, keepdims=True), (256, 128))
    gd_ref[...] += mm_nt(back, hidden)
    gc_ref[...] += mm_nt(win_ref[...], grad_pre)

    @pl.when(step == 1)
    def _():
        rows = []
        for dy in range(3):
            for cx in range(4):
                r0, r1 = (dy * 4 + cx) * 64, ((dy + 1) * 4 + cx) * 64
                rows.append(gc_ref[r0 : r0 + 64, 0:128] + gc_ref[r1 : r1 + 64, 128:256])
        taps = []
        for dy in range(3):
            for dx in range(3):
                taps.append(rows[dy * 4 + dx] + pltpu.roll(rows[dy * 4 + dx + 1], 64, axis=1))
        taps.append(jnp.zeros((64, 128), F32))
        conv = jnp.concatenate(taps, axis=0)
        conv = jnp.concatenate([conv[q * 128 : q * 128 + 128, :].T for q in range(5)], axis=1)[0:64, :]
        kk = down_col(640)
        cc = lane_row(1024)
        i, tap = kk & 63, kk >> 6
        place = ones_where(cc == jnp.where(tap < 9, ((i >> 4) << 8) + (i & 15) * 9 + tap, -1))
        conv = [mm(h, place) for h in halves(conv)]
        kk = down_col(256)
        i, ab = kk & 63, kk >> 6
        place = ones_where(cc == ((i >> 4) << 8) + 144 + (i & 15) * 4 + ab)
        down = [mm(h, place) for h in halves(gd_ref[...])]
        gb = gb_ref[0:64, :] + gb_ref[64:128, :] + gb_ref[128:192, :] + gb_ref[192:256, :]
        bias = [h.astype(F32)[:, 0:1] for h in halves(gb)]
        lane16 = lane_row(1024)
        for part in range(2):
            for c in range(4):
                d = jnp.concatenate(
                    [down[part][s * 16 : s * 16 + 16, c * 256 : c * 256 + 256] for s in range(4)], axis=1
                )
                both = conv[part][c * 16 : c * 16 + 16, :] + d
                both = jnp.where(lane16 == 208, bias[part][c * 16 : c * 16 + 16, :], both)
                sum_ref[c, 32 + part * 16 : 48 + part * 16, :] = both.astype(BF)
        for d in range(4):
            out_refs[d][...] = sum_ref[me ^ d]


def spread_body(me_ref, *refs):
    in_refs, out_ref, msg_ref = refs[0:4], refs[4], refs[5]
    step = pl.program_id(0)

    @pl.when(step == 0)
    def _():
        for d in range(4):
            msg_ref[me_ref[0] ^ d] = in_refs[d][...]

    stack = jnp.concatenate(
        [msg_ref[c, 0:32, g * 256 : g * 256 + 256] for g in range(4) for c in range(4)], axis=0
    )
    row = down_col(128, step * 128)
    source = (((row >> 3) & 3) << 7) | (((row >> 1) & 3) << 5) | ((row & 1) << 4) | (row >> 5)
    out_ref[:, 0:256] = mm(ones_where(lane_row(512) == source), stack).astype(BF)
    total = jnp.zeros((16, 1024), F32)
    for c in range(4):
        total = total + (msg_ref[c, 32:48, :].astype(F32) + msg_ref[c, 48:64, :].astype(F32))
    parts = [
        h[:, s * 256 + o : s * 256 + o + 128] for h in halves(total) for o in (0, 128) for s in range(4)
    ]
    stack = jnp.concatenate(parts, axis=0)
    r, p = row & 7, row >> 3
    source = jnp.where(r < 4, (r << 6) + p, -1)
    out_ref[:, 256:384] = mm(ones_where(lane_row(256) == source), stack).astype(BF)


def place_body(msg_ref, slot_ref, out_ref):
    step = pl.program_id(0)
    quarter = msg_ref[:, 0:256]
    slot = slot_ref[0:1, :].astype(jnp.int32)
    row = down_col(128, step * 128)
    lane = lane_row(256)
    half = row & 1
    li = down_col(256)
    to = (((li >> 5) & 3) << 6) | (li & 31)
    total = jnp.zeros((128, 256), F32)
    for qc in range(2):
        got = mm(ones_where(slot == ((row >> 1) << 1) + qc), quarter)
        total = total + mm(keep((lane >> 7) == half, got), ones_where(lane == to + qc * 32))
    out_ref[:, 0:256] = total.astype(BF)
    r = down_col(16)
    src = lane_row(512) & 7
    src = jnp.where(src < 4, src & 1, -1)
    summed = mm(ones_where(src == jnp.where(r < 4, r & 1, -2)), msg_ref[:, 256:384])
    high, low = halves(summed)
    both = jnp.where(iota((16, 128), 0) < 2, high.astype(F32), low.astype(F32)).astype(BF)
    r = row & 7
    out_ref[:, 256:384] = mm(ones_where(lane_row(16) == jnp.where(r < 4, r, -1)), both).astype(BF)


def finish_body(msg_ref, coarse_ref, conv_ref, down_ref, bias_ref):
    step = pl.program_id(0)
    row = down_col(128, step * 128)
    col = lane_row(512)
    qr, g, hf, a, k = row >> 8, (row >> 6) & 3, (row >> 5) & 1, (row >> 4) & 1, row & 15
    source = (k << 5) | (g << 3) | (a << 2) | (qr << 1) | hf
    got = mm(ones_where(col == source), msg_ref[:, 0:256]).astype(BF)
    coarse_ref[...] = jnp.concatenate([got[q * 32 : q * 32 + 32, :] for q in range(4)], axis=1)

    @pl.when(step == 0)
    def _():
        row = down_col(256)
        got = mm(ones_where(col == ((row & 63) << 3) + (row >> 6)), msg_ref[:, 256:384])
        near = down_col(1024)
        to = jnp.where((near & 255) < 144, (near >> 8) * 144 + (near & 255), -1)
        place = ones_where(lane_row(576) == to)
        lane = lane_row(128)
        shift = ones_where(down_col(128) == jnp.where(lane < 64, lane + 16, -1))
        conv = jnp.zeros((16, 576), F32)
        down = jnp.zeros((64, 128), F32)
        for h in range(2):
            low, high = got[h * 128 : h * 128 + 64, :], got[h * 128 + 64 : h * 128 + 128, :]
            wide = jnp.concatenate(
                [x[s * 16 : s * 16 + 16, :] for s in range(4) for x in (low, high)], axis=1
            )
            conv = conv + mm(wide.astype(BF), place)
            down = down + mm(high.astype(BF), shift)
        conv_ref[...] = conv
        down_ref[...] = down[:, 0:64]
        bias = got[64:80, 80:81] + got[192:208, 80:81]
        bias_ref[...] = jnp.sum(jnp.where(lane_row(16) == down_col(16), bias, 0.0), axis=0, keepdims=True)


def to_peers(parts):
    return [parts[0]] + [
        lax.ppermute(parts[d], "chan", [(i, i ^ d) for i in range(4)]) for d in range(1, 4)
    ]


def on_device(
    features,
    conv_weight,
    conv_bias,
    down_weight,
    cotangent,
    edge_links,
    edge_turns,
    corner_links,
    corner_turns,
    child_slot,
):
    msg_spec = whole(MSG)
    block = pl.BlockSpec((128, 384), lambda i: (i, 0))
    msg = jax.ShapeDtypeStruct(MSG, BF)

    def to_nodes(x):
        return lax.all_to_all(x.reshape(64, 8, 384), "tile", 0, 0, tiled=True).reshape(MSG)

    me = lax.axis_index("chan").astype(jnp.int32).reshape(1)
    scalar = pl.BlockSpec(memory_space=pltpu.SMEM)
    peer_rows = jax.ShapeDtypeStruct((32, 4096), BF)
    pieces, *tiles = call(
        send_body,
        (msg, peer_rows, peer_rows, peer_rows),
        (4,),
        [scalar, whole((128, 4096)), whole((32, 4096))] + [whole((4, 8))] * 4 + [whole((1, 8))],
        (block,) + (whole((32, 4096)),) * 3,
        flops=10**9,
        moved=2 * 10**6,
    )(
        me,
        features.reshape(128, 4096),
        cotangent.reshape(32, 4096),
        edge_links.T,
        edge_turns.T,
        corner_links.T,
        corner_turns.T,
        child_slot.reshape(1, 8),
    )
    tiles = to_peers([None] + list(tiles))[1:]
    pieces, *tiles = lax.optimization_barrier((to_nodes(pieces), *tiles))
    picked, slots = call(
        pick_body,
        (msg, jax.ShapeDtypeStruct((8, 512), F32)),
        (4,),
        [msg_spec],
        (block, pl.BlockSpec((8, 128), lambda i: (0, i))),
        flops=10**9,
        moved=10**6,
    )(pieces)
    picked = to_nodes(picked)
    group = jax.ShapeDtypeStruct((192, 384), BF)
    picked = call(
        regroup_body,
        (group,) * 4,
        (1,),
        [scalar, msg_spec, whole((16, 576)), whole((1, 16)), whole((64, 64))],
        (whole((192, 384)),) * 4,
        flops=4 * 10**8,
        moved=10**6,
    )(me, picked, conv_weight, conv_bias.reshape(1, 16), down_weight)
    picked = to_peers(picked)
    pair = pl.BlockSpec((1, 16, 4096), lambda i, m: (i, 0, 0))
    local = pl.pallas_call(
        level_body,
        out_shape=(jax.ShapeDtypeStruct((64, 1024), BF),) * 4,
        grid_spec=pltpu.PrefetchScalarGridSpec(
            num_scalar_prefetch=1,
            grid=(2,),
            in_specs=[pl.BlockSpec((1, 16, 4096), lambda i, m: (m[0] * 2 + i, 0, 0))]
            + [pair] * 3
            + [whole((192, 384))] * 4,
            out_specs=(whole((64, 1024)),) * 4,
            scratch_shapes=(
                pltpu.VMEM((4, 16, 4096), BF),
                pltpu.VMEM((4, 192, 384), BF),
                pltpu.VMEM((4, 64, 1024), BF),
                pltpu.VMEM((1024, 1024), BF),
                pltpu.VMEM((1024, 256), F32),
                pltpu.VMEM((64, 256), F32),
                pltpu.VMEM((256, 128), F32),
                pltpu.VMEM((256, 1024), BF),
                pltpu.VMEM((64, 256), BF),
                pltpu.VMEM((256, 64), BF),
                pltpu.VMEM((256, 128), F32),
            ),
        ),
        compiler_params=pltpu.CompilerParams(vmem_limit_bytes=48 << 20),
        cost_estimate=pl.CostEstimate(flops=4 * 10**9, bytes_accessed=4 * 10**6, transcendentals=0),
    )(me, features, *[t.reshape(2, 16, 4096) for t in tiles], *picked)
    local = to_peers(local)
    out = call(
        spread_body,
        msg,
        (4,),
        [scalar] + [whole((64, 1024))] * 4,
        block,
        (pltpu.VMEM((4, 64, 1024), BF),),
        flops=4 * 10**8,
        moved=10**6,
    )(me, *local)
    out = to_nodes(out)
    out = call(place_body, msg, (4,), [msg_spec, whole((8, 512))], block, flops=5 * 10**8, moved=10**6)(
        out, slots
    )
    out = to_nodes(out)
    coarse, grad_conv, grad_down, grad_bias = call(
        finish_body,
        (
            jax.ShapeDtypeStruct((32, 4096), BF),
            jax.ShapeDtypeStruct((16, 576), F32),
            jax.ShapeDtypeStruct((64, 64), F32),
            jax.ShapeDtypeStruct((1, 16), F32),
        ),
        (4,),
        [msg_spec],
        (
            pl.BlockSpec((32, 1024), lambda i: (0, i)),
            whole((16, 576)),
            whole((64, 64)),
            whole((1, 16)),
        ),
        flops=4 * 10**8,
        moved=10**6,
    )(out)
    return (coarse.reshape(2, 16, 4096), grad_conv, grad_bias.reshape(16), grad_down)


def solution(mesh):
    in_specs = (
        P("tile", "chan", None),
        P("chan", None),
        P("chan"),
        P(None, "chan"),
        P("tile", "chan", None),
        P("tile", None),
        P("tile", None),
        P("tile", None),
        P("tile", None),
        P("tile"),
    )
    out_specs = (P("tile", "chan", None), P("chan", None), P("chan"), P(None, "chan"))
    return jax.shard_map(
        on_device, mesh=mesh, in_specs=in_specs, out_specs=out_specs, check_vma=False
    )
```

```python
import jax
import jax.numpy as jnp
from jax import lax
from jax.experimental import pallas as pl
from jax.experimental.pallas import tpu as pltpu
from jax.sharding import PartitionSpec as P

BF = jnp.bfloat16
F32 = jnp.float32
NODES = 64
MSG = (NODES * 8, 384)


def iota(shape, dim):
    return lax.broadcasted_iota(jnp.int32, shape, dim)


def down_col(n, start=0):
    return iota((n, 1), 0) + start


def lane_row(n):
    return iota((1, n), 1)


def ones_where(mask):
    return jnp.where(mask, 1.0, 0.0).astype(BF)


def keep(mask, x):
    return jnp.where(mask, x, 0.0).astype(BF)


def mm(a, b):
    return jnp.dot(a, b, preferred_element_type=F32)


def mm_nt(a, b):
    return lax.dot_general(a, b, (((1,), (1,)), ((), ())), preferred_element_type=F32)


def halves(x):
    high = x.astype(BF)
    return high, (x - high.astype(F32)).astype(BF)


def call(body, out_shape, grid, in_specs, out_specs, scratch=(), flops=0, moved=0):
    return pl.pallas_call(
        body,
        out_shape=out_shape,
        grid=grid,
        in_specs=in_specs,
        out_specs=out_specs,
        scratch_shapes=scratch,
        compiler_params=pltpu.CompilerParams(vmem_limit_bytes=48 << 20),
        cost_estimate=pl.CostEstimate(flops=flops, bytes_accessed=moved, transcendentals=0),
    )


def whole(shape):
    return pl.BlockSpec(shape, lambda *i: (0,) * len(shape))


def send_body(me_ref, feat_ref, cot_ref, el_ref, et_ref, cl_ref, ct_ref, slot_ref, out_ref, *peer_refs):
    for d in range(1, 4):
        peer = me_ref[0] ^ d
        peer_refs[d - 1][...] = feat_ref[pl.ds(pl.multiple_of(peer * 32, 32), 32), :]

    cot = cot_ref[...]
    stack = jnp.concatenate([cot[:, q * 256 : q * 256 + 256] for q in range(16)], axis=0)
    row = down_col(512)
    k, g, a, qr, hf = row >> 5, (row >> 3) & 3, (row >> 2) & 1, (row >> 1) & 1, row & 1
    source = (qr << 8) | (g << 6) | (hf << 5) | (a << 4) | k
    out_ref[:, 0:256] = mm(ones_where(lane_row(512) == source), stack).astype(BF)

    first = feat_ref[:, 0:128]
    last = feat_ref[:, 3968:4096]
    p = down_col(64)
    lane = lane_row(128)
    rim_n = mm_nt(ones_where(lane == 63 - p), first)
    rim_s = mm_nt(ones_where(lane == 64 + p), last)
    pc = down_col(128)
    pos = pc & 63
    want = jnp.where(pc < 64, pos * 64, (63 - pos) * 64 + 63)
    rim_we = mm_nt(ones_where(lane_row(4096) == want), feat_ref[...])
    cr = down_col(16)
    at_first = jnp.where(cr == 0, 0, jnp.where(cr == 3, 63, -1))
    at_last = jnp.where(cr == 1, 64, jnp.where(cr == 2, 127, -1))
    corners = mm_nt(ones_where(lane == at_first), first) + mm_nt(ones_where(lane == at_last), last)
    tc = down_col(128)
    by_chan = jnp.zeros((16, 128), F32)
    for c in range(4):
        spread = jnp.broadcast_to(corners[c : c + 1, :], (16, 128))
        by_chan = by_chan + mm(keep((lane & 15) == cr, spread), ones_where(lane == (tc >> 4) * 4 + c))

    def over_lanes(x):
        rows = jnp.zeros((x.shape[0], 128), jnp.int32)
        for t in range(8):
            rows = jnp.where((lane & 7) == t, x[:, t : t + 1], rows)
        return rows

    def in_row(x, first_field):
        rows = over_lanes(x)
        side = iota(rows.shape, 0)
        mine = (iota(rows.shape, 1) >> 3) == side + first_field
        return jnp.sum(jnp.where(mine, rows, 0).astype(F32), axis=0, keepdims=True)

    side = iota((4, 8), 0)
    el, cl, slot = el_ref[...], cl_ref[...], slot_ref[...]
    edge = in_row(el >> 3, 0) + in_row((side + 2 + et_ref[...]) & 3, 4) + in_row(el & 7, 8)
    edge = edge + in_row(slot >> 3, 12) + in_row(slot & 7, 13)
    node = over_lanes(jnp.where(cl < 0, 127, cl >> 3)).astype(F32)
    pixel = over_lanes((cl & 7) * 4 + ((side + 2 + ct_ref[...]) & 3)).astype(F32)
    field = lane >> 3
    sub = down_col(16)
    small = jnp.where(sub == 0, edge, 0.0)
    for part in range(4):
        line = jnp.where(field == 14, node[part : part + 1, :], 0.0)
        line = jnp.where(field == 15, pixel[part : part + 1, :], line)
        small = small + jnp.where(sub == part + 1, line, 0.0)
    parts = [rim_n, rim_we[0:64], rim_s, rim_we[64:128], by_chan, small, jnp.zeros((96, 128), F32)]
    stack = jnp.concatenate([x.astype(BF) for x in parts], axis=0)
    r, node = row & 7, row >> 3
    source = jnp.where(r == 4, 256 + (node & 15), jnp.where(r == 5, 272, jnp.where(r == 6, 273 + (node >> 4), -1)))
    source = jnp.where(r < 4, r * 64 + node, source)
    out_ref[:, 256:384] = mm(ones_where(lane_row(384) == source), stack).astype(BF)


def pick_body(msg_ref, out_ref, slot_ref):
    cot = msg_ref[:, 0:256]
    misc = msg_ref[:, 256:384]
    col = lane_row(512)
    lane = lane_row(128)
    sub = down_col(512)
    near = down_col(128)
    base = (sub >> 3) << 3
    both = mm(ones_where((col == base + 5) | (col == base + 6)), misc)
    fields = mm(keep((lane & 7) == (sub & 7), both), ones_where((near >> 3) == lane))
    flip = fields.T
    slot_ref[...] = jnp.broadcast_to(flip[12:13, :] * 8.0 + flip[13:14, :], (8, 512))
    num = fields.astype(jnp.int32)

    def field(f):
        return num[:, f : f + 1]

    slot_row = field(12) * 8 + ((field(13) >> 1) << 1)
    lane2 = lane_row(256)
    fold_r = down_col(256)
    fold = ones_where(lane == (((fold_r >> 6) << 5) | (fold_r & 31)))
    mine = ((lane2 >> 5) & 1) == (field(13) & 1)
    for hf in range(2):
        got = mm(ones_where(col == slot_row + hf), cot)
        out_ref[:, hf * 128 : hf * 128 + 128] = mm(keep(mine, got), fold).astype(BF)
    total = jnp.zeros((512, 128), F32)
    for k in range(4):
        got = mm(ones_where(col == field(k) * 8 + field(4 + k)), misc)
        place = ones_where(lane == k * 16 + (near & 15))
        total = total + mm(keep((lane >> 4) == field(8 + k), got), place)
    got = mm(ones_where(col == field(14) * 8 + 4), misc)
    total = total + mm(keep(lane == field(15), got), ones_where(jnp.broadcast_to(lane == 64, (128, 128))))
    out_ref[:, 256:384] = total.astype(BF)


def regroup_body(me_ref, msg_ref, conv_ref, bias_ref, down_ref, *out_refs):
    row = down_col(128)
    col = lane_row(512)
    pair, g, k, p = row >> 6, (row >> 4) & 3, row & 15, row & 63
    zero = jnp.zeros((64, 64), BF)
    lane = lane_row(128)
    bias = jnp.where(lane_row(16) == down_col(16), bias_ref[...], 0.0)
    bias = jnp.sum(bias, axis=1, keepdims=True)
    b0 = bias.astype(BF).astype(F32)
    b1 = (bias - b0).astype(BF).astype(F32)
    b2 = (bias - b0) - b1
    bias = jnp.where(lane == 0, b0, jnp.where(lane == 1, b1, jnp.where(lane == 2, b2, 0.0))).astype(BF)
    for d in range(4):
        out_ref = out_refs[d]
        tile = ((me_ref[0] ^ d) << 1) | pair
        out_ref[0:128, 0:256] = mm(
            ones_where(col == ((k << 5) | (g << 3) | tile)), msg_ref[:, 0:256]
        ).astype(BF)
        out_ref[0:128, 256:384] = mm(ones_where(col == ((p << 3) | tile)), msg_ref[:, 256:384]).astype(BF)
        out_ref[128:192, 0:128] = jnp.concatenate([down_ref[...], zero], axis=1)
        out_ref[128:144, 128:384] = conv_ref[:, 0:256]
        out_ref[144:160, 128:384] = conv_ref[:, 256:512]
        out_ref[160:176, 128:256] = jnp.concatenate([conv_ref[:, 512:576], zero[0:16]], axis=1)
        out_ref[160:176, 256:384] = bias
        out_ref[176:192, 128:384] = jnp.zeros((16, 256), BF)


def lay_weights(raw_ref, w_ref, down_ref, down_t_ref, bias_ref):
    raw = jnp.concatenate(
        [
            jnp.concatenate([raw_ref[c, 128 + q * 16 : 144 + q * 16, 128 : 128 + n] for c in range(4)], axis=0)
            for q, n in ((0, 256), (1, 256), (2, 128))
        ],
        axis=1,
    )
    e = iota((640, 1), 0)
    i = (e * 7282) >> 16
    tap = e - i * 9
    dy = (tap * 86) >> 8
    to = jnp.where(e < 576, dy * 256 + (tap - dy * 3) * 64 + i, -9999)
    col = lane_row(1536)
    shifted = mm(raw, ones_where(jnp.where(col < 768, col, col - 832) == to)).astype(BF)
    zero = jnp.zeros((64, 256), BF)
    for a in range(2):
        for b in range(2):
            part = shifted[:, b * 768 : b * 768 + 768]
            row = (a * 2 + b) * 64
            w_ref[row : row + 64, :] = jnp.concatenate([zero, part] if a else [part, zero], axis=1)
    down = jnp.zeros((64, 256), F32)
    down_t = jnp.zeros((256, 64), F32)
    for c in range(4):
        mine = raw_ref[c, 128:192, 0:128]
        l = down_col(128)
        to = jnp.where(l < 64, (l & 3) * 64 + c * 16 + (l >> 2), -1)
        down = down + mm(mine, ones_where(lane_row(256) == to))
        l = lane_row(128)
        to = jnp.where(l < 64, (l & 3) * 64 + c * 16 + (l >> 2), -1)
        down_t = down_t + mm_nt(ones_where(down_col(256) == to), mine)
    down_ref[...] = down.astype(BF)
    down_t_ref[...] = down_t.astype(BF)
    bias = jnp.concatenate([raw_ref[c, 160:176, 256:259].astype(F32) for c in range(4)], axis=0)
    bias = (bias[:, 0:1] + bias[:, 1:2]) + bias[:, 2:3]
    bias_ref[...] = jnp.broadcast_to(jnp.concatenate([bias] * 4, axis=0), (256, 128))


def level_body(me_ref, *refs):
    feat_refs, in_refs, out_refs = refs[0:4], refs[4:8], refs[8:12]
    x_ref, msg_ref, sum_ref, win_ref, gc_ref, gd_ref, gb_ref, w_ref, down_ref, down_t_ref, bias_ref = refs[12:]
    step = pl.program_id(0)
    me = me_ref[0]

    @pl.when(step == 0)
    def _():
        for d in range(4):
            msg_ref[me ^ d] = in_refs[d][...]
        lay_weights(msg_ref, w_ref, down_ref, down_t_ref, bias_ref)

    for d in range(4):
        x_ref[me ^ d] = feat_refs[d][0]
    half = pl.multiple_of(step * 64, 64)
    x = jnp.concatenate([x_ref[c] for c in range(4)], axis=0)
    stack = jnp.concatenate([x[:, q * 512 : q * 512 + 512] for q in range(8)], axis=0)
    l_in = down_col(512)
    to = (
        (((l_in >> 6) & 1) << 8)
        | ((l_in & 1) << 7)
        | ((l_in >> 7) << 5)
        | ((l_in >> 1) & 31)
    )
    split = mm(stack, ones_where(lane_row(512) == to))

    def plane(a, b):
        s = (a * 2 + b) * 128
        return jnp.concatenate([split[q * 64 : q * 64 + 64, s : s + 128] for q in range(8)], axis=1)

    rim = [msg_ref[c, pl.ds(half, 64), 256:384].astype(F32) for c in range(4)]
    flip = [r.T.astype(BF) for r in rim]

    def strip(k):
        return jnp.concatenate([f[k * 16 : k * 16 + 16, :] for f in flip], axis=0)

    def corner(k):
        return jnp.concatenate([r[k * 16 : k * 16 + 16, 64:65] for r in rim], axis=0)

    lane = lane_row(1024)
    v = lane & 31
    pos = down_col(64)
    cols = []
    for a in range(2):
        y = ((lane >> 5) << 1) + a
        west = jnp.where(v == 0, 63 - y, -1)
        east = jnp.where(v == 31, y, -1)
        side = mm(strip(1), ones_where(west == pos)) + mm(strip(3), ones_where(east == pos))
        even, odd = plane(a, 0), plane(a, 1)
        cols.append(
            [
                jnp.where(v == 0, side, pltpu.roll(odd, 1, axis=1)),
                even,
                odd,
                jnp.where(v == 31, side, pltpu.roll(even, 1023, axis=1)),
            ]
        )
    lane_e = lane_row(512)
    inner = lane_e & 127
    at = ((inner & 31) << 1) + (lane_e >> 7)
    north = jnp.where(inner < 32, at - 1, -1)
    south = jnp.where(inner >= 96, 64 - at, -1)
    ends = mm(strip(0), ones_where(north == pos)) + mm(strip(2), ones_where(south == pos))
    for spot, k in ((0, 0), (96, 1), (384 + 31, 3), (384 + 127, 2)):
        ends = jnp.where(lane_e == spot, corner(k), ends)
    blank = jnp.zeros((64, 896), F32)
    for cx in range(4):
        end = ends[:, cx * 128 : cx * 128 + 128]
        top = jnp.where(lane < 32, jnp.concatenate([end, blank], axis=1), pltpu.roll(cols[1][cx], 32, axis=1))
        low = jnp.where(lane >= 992, jnp.concatenate([blank, end], axis=1), pltpu.roll(cols[0][cx], 992, axis=1))
        for ry, w in enumerate((top, cols[0][cx], cols[1][cx], low)):
            at_row = (ry * 4 + cx) * 64
            win_ref[at_row : at_row + 64, :] = w.astype(BF)

    pre = mm(w_ref[...], win_ref[...]) + bias_ref[:, 0:1]
    sig = 1.0 / (1.0 + jnp.exp(-pre))
    hidden = (pre * sig).astype(BF)
    quarter = mm(down_ref[...], hidden).astype(BF)
    for c in range(4):
        sum_ref[c, pl.ds(pl.multiple_of(step * 16, 16), 16), :] = quarter[c * 16 : c * 16 + 16, :]
    back = jnp.concatenate(
        [
            jnp.concatenate(
                [msg_ref[c, pl.ds(half + g * 16, 16), 0:256] for c in range(4)], axis=0
            )
            for g in range(4)
        ],
        axis=1,
    )
    grad_hidden = mm(down_t_ref[...], back)
    grad_pre = (grad_hidden * (sig * (1.0 + pre * (1.0 - sig)))).astype(BF)

    @pl.when(step == 0)
    def _():
        gc_ref[...] = jnp.zeros_like(gc_ref)
        gd_ref[...] = jnp.zeros_like(gd_ref)
        gb_ref[...] = jnp.zeros_like(gb_ref)

    gb_ref[...] += jnp.broadcast_to(jnp.sum(grad_pre.astype(F32), axis=1, keepdims=True), (256, 128))
    gd_ref[...] += mm_nt(back, hidden)
    gc_ref[...] += mm_nt(win_ref[...], grad_pre)

    @pl.when(step == 1)
    def _():
        rows = []
        for dy in range(3):
            for cx in range(4):
                r0, r1 = (dy * 4 + cx) * 64, ((dy + 1) * 4 + cx) * 64
                rows.append(gc_ref[r0 : r0 + 64, 0:128] + gc_ref[r1 : r1 + 64, 128:256])
        taps = []
        for dy in range(3):
            for dx in range(3):
                taps.append(rows[dy * 4 + dx] + pltpu.roll(rows[dy * 4 + dx + 1], 64, axis=1))
        taps.append(jnp.zeros((64, 128), F32))
        conv = jnp.concatenate(taps, axis=0)
        conv = jnp.concatenate([conv[q * 128 : q * 128 + 128, :].T for q in range(5)], axis=1)[0:64, :]
        kk = down_col(640)
        cc = lane_row(1024)
        i, tap = kk & 63, kk >> 6
        place = ones_where(cc == jnp.where(tap < 9, ((i >> 4) << 8) + (i & 15) * 9 + tap, -1))
        conv = [mm(h, place) for h in halves(conv)]
        kk = down_col(256)
        i, ab = kk & 63, kk >> 6
        place = ones_where(cc == ((i >> 4) << 8) + 144 + (i & 15) * 4 + ab)
        down = [mm(h, place) for h in halves(gd_ref[...])]
        gb = gb_ref[0:64, :] + gb_ref[64:128, :] + gb_ref[128:192, :] + gb_ref[192:256, :]
        bias = [h.astype(F32)[:, 0:1] for h in halves(gb)]
        lane16 = lane_row(1024)
        for part in range(2):
            for c in range(4):
                d = jnp.concatenate(
                    [down[part][s * 16 : s * 16 + 16, c * 256 : c * 256 + 256] for s in range(4)], axis=1
                )
                both = conv[part][c * 16 : c * 16 + 16, :] + d
                both = jnp.where(lane16 == 208, bias[part][c * 16 : c * 16 + 16, :], both)
                sum_ref[c, 32 + part * 16 : 48 + part * 16, :] = both.astype(BF)
        for d in range(4):
            out_refs[d][...] = sum_ref[me ^ d]


def spread_body(me_ref, *refs):
    in_refs, out_ref, msg_ref = refs[0:4], refs[4], refs[5]
    for d in range(4):
        msg_ref[me_ref[0] ^ d] = in_refs[d][...]
    stack = jnp.concatenate(
        [msg_ref[c, 0:32, g * 256 : g * 256 + 256] for g in range(4) for c in range(4)], axis=0
    )
    row = down_col(512)
    source = (((row >> 3) & 3) << 7) | (((row >> 1) & 3) << 5) | ((row & 1) << 4) | (row >> 5)
    out_ref[:, 0:256] = mm(ones_where(lane_row(512) == source), stack).astype(BF)
    total = jnp.zeros((16, 1024), F32)
    for c in range(4):
        total = total + (msg_ref[c, 32:48, :].astype(F32) + msg_ref[c, 48:64, :].astype(F32))
    parts = [
        h[:, s * 256 + o : s * 256 + o + 128] for h in halves(total) for o in (0, 128) for s in range(4)
    ]
    stack = jnp.concatenate(parts, axis=0)
    r, p = row & 7, row >> 3
    source = jnp.where(r < 4, (r << 6) + p, -1)
    out_ref[:, 256:384] = mm(ones_where(lane_row(256) == source), stack).astype(BF)


def place_body(msg_ref, slot_ref, out_ref):
    quarter = msg_ref[:, 0:256]
    slot = slot_ref[0:1, :].astype(jnp.int32)
    row = down_col(512)
    lane = lane_row(256)
    half = row & 1
    li = down_col(256)
    to = (((li >> 5) & 3) << 6) | (li & 31)
    total = jnp.zeros((512, 256), F32)
    for qc in range(2):
        got = mm(ones_where(slot == ((row >> 1) << 1) + qc), quarter)
        total = total + mm(keep((lane >> 7) == half, got), ones_where(lane == to + qc * 32))
    out_ref[:, 0:256] = total.astype(BF)
    r = down_col(16)
    src = lane_row(512) & 7
    src = jnp.where(src < 4, src & 1, -1)
    summed = mm(ones_where(src == jnp.where(r < 4, r & 1, -2)), msg_ref[:, 256:384])
    high, low = halves(summed)
    both = jnp.where(iota((16, 128), 0) < 2, high.astype(F32), low.astype(F32)).astype(BF)
    r = row & 7
    out_ref[:, 256:384] = mm(ones_where(lane_row(16) == jnp.where(r < 4, r, -1)), both).astype(BF)


def finish_body(msg_ref, coarse_ref, conv_ref, down_ref, bias_ref):
    row = down_col(512)
    col = lane_row(512)
    qr, g, hf, a, k = row >> 8, (row >> 6) & 3, (row >> 5) & 1, (row >> 4) & 1, row & 15
    source = (k << 5) | (g << 3) | (a << 2) | (qr << 1) | hf
    got = mm(ones_where(col == source), msg_ref[:, 0:256]).astype(BF)
    for q in range(16):
        coarse_ref[:, q * 256 : q * 256 + 256] = got[q * 32 : q * 32 + 32, :]

    row = down_col(256)
    got = mm(ones_where(col == ((row & 63) << 3) + (row >> 6)), msg_ref[:, 256:384])
    near = down_col(1024)
    to = jnp.where((near & 255) < 144, (near >> 8) * 144 + (near & 255), -1)
    place = ones_where(lane_row(576) == to)
    lane = lane_row(128)
    shift = ones_where(down_col(128) == jnp.where(lane < 64, lane + 16, -1))
    conv = jnp.zeros((16, 576), F32)
    down = jnp.zeros((64, 128), F32)
    for h in range(2):
        low, high = got[h * 128 : h * 128 + 64, :], got[h * 128 + 64 : h * 128 + 128, :]
        wide = jnp.concatenate(
            [x[s * 16 : s * 16 + 16, :] for s in range(4) for x in (low, high)], axis=1
        )
        conv = conv + mm(wide.astype(BF), place)
        down = down + mm(high.astype(BF), shift)
    conv_ref[...] = conv
    down_ref[...] = down[:, 0:64]
    bias = got[64:80, 80:81] + got[192:208, 80:81]
    bias_ref[...] = jnp.sum(jnp.where(lane_row(16) == down_col(16), bias, 0.0), axis=0, keepdims=True)


def to_peers(parts):
    return [parts[0]] + [
        lax.ppermute(parts[d], "chan", [(i, i ^ d) for i in range(4)]) for d in range(1, 4)
    ]


def on_device(
    features,
    conv_weight,
    conv_bias,
    down_weight,
    cotangent,
    edge_links,
    edge_turns,
    corner_links,
    corner_turns,
    child_slot,
):
    msg_spec = whole(MSG)
    msg = jax.ShapeDtypeStruct(MSG, BF)

    def to_nodes(x):
        return lax.all_to_all(x.reshape(64, 8, 384), "tile", 0, 0, tiled=True).reshape(MSG)

    me = lax.axis_index("chan").astype(jnp.int32).reshape(1)
    scalar = pl.BlockSpec(memory_space=pltpu.SMEM)
    peer_rows = jax.ShapeDtypeStruct((32, 4096), BF)
    pieces, *tiles = call(
        send_body,
        (msg, peer_rows, peer_rows, peer_rows),
        (1,),
        [scalar, whole((128, 4096)), whole((32, 4096))] + [whole((4, 8))] * 4 + [whole((1, 8))],
        (msg_spec,) + (whole((32, 4096)),) * 3,
        flops=10**9,
        moved=2 * 10**6,
    )(
        me,
        features.reshape(128, 4096),
        cotangent.reshape(32, 4096),
        edge_links.T,
        edge_turns.T,
        corner_links.T,
        corner_turns.T,
        child_slot.reshape(1, 8),
    )
    tiles = to_peers([None] + list(tiles))[1:]
    pieces, *tiles = lax.optimization_barrier((to_nodes(pieces), *tiles))
    picked, slots = call(
        pick_body,
        (msg, jax.ShapeDtypeStruct((8, 512), F32)),
        (1,),
        [msg_spec],
        (msg_spec, whole((8, 512))),
        flops=10**9,
        moved=10**6,
    )(pieces)
    picked = to_nodes(picked)
    group = jax.ShapeDtypeStruct((192, 384), BF)
    picked = call(
        regroup_body,
        (group,) * 4,
        (1,),
        [scalar, msg_spec, whole((16, 576)), whole((1, 16)), whole((64, 64))],
        (whole((192, 384)),) * 4,
        flops=4 * 10**8,
        moved=10**6,
    )(me, picked, conv_weight, conv_bias.reshape(1, 16), down_weight)
    picked = to_peers(picked)
    pair = pl.BlockSpec((1, 16, 4096), lambda i, m: (i, 0, 0))
    local = pl.pallas_call(
        level_body,
        out_shape=(jax.ShapeDtypeStruct((64, 1024), BF),) * 4,
        grid_spec=pltpu.PrefetchScalarGridSpec(
            num_scalar_prefetch=1,
            grid=(2,),
            in_specs=[pl.BlockSpec((1, 16, 4096), lambda i, m: (m[0] * 2 + i, 0, 0))]
            + [pair] * 3
            + [whole((192, 384))] * 4,
            out_specs=(whole((64, 1024)),) * 4,
            scratch_shapes=(
                pltpu.VMEM((4, 16, 4096), BF),
                pltpu.VMEM((4, 192, 384), BF),
                pltpu.VMEM((4, 64, 1024), BF),
                pltpu.VMEM((1024, 1024), BF),
                pltpu.VMEM((1024, 256), F32),
                pltpu.VMEM((64, 256), F32),
                pltpu.VMEM((256, 128), F32),
                pltpu.VMEM((256, 1024), BF),
                pltpu.VMEM((64, 256), BF),
                pltpu.VMEM((256, 64), BF),
                pltpu.VMEM((256, 128), F32),
            ),
        ),
        compiler_params=pltpu.CompilerParams(vmem_limit_bytes=48 << 20),
        cost_estimate=pl.CostEstimate(flops=4 * 10**9, bytes_accessed=4 * 10**6, transcendentals=0),
    )(me, features, *[t.reshape(2, 16, 4096) for t in tiles], *picked)
    local = to_peers(local)
    out = call(
        spread_body,
        msg,
        (1,),
        [scalar] + [whole((64, 1024))] * 4,
        msg_spec,
        (pltpu.VMEM((4, 64, 1024), BF),),
        flops=4 * 10**8,
        moved=10**6,
    )(me, *local)
    out = to_nodes(out)
    out = call(place_body, msg, (1,), [msg_spec, whole((8, 512))], msg_spec, flops=5 * 10**8, moved=10**6)(
        out, slots
    )
    out = to_nodes(out)
    coarse, grad_conv, grad_down, grad_bias = call(
        finish_body,
        (
            jax.ShapeDtypeStruct((32, 4096), BF),
            jax.ShapeDtypeStruct((16, 576), F32),
            jax.ShapeDtypeStruct((64, 64), F32),
            jax.ShapeDtypeStruct((1, 16), F32),
        ),
        (1,),
        [msg_spec],
        (
            whole((32, 4096)),
            whole((16, 576)),
            whole((64, 64)),
            whole((1, 16)),
        ),
        flops=4 * 10**8,
        moved=10**6,
    )(out)
    return (coarse.reshape(2, 16, 4096), grad_conv, grad_bias.reshape(16), grad_down)


def solution(mesh):
    in_specs = (
        P("tile", "chan", None),
        P("chan", None),
        P("chan"),
        P(None, "chan"),
        P("tile", "chan", None),
        P("tile", None),
        P("tile", None),
        P("tile", None),
        P("tile", None),
        P("tile"),
    )
    out_specs = (P("tile", "chan", None), P("chan", None), P("chan"), P(None, "chan"))
    return jax.shard_map(
        on_device, mesh=mesh, in_specs=in_specs, out_specs=out_specs, check_vma=False
    )
```

```python
import jax
import jax.numpy as jnp
from jax import lax
from jax.experimental import pallas as pl
from jax.experimental.pallas import tpu as pltpu
from jax.sharding import PartitionSpec as P

BF = jnp.bfloat16
F32 = jnp.float32
NODES = 64
MSG = (NODES * 8, 384)


def iota(shape, dim):
    return lax.broadcasted_iota(jnp.int32, shape, dim)


def down_col(n, start=0):
    return iota((n, 1), 0) + start


def lane_row(n):
    return iota((1, n), 1)


def ones_where(mask):
    return jnp.where(mask, 1.0, 0.0).astype(BF)


def keep(mask, x):
    return jnp.where(mask, x, 0.0).astype(BF)


def mm(a, b):
    return jnp.dot(a, b, preferred_element_type=F32)


def mm_nt(a, b):
    return lax.dot_general(a, b, (((1,), (1,)), ((), ())), preferred_element_type=F32)


def halves(x):
    high = x.astype(BF)
    return high, (x - high.astype(F32)).astype(BF)


def call(body, out_shape, grid, in_specs, out_specs, scratch=(), flops=0, moved=0):
    return pl.pallas_call(
        body,
        out_shape=out_shape,
        grid=grid,
        in_specs=in_specs,
        out_specs=out_specs,
        scratch_shapes=scratch,
        compiler_params=pltpu.CompilerParams(vmem_limit_bytes=48 << 20),
        cost_estimate=pl.CostEstimate(flops=flops, bytes_accessed=moved, transcendentals=0),
    )


def whole(shape):
    return pl.BlockSpec(shape, lambda *i: (0,) * len(shape))


def pack_weights(conv_ref, bias_ref, down_ref, raw_ref):
    zero = jnp.zeros((64, 64), BF)
    lane = lane_row(128)
    bias = jnp.where(lane_row(16) == down_col(16), bias_ref[...], 0.0)
    bias = jnp.sum(bias, axis=1, keepdims=True)
    b0 = bias.astype(BF).astype(F32)
    b1 = (bias - b0).astype(BF).astype(F32)
    b2 = (bias - b0) - b1
    bias = jnp.where(lane == 0, b0, jnp.where(lane == 1, b1, jnp.where(lane == 2, b2, 0.0))).astype(BF)
    raw_ref[:, 0:128] = jnp.concatenate([down_ref[...], zero], axis=1)
    raw_ref[0:16, 128:384] = conv_ref[:, 0:256]
    raw_ref[16:32, 128:384] = conv_ref[:, 256:512]
    raw_ref[32:48, 128:256] = jnp.concatenate([conv_ref[:, 512:576], zero[0:16]], axis=1)
    raw_ref[32:48, 256:384] = bias
    raw_ref[48:64, 128:384] = jnp.zeros((16, 256), BF)


def send_body(
    me_ref,
    feat_ref,
    cot_ref,
    el_ref,
    et_ref,
    cl_ref,
    ct_ref,
    slot_ref,
    conv_ref,
    bias_ref,
    down_ref,
    out_ref,
    raw_ref,
    *peer_refs,
):
    pack_weights(conv_ref, bias_ref, down_ref, raw_ref)
    for d in range(1, 4):
        peer = me_ref[0] ^ d
        peer_refs[d - 1][...] = feat_ref[pl.ds(pl.multiple_of(peer * 32, 32), 32), :]

    cot = cot_ref[...]
    stack = jnp.concatenate([cot[:, q * 256 : q * 256 + 256] for q in range(16)], axis=0)
    row = down_col(512)
    k, g, a, qr, hf = row >> 5, (row >> 3) & 3, (row >> 2) & 1, (row >> 1) & 1, row & 1
    source = (qr << 8) | (g << 6) | (hf << 5) | (a << 4) | k
    out_ref[:, 0:256] = mm(ones_where(lane_row(512) == source), stack).astype(BF)

    first = feat_ref[:, 0:128]
    last = feat_ref[:, 3968:4096]
    p = down_col(64)
    lane = lane_row(128)
    rim_n = mm_nt(ones_where(lane == 63 - p), first)
    rim_s = mm_nt(ones_where(lane == 64 + p), last)
    pc = down_col(128)
    pos = pc & 63
    want = jnp.where(pc < 64, pos * 64, (63 - pos) * 64 + 63)
    rim_we = mm_nt(ones_where(lane_row(4096) == want), feat_ref[...])
    cr = down_col(16)
    at_first = jnp.where(cr == 0, 0, jnp.where(cr == 3, 63, -1))
    at_last = jnp.where(cr == 1, 64, jnp.where(cr == 2, 127, -1))
    corners = mm_nt(ones_where(lane == at_first), first) + mm_nt(ones_where(lane == at_last), last)
    tc = down_col(128)
    by_chan = jnp.zeros((16, 128), F32)
    for c in range(4):
        spread = jnp.broadcast_to(corners[c : c + 1, :], (16, 128))
        by_chan = by_chan + mm(keep((lane & 15) == cr, spread), ones_where(lane == (tc >> 4) * 4 + c))

    def over_lanes(x):
        rows = jnp.zeros((x.shape[0], 128), jnp.int32)
        for t in range(8):
            rows = jnp.where((lane & 7) == t, x[:, t : t + 1], rows)
        return rows

    def in_row(x, first_field):
        rows = over_lanes(x)
        side = iota(rows.shape, 0)
        mine = (iota(rows.shape, 1) >> 3) == side + first_field
        return jnp.sum(jnp.where(mine, rows, 0).astype(F32), axis=0, keepdims=True)

    side = iota((4, 8), 0)
    el, cl, slot = el_ref[...], cl_ref[...], slot_ref[...]
    edge = in_row(el >> 3, 0) + in_row((side + 2 + et_ref[...]) & 3, 4) + in_row(el & 7, 8)
    edge = edge + in_row(slot >> 3, 12) + in_row(slot & 7, 13)
    node = over_lanes(jnp.where(cl < 0, 127, cl >> 3)).astype(F32)
    pixel = over_lanes((cl & 7) * 4 + ((side + 2 + ct_ref[...]) & 3)).astype(F32)
    field = lane >> 3
    sub = down_col(16)
    small = jnp.where(sub == 0, edge, 0.0)
    for part in range(4):
        line = jnp.where(field == 14, node[part : part + 1, :], 0.0)
        line = jnp.where(field == 15, pixel[part : part + 1, :], line)
        small = small + jnp.where(sub == part + 1, line, 0.0)
    parts = [rim_n, rim_we[0:64], rim_s, rim_we[64:128], by_chan, small, jnp.zeros((96, 128), F32)]
    stack = jnp.concatenate([x.astype(BF) for x in parts], axis=0)
    r, node = row & 7, row >> 3
    source = jnp.where(r == 4, 256 + (node & 15), jnp.where(r == 5, 272, jnp.where(r == 6, 273 + (node >> 4), -1)))
    source = jnp.where(r < 4, r * 64 + node, source)
    out_ref[:, 256:384] = mm(ones_where(lane_row(384) == source), stack).astype(BF)


def pick_body(msg_ref, out_ref, slot_ref):
    cot = msg_ref[:, 0:256]
    misc = msg_ref[:, 256:384]
    col = lane_row(512)
    lane = lane_row(128)
    sub = down_col(512)
    near = down_col(128)
    base = (sub >> 3) << 3
    both = mm(ones_where((col == base + 5) | (col == base + 6)), misc)
    fields = mm(keep((lane & 7) == (sub & 7), both), ones_where((near >> 3) == lane))
    flip = fields.T
    slot_ref[...] = jnp.broadcast_to(flip[12:13, :] * 8.0 + flip[13:14, :], (8, 512))
    num = fields.astype(jnp.int32)

    def field(f):
        return num[:, f : f + 1]

    slot_row = field(12) * 8 + ((field(13) >> 1) << 1)
    lane2 = lane_row(256)
    fold_r = down_col(256)
    fold = ones_where(lane == (((fold_r >> 6) << 5) | (fold_r & 31)))
    mine = ((lane2 >> 5) & 1) == (field(13) & 1)
    for hf in range(2):
        got = mm(ones_where(col == slot_row + hf), cot)
        out_ref[:, hf * 128 : hf * 128 + 128] = mm(keep(mine, got), fold).astype(BF)
    total = jnp.zeros((512, 128), F32)
    for k in range(4):
        got = mm(ones_where(col == field(k) * 8 + field(4 + k)), misc)
        place = ones_where(lane == k * 16 + (near & 15))
        total = total + mm(keep((lane >> 4) == field(8 + k), got), place)
    got = mm(ones_where(col == field(14) * 8 + 4), misc)
    total = total + mm(keep(lane == field(15), got), ones_where(jnp.broadcast_to(lane == 64, (128, 128))))
    out_ref[:, 256:384] = total.astype(BF)


def regroup_body(me_ref, msg_ref, *out_refs):
    row = down_col(128)
    col = lane_row(512)
    lane = lane_row(128)
    pair, g, k, p = row >> 6, (row >> 4) & 3, row & 15, row & 63
    for d in range(4):
        out_ref = out_refs[d]
        tile = ((me_ref[0] ^ d) << 1) | pair
        out_ref[:, 0:256] = mm(ones_where(col == ((k << 5) | (g << 3) | tile)), msg_ref[:, 0:256]).astype(BF)
        got = mm(ones_where(col == ((p << 3) | tile)), msg_ref[:, 256:384])
        rims = jnp.where(lane < 64, got[0:64], pltpu.roll(got[64:128], 64, axis=1))
        pixels = jnp.zeros((16, 128), F32)
        for q in range(8):
            pixels = jnp.where(lane == q, got[q * 16 : q * 16 + 16, 64:65], pixels)
        rest = jnp.zeros((48, 128), F32)
        out_ref[:, 256:384] = jnp.concatenate([rims, pixels, rest], axis=0).astype(BF)


def lay_weights(raw_ref, w_ref, down_ref, down_t_ref, bias_ref):
    raw = jnp.concatenate(
        [
            jnp.concatenate([raw_ref[c, q * 16 : q * 16 + 16, 128 : 128 + n] for c in range(4)], axis=0)
            for q, n in ((0, 256), (1, 256), (2, 128))
        ],
        axis=1,
    )
    e = iota((640, 1), 0)
    i = (e * 7282) >> 16
    tap = e - i * 9
    dy = (tap * 86) >> 8
    to = jnp.where(e < 576, dy * 256 + (tap - dy * 3) * 64 + i, -9999)
    col = lane_row(1536)
    shifted = mm(raw, ones_where(jnp.where(col < 768, col, col - 832) == to)).astype(BF)
    zero = jnp.zeros((64, 256), BF)
    for a in range(2):
        for b in range(2):
            part = shifted[:, b * 768 : b * 768 + 768]
            row = (a * 2 + b) * 64
            w_ref[row : row + 64, :] = jnp.concatenate([zero, part] if a else [part, zero], axis=1)
    down = jnp.zeros((64, 256), F32)
    down_t = jnp.zeros((256, 64), F32)
    for c in range(4):
        mine = raw_ref[c, 0:64, 0:128]
        l = down_col(128)
        to = jnp.where(l < 64, (l & 3) * 64 + c * 16 + (l >> 2), -1)
        down = down + mm(mine, ones_where(lane_row(256) == to))
        l = lane_row(128)
        to = jnp.where(l < 64, (l & 3) * 64 + c * 16 + (l >> 2), -1)
        down_t = down_t + mm_nt(ones_where(down_col(256) == to), mine)
    down_ref[...] = down.astype(BF)
    down_t_ref[...] = down_t.astype(BF)
    bias = jnp.concatenate([raw_ref[c, 32:48, 256:259].astype(F32) for c in range(4)], axis=0)
    bias = (bias[:, 0:1] + bias[:, 1:2]) + bias[:, 2:3]
    bias_ref[...] = jnp.broadcast_to(jnp.concatenate([bias] * 4, axis=0), (256, 128))


def ready_body(me_ref, *refs):
    feat_refs, raw_refs = refs[0:4], refs[4:8]
    win_ref, w_ref, down_ref, down_t_ref, bias_ref, x_ref, raw_ref = refs[8:]
    me = me_ref[0]
    for d in range(4):
        raw_ref[me ^ d] = raw_refs[d][...]
        x_ref[me ^ d] = feat_refs[d][...]
    lay_weights(raw_ref, w_ref, down_ref, down_t_ref, bias_ref)
    l_in = down_col(512)
    to = (((l_in >> 6) & 1) << 8) | ((l_in & 1) << 7) | ((l_in >> 7) << 5) | ((l_in >> 1) & 31)
    order = ones_where(lane_row(512) == to)
    lane = lane_row(1024)
    v = lane & 31
    for t in range(2):
        x = jnp.concatenate([x_ref[c, t * 16 : t * 16 + 16, :] for c in range(4)], axis=0)
        stack = jnp.concatenate([x[:, q * 512 : q * 512 + 512] for q in range(8)], axis=0)
        split = mm(stack, order)
        cols = []
        for a in range(2):
            even, odd = [
                jnp.concatenate(
                    [split[q * 64 : q * 64 + 64, (a * 2 + b) * 128 : (a * 2 + b) * 128 + 128] for q in range(8)],
                    axis=1,
                )
                for b in range(2)
            ]
            cols.append(
                [
                    jnp.where(v == 0, 0.0, pltpu.roll(odd, 1, axis=1)),
                    even,
                    odd,
                    jnp.where(v == 31, 0.0, pltpu.roll(even, 1023, axis=1)),
                ]
            )
        for cx in range(4):
            top = jnp.where(lane < 32, 0.0, pltpu.roll(cols[1][cx], 32, axis=1))
            low = jnp.where(lane >= 992, 0.0, pltpu.roll(cols[0][cx], 992, axis=1))
            for ry, w in enumerate((top, cols[0][cx], cols[1][cx], low)):
                row = (ry * 4 + cx) * 64
                win_ref[t, row : row + 64, :] = w.astype(BF)


def level_body(me_ref, *refs):
    in_refs, (base_ref, w_ref, down_ref, down_t_ref, bias_ref) = refs[0:4], refs[4:9]
    out_refs, (msg_ref, sum_ref, win_ref, gc_ref) = refs[9:13], refs[13:]
    me = me_ref[0]
    for d in range(4):
        msg_ref[me ^ d] = in_refs[d][...]
    flip = [msg_ref[c, 0:64, 256:384].astype(F32).T.astype(BF) for c in range(4)]

    def strip(k):
        return jnp.concatenate(
            [f[t * 64 + k * 16 : t * 64 + k * 16 + 16, :] for t in range(2) for f in flip], axis=0
        )

    pixels = jnp.concatenate([msg_ref[c, 64:80, 256:384] for c in range(4)], axis=0).astype(F32)
    lane = lane_row(1024)
    v = lane & 31
    pos = down_col(64)
    sides = {}
    for ry in range(4):
        y = ((lane >> 5) << 1) + (ry - 1)
        sides[ry, 0] = mm(strip(1), ones_where(jnp.where(v == 0, 63 - y, -1) == pos)).astype(BF)
        sides[ry, 3] = mm(strip(3), ones_where(jnp.where(v == 31, y, -1) == pos)).astype(BF)
    lane_e = lane_row(512)
    inner = lane_e & 127
    at = ((inner & 31) << 1) + (lane_e >> 7)
    north = jnp.where(inner < 32, at - 1, -1)
    south = jnp.where(inner >= 96, 64 - at, -1)
    ends = mm(strip(0), ones_where(north == pos)) + mm(strip(2), ones_where(south == pos))
    gd = jnp.zeros((64, 256), F32)
    gb = jnp.zeros((256, 1), F32)
    for t in range(2):
        end = ends[t * 64 : t * 64 + 64, :]
        for spot, k in ((0, 0), (96, 1), (384 + 31, 3), (384 + 127, 2)):
            end = jnp.where(lane_e == spot, pixels[:, t * 4 + k : t * 4 + k + 1], end)
        for ry in range(4):
            for cx in range(4):
                row = (ry * 4 + cx) * 64
                w = base_ref[t, row : row + 64, :]
                if (ry, cx) in sides:
                    w = w + sides[ry, cx][t * 64 : t * 64 + 64, :]
                win_ref[t, row : row + 64, :] = w
                edge = end[:, cx * 128 : cx * 128 + 128]
                if ry == 0:
                    fix = jnp.where(lane_row(128) < 64, edge, 0.0).astype(BF)
                    win_ref[t, row : row + 64, 0:128] = w[:, 0:128] + fix
                if ry == 3:
                    fix = jnp.where(lane_row(128) >= 64, edge, 0.0).astype(BF)
                    win_ref[t, row : row + 64, 896:1024] = w[:, 896:1024] + fix
    for t in range(2):
        pre = mm(w_ref[...], win_ref[t]) + bias_ref[:, 0:1]
        sig = 1.0 / (1.0 + jnp.exp(-pre))
        hidden = (pre * sig).astype(BF)
        quarter = mm(down_ref[...], hidden).astype(BF)
        for c in range(4):
            sum_ref[c, t * 16 : t * 16 + 16, :] = quarter[c * 16 : c * 16 + 16, :]
        back = jnp.concatenate(
            [
                jnp.concatenate(
                    [msg_ref[c, t * 64 + g * 16 : t * 64 + g * 16 + 16, 0:256] for c in range(4)], axis=0
                )
                for g in range(4)
            ],
            axis=1,
        )
        grad_hidden = mm(down_t_ref[...], back)
        grad_pre = (grad_hidden * (sig * (1.0 + pre * (1.0 - sig)))).astype(BF)
        gb = gb + jnp.sum(grad_pre.astype(F32), axis=1, keepdims=True)
        gd = gd + mm_nt(back, hidden)
        part = mm_nt(win_ref[t], grad_pre)
        gc_ref[...] = part if t == 0 else gc_ref[...] + part
    rows = []
    for dy in range(3):
        for cx in range(4):
            r0, r1 = (dy * 4 + cx) * 64, ((dy + 1) * 4 + cx) * 64
            rows.append(gc_ref[r0 : r0 + 64, 0:128] + gc_ref[r1 : r1 + 64, 128:256])
    taps = []
    for dy in range(3):
        for dx in range(3):
            taps.append(rows[dy * 4 + dx] + pltpu.roll(rows[dy * 4 + dx + 1], 64, axis=1))
    taps.append(jnp.zeros((64, 128), F32))
    conv = jnp.concatenate(taps, axis=0)
    conv = jnp.concatenate([conv[q * 128 : q * 128 + 128, :].T for q in range(5)], axis=1)[0:64, :]
    kk = down_col(640)
    cc = lane_row(1024)
    i, tap = kk & 63, kk >> 6
    place = ones_where(cc == jnp.where(tap < 9, ((i >> 4) << 8) + (i & 15) * 9 + tap, -1))
    conv = [mm(h, place) for h in halves(conv)]
    kk = down_col(256)
    i, ab = kk & 63, kk >> 6
    place = ones_where(cc == ((i >> 4) << 8) + 144 + (i & 15) * 4 + ab)
    down = [mm(h, place) for h in halves(gd)]
    gb = gb[0:64, :] + gb[64:128, :] + gb[128:192, :] + gb[192:256, :]
    bias = [h.astype(F32) for h in halves(gb)]
    lane16 = lane_row(1024)
    for part in range(2):
        for c in range(4):
            d = jnp.concatenate(
                [down[part][s * 16 : s * 16 + 16, c * 256 : c * 256 + 256] for s in range(4)], axis=1
            )
            both = conv[part][c * 16 : c * 16 + 16, :] + d
            both = jnp.where(lane16 == 208, bias[part][c * 16 : c * 16 + 16, :], both)
            sum_ref[c, 32 + part * 16 : 48 + part * 16, :] = both.astype(BF)
    for d in range(4):
        out_refs[d][...] = sum_ref[me ^ d]


def spread_body(me_ref, *refs):
    in_refs, out_ref, msg_ref = refs[0:4], refs[4], refs[5]
    for d in range(4):
        msg_ref[me_ref[0] ^ d] = in_refs[d][...]
    stack = jnp.concatenate(
        [msg_ref[c, 0:32, g * 256 : g * 256 + 256] for g in range(4) for c in range(4)], axis=0
    )
    row = down_col(512)
    source = (((row >> 3) & 3) << 7) | (((row >> 1) & 3) << 5) | ((row & 1) << 4) | (row >> 5)
    out_ref[:, 0:256] = mm(ones_where(lane_row(512) == source), stack).astype(BF)
    total = jnp.zeros((16, 1024), F32)
    for c in range(4):
        total = total + (msg_ref[c, 32:48, :].astype(F32) + msg_ref[c, 48:64, :].astype(F32))
    parts = [
        h[:, s * 256 + o : s * 256 + o + 128] for h in halves(total) for o in (0, 128) for s in range(4)
    ]
    stack = jnp.concatenate(parts, axis=0)
    r, p = row & 7, row >> 3
    source = jnp.where(r < 4, (r << 6) + p, -1)
    out_ref[:, 256:384] = mm(ones_where(lane_row(256) == source), stack).astype(BF)


def place_body(msg_ref, slot_ref, out_ref):
    quarter = msg_ref[:, 0:256]
    slot = slot_ref[0:1, :].astype(jnp.int32)
    row = down_col(512)
    lane = lane_row(256)
    half = row & 1
    li = down_col(256)
    to = (((li >> 5) & 3) << 6) | (li & 31)
    total = jnp.zeros((512, 256), F32)
    for qc in range(2):
        got = mm(ones_where(slot == ((row >> 1) << 1) + qc), quarter)
        total = total + mm(keep((lane >> 7) == half, got), ones_where(lane == to + qc * 32))
    out_ref[:, 0:256] = total.astype(BF)
    r = down_col(16)
    src = lane_row(512) & 7
    src = jnp.where(src < 4, src & 1, -1)
    summed = mm(ones_where(src == jnp.where(r < 4, r & 1, -2)), msg_ref[:, 256:384])
    high, low = halves(summed)
    both = jnp.where(iota((16, 128), 0) < 2, high.astype(F32), low.astype(F32)).astype(BF)
    r = row & 7
    out_ref[:, 256:384] = mm(ones_where(lane_row(16) == jnp.where(r < 4, r, -1)), both).astype(BF)


def finish_body(msg_ref, coarse_ref, conv_ref, down_ref, bias_ref):
    row = down_col(512)
    col = lane_row(512)
    qr, g, hf, a, k = row >> 8, (row >> 6) & 3, (row >> 5) & 1, (row >> 4) & 1, row & 15
    source = (k << 5) | (g << 3) | (a << 2) | (qr << 1) | hf
    got = mm(ones_where(col == source), msg_ref[:, 0:256]).astype(BF)
    for q in range(16):
        coarse_ref[:, q * 256 : q * 256 + 256] = got[q * 32 : q * 32 + 32, :]

    row = down_col(256)
    got = mm(ones_where(col == ((row & 63) << 3) + (row >> 6)), msg_ref[:, 256:384])
    near = down_col(1024)
    to = jnp.where((near & 255) < 144, (near >> 8) * 144 + (near & 255), -1)
    place = ones_where(lane_row(576) == to)
    lane = lane_row(128)
    shift = ones_where(down_col(128) == jnp.where(lane < 64, lane + 16, -1))
    conv = jnp.zeros((16, 576), F32)
    down = jnp.zeros((64, 128), F32)
    for h in range(2):
        low, high = got[h * 128 : h * 128 + 64, :], got[h * 128 + 64 : h * 128 + 128, :]
        wide = jnp.concatenate(
            [x[s * 16 : s * 16 + 16, :] for s in range(4) for x in (low, high)], axis=1
        )
        conv = conv + mm(wide.astype(BF), place)
        down = down + mm(high.astype(BF), shift)
    conv_ref[...] = conv
    down_ref[...] = down[:, 0:64]
    bias = got[64:80, 80:81] + got[192:208, 80:81]
    bias_ref[...] = jnp.sum(jnp.where(lane_row(16) == down_col(16), bias, 0.0), axis=0, keepdims=True)


def to_peers(parts):
    return [parts[0]] + [
        lax.ppermute(parts[d], "chan", [(i, i ^ d) for i in range(4)]) for d in range(1, 4)
    ]


def on_device(
    features,
    conv_weight,
    conv_bias,
    down_weight,
    cotangent,
    edge_links,
    edge_turns,
    corner_links,
    corner_turns,
    child_slot,
):
    msg_spec = whole(MSG)
    msg = jax.ShapeDtypeStruct(MSG, BF)

    def to_nodes(x):
        return lax.all_to_all(x.reshape(64, 8, 384), "tile", 0, 0, tiled=True).reshape(MSG)

    me = lax.axis_index("chan").astype(jnp.int32).reshape(1)
    scalar = pl.BlockSpec(memory_space=pltpu.SMEM)
    peer_rows = jax.ShapeDtypeStruct((32, 4096), BF)
    pieces, raw, *tiles = call(
        send_body,
        (msg, jax.ShapeDtypeStruct((64, 384), BF), peer_rows, peer_rows, peer_rows),
        (1,),
        [scalar, whole((128, 4096)), whole((32, 4096))]
        + [whole((4, 8))] * 4
        + [whole((1, 8)), whole((16, 576)), whole((1, 16)), whole((64, 64))],
        (msg_spec, whole((64, 384))) + (whole((32, 4096)),) * 3,
        flops=10**9,
        moved=2 * 10**6,
    )(
        me,
        *[
            pltpu.with_memory_space_constraint(x, pltpu.HBM)
            for x in (
                features.reshape(128, 4096),
                cotangent.reshape(32, 4096),
                edge_links.T,
                edge_turns.T,
                corner_links.T,
                corner_turns.T,
                child_slot.reshape(1, 8),
                conv_weight,
                conv_bias.reshape(1, 16),
                down_weight,
            )
        ],
    )
    raw = to_peers([raw] * 4)
    tiles = to_peers([None] + list(tiles))[1:]
    pieces, raw, tiles = lax.optimization_barrier((to_nodes(pieces), raw, tiles))
    picked, slots = call(
        pick_body,
        (msg, jax.ShapeDtypeStruct((8, 512), F32)),
        (1,),
        [msg_spec],
        (msg_spec, whole((8, 512))),
        flops=10**9,
        moved=10**6,
    )(pieces)
    picked = to_nodes(picked)
    own = pl.BlockSpec((32, 4096), lambda i, m: (m[0], 0))
    vmem = pl.BlockSpec(memory_space=pltpu.VMEM)
    ready = pl.pallas_call(
        ready_body,
        out_shape=(
            jax.ShapeDtypeStruct((2, 1024, 1024), BF),
            jax.ShapeDtypeStruct((256, 1024), BF),
            jax.ShapeDtypeStruct((64, 256), BF),
            jax.ShapeDtypeStruct((256, 64), BF),
            jax.ShapeDtypeStruct((256, 128), F32),
        ),
        grid_spec=pltpu.PrefetchScalarGridSpec(
            num_scalar_prefetch=1,
            grid=(1,),
            in_specs=[own] + [whole((32, 4096))] * 3 + [whole((64, 384))] * 4,
            out_specs=(vmem,) * 5,
            scratch_shapes=(pltpu.VMEM((4, 32, 4096), BF), pltpu.VMEM((4, 64, 384), BF)),
        ),
        compiler_params=pltpu.CompilerParams(vmem_limit_bytes=32 << 20),
        cost_estimate=pl.CostEstimate(flops=10**9, bytes_accessed=4 * 10**6, transcendentals=0),
    )(me, features.reshape(128, 4096), *tiles, *raw)
    group = jax.ShapeDtypeStruct((128, 384), BF)
    picked = call(
        regroup_body,
        (group,) * 4,
        (1,),
        [scalar, msg_spec],
        (whole((128, 384)),) * 4,
        flops=4 * 10**8,
        moved=10**6,
    )(me, picked)
    picked = to_peers(picked)
    local = pl.pallas_call(
        level_body,
        out_shape=(jax.ShapeDtypeStruct((64, 1024), BF),) * 4,
        in_specs=[scalar] + [vmem] * 9,
        out_specs=(vmem,) * 4,
        scratch_shapes=(
            pltpu.VMEM((4, 128, 384), BF),
            pltpu.VMEM((4, 64, 1024), BF),
            pltpu.VMEM((2, 1024, 1024), BF),
            pltpu.VMEM((1024, 256), F32),
        ),
        compiler_params=pltpu.CompilerParams(vmem_limit_bytes=32 << 20),
        cost_estimate=pl.CostEstimate(flops=4 * 10**9, bytes_accessed=4 * 10**6, transcendentals=0),
    )(me, *picked, *ready)
    local = to_peers(local)
    out = call(
        spread_body,
        msg,
        (1,),
        [scalar] + [whole((64, 1024))] * 4,
        msg_spec,
        (pltpu.VMEM((4, 64, 1024), BF),),
        flops=4 * 10**8,
        moved=10**6,
    )(me, *local)
    out = to_nodes(out)
    out = call(place_body, msg, (1,), [msg_spec, whole((8, 512))], msg_spec, flops=5 * 10**8, moved=10**6)(
        out, slots
    )
    out = to_nodes(out)
    coarse, grad_conv, grad_down, grad_bias = call(
        finish_body,
        (
            jax.ShapeDtypeStruct((32, 4096), BF),
            jax.ShapeDtypeStruct((16, 576), F32),
            jax.ShapeDtypeStruct((64, 64), F32),
            jax.ShapeDtypeStruct((1, 16), F32),
        ),
        (1,),
        [msg_spec],
        (
            whole((32, 4096)),
            whole((16, 576)),
            whole((64, 64)),
            whole((1, 16)),
        ),
        flops=4 * 10**8,
        moved=10**6,
    )(out)
    return (coarse.reshape(2, 16, 4096), grad_conv, grad_bias.reshape(16), grad_down)


def solution(mesh):
    in_specs = (
        P("tile", "chan", None),
        P("chan", None),
        P("chan"),
        P(None, "chan"),
        P("tile", "chan", None),
        P("tile", None),
        P("tile", None),
        P("tile", None),
        P("tile", None),
        P("tile"),
    )
    out_specs = (P("tile", "chan", None), P("chan", None), P("chan"), P(None, "chan"))
    return jax.shard_map(
        on_device, mesh=mesh, in_specs=in_specs, out_specs=out_specs, check_vma=False
    )
```

```python
import jax
import jax.numpy as jnp
from jax import lax
from jax.experimental import pallas as pl
from jax.experimental.pallas import tpu as pltpu
from jax.sharding import PartitionSpec as P

BF = jnp.bfloat16
F32 = jnp.float32
NODES = 64
MSG = (NODES * 8, 384)


def iota(shape, dim):
    return lax.broadcasted_iota(jnp.int32, shape, dim)


def down_col(n, start=0):
    return iota((n, 1), 0) + start


def lane_row(n):
    return iota((1, n), 1)


def ones_where(mask):
    return jnp.where(mask, 1.0, 0.0).astype(BF)


def keep(mask, x):
    return jnp.where(mask, x, 0.0).astype(BF)


def mm(a, b):
    return jnp.dot(a, b, preferred_element_type=F32)


def mm_nt(a, b):
    return lax.dot_general(a, b, (((1,), (1,)), ((), ())), preferred_element_type=F32)


def halves(x):
    high = x.astype(BF)
    return high, (x - high.astype(F32)).astype(BF)


def call(body, out_shape, grid, in_specs, out_specs, scratch=(), flops=0, moved=0):
    return pl.pallas_call(
        body,
        out_shape=out_shape,
        grid=grid,
        in_specs=in_specs,
        out_specs=out_specs,
        scratch_shapes=scratch,
        compiler_params=pltpu.CompilerParams(vmem_limit_bytes=48 << 20),
        cost_estimate=pl.CostEstimate(flops=flops, bytes_accessed=moved, transcendentals=0),
    )


def whole(shape):
    return pl.BlockSpec(shape, lambda *i: (0,) * len(shape))


def pack_weights(conv_ref, bias_ref, down_ref, raw_ref):
    zero = jnp.zeros((64, 64), BF)
    lane = lane_row(128)
    bias = jnp.where(lane_row(16) == down_col(16), bias_ref[...], 0.0)
    bias = jnp.sum(bias, axis=1, keepdims=True)
    b0 = bias.astype(BF).astype(F32)
    b1 = (bias - b0).astype(BF).astype(F32)
    b2 = (bias - b0) - b1
    bias = jnp.where(lane == 0, b0, jnp.where(lane == 1, b1, jnp.where(lane == 2, b2, 0.0))).astype(BF)
    raw_ref[:, 0:128] = jnp.concatenate([down_ref[...], zero], axis=1)
    raw_ref[0:16, 128:384] = conv_ref[:, 0:256]
    raw_ref[16:32, 128:384] = conv_ref[:, 256:512]
    raw_ref[32:48, 128:256] = jnp.concatenate([conv_ref[:, 512:576], zero[0:16]], axis=1)
    raw_ref[32:48, 256:384] = bias
    raw_ref[48:64, 128:384] = jnp.zeros((16, 256), BF)


def send_body(
    me_ref,
    feat_ref,
    cot_ref,
    el_ref,
    et_ref,
    cl_ref,
    ct_ref,
    slot_ref,
    conv_ref,
    bias_ref,
    down_ref,
    out_ref,
    raw_ref,
    *peer_refs,
):
    pack_weights(conv_ref, bias_ref, down_ref, raw_ref)
    for d in range(1, 4):
        peer = me_ref[0] ^ d
        first_ref, second_ref = peer_refs[d - 1], peer_refs[d + 2]
        first_ref[:, 0:4096] = feat_ref[pl.ds(pl.multiple_of(peer * 32, 16), 16), :]
        second_ref[...] = feat_ref[pl.ds(pl.multiple_of(peer * 32 + 16, 16), 16), :]
        for q in range(4):
            first_ref[:, 4096 + q * 384 : 4480 + q * 384] = raw_ref[q * 16 : q * 16 + 16, :]

    cot = cot_ref[...]
    stack = jnp.concatenate([cot[:, q * 256 : q * 256 + 256] for q in range(16)], axis=0)
    row = down_col(512)
    k, g, a, qr, hf = row >> 5, (row >> 3) & 3, (row >> 2) & 1, (row >> 1) & 1, row & 1
    source = (qr << 8) | (g << 6) | (hf << 5) | (a << 4) | k
    out_ref[:, 0:256] = mm(ones_where(lane_row(512) == source), stack).astype(BF)

    first = feat_ref[:, 0:128]
    last = feat_ref[:, 3968:4096]
    p = down_col(64)
    lane = lane_row(128)
    rim_n = mm_nt(ones_where(lane == 63 - p), first)
    rim_s = mm_nt(ones_where(lane == 64 + p), last)
    pc = down_col(128)
    pos = pc & 63
    want = jnp.where(pc < 64, pos * 64, (63 - pos) * 64 + 63)
    rim_we = mm_nt(ones_where(lane_row(4096) == want), feat_ref[...])
    cr = down_col(16)
    at_first = jnp.where(cr == 0, 0, jnp.where(cr == 3, 63, -1))
    at_last = jnp.where(cr == 1, 64, jnp.where(cr == 2, 127, -1))
    corners = mm_nt(ones_where(lane == at_first), first) + mm_nt(ones_where(lane == at_last), last)
    tc = down_col(128)
    by_chan = jnp.zeros((16, 128), F32)
    for c in range(4):
        spread = jnp.broadcast_to(corners[c : c + 1, :], (16, 128))
        by_chan = by_chan + mm(keep((lane & 15) == cr, spread), ones_where(lane == (tc >> 4) * 4 + c))

    def over_lanes(x):
        rows = jnp.zeros((x.shape[0], 128), jnp.int32)
        for t in range(8):
            rows = jnp.where((lane & 7) == t, x[:, t : t + 1], rows)
        return rows

    def in_row(x, first_field):
        rows = over_lanes(x)
        side = iota(rows.shape, 0)
        mine = (iota(rows.shape, 1) >> 3) == side + first_field
        return jnp.sum(jnp.where(mine, rows, 0).astype(F32), axis=0, keepdims=True)

    side = iota((4, 8), 0)
    el, cl, slot = el_ref[...], cl_ref[...], slot_ref[...]
    edge = in_row(el >> 3, 0) + in_row((side + 2 + et_ref[...]) & 3, 4) + in_row(el & 7, 8)
    edge = edge + in_row(slot >> 3, 12) + in_row(slot & 7, 13)
    node = over_lanes(jnp.where(cl < 0, 127, cl >> 3)).astype(F32)
    pixel = over_lanes((cl & 7) * 4 + ((side + 2 + ct_ref[...]) & 3)).astype(F32)
    field = lane >> 3
    sub = down_col(16)
    small = jnp.where(sub == 0, edge, 0.0)
    for part in range(4):
        line = jnp.where(field == 14, node[part : part + 1, :], 0.0)
        line = jnp.where(field == 15, pixel[part : part + 1, :], line)
        small = small + jnp.where(sub == part + 1, line, 0.0)
    parts = [rim_n, rim_we[0:64], rim_s, rim_we[64:128], by_chan, small, jnp.zeros((96, 128), F32)]
    stack = jnp.concatenate([x.astype(BF) for x in parts], axis=0)
    r, node = row & 7, row >> 3
    source = jnp.where(r == 4, 256 + (node & 15), jnp.where(r == 5, 272, jnp.where(r == 6, 273 + (node >> 4), -1)))
    source = jnp.where(r < 4, r * 64 + node, source)
    out_ref[:, 256:384] = mm(ones_where(lane_row(384) == source), stack).astype(BF)


def pick_body(msg_ref, out_ref, slot_ref):
    cot = msg_ref[:, 0:256]
    misc = msg_ref[:, 256:384]
    col = lane_row(512)
    lane = lane_row(128)
    sub = down_col(512)
    near = down_col(128)
    base = (sub >> 3) << 3
    both = mm(ones_where((col == base + 5) | (col == base + 6)), misc)
    fields = mm(keep((lane & 7) == (sub & 7), both), ones_where((near >> 3) == lane))
    flip = fields.T
    slot_ref[...] = jnp.broadcast_to(flip[12:13, :] * 8.0 + flip[13:14, :], (8, 512))
    num = fields.astype(jnp.int32)

    def field(f):
        return num[:, f : f + 1]

    slot_row = field(12) * 8 + ((field(13) >> 1) << 1)
    lane2 = lane_row(256)
    fold_r = down_col(256)
    fold = ones_where(lane == (((fold_r >> 6) << 5) | (fold_r & 31)))
    mine = ((lane2 >> 5) & 1) == (field(13) & 1)
    for hf in range(2):
        got = mm(ones_where(col == slot_row + hf), cot)
        out_ref[:, hf * 128 : hf * 128 + 128] = mm(keep(mine, got), fold).astype(BF)
    total = jnp.zeros((512, 128), F32)
    for k in range(4):
        got = mm(ones_where(col == field(k) * 8 + field(4 + k)), misc)
        place = ones_where(lane == k * 16 + (near & 15))
        total = total + mm(keep((lane >> 4) == field(8 + k), got), place)
    got = mm(ones_where(col == field(14) * 8 + 4), misc)
    total = total + mm(keep(lane == field(15), got), ones_where(jnp.broadcast_to(lane == 64, (128, 128))))
    out_ref[:, 256:384] = total.astype(BF)


def regroup_body(me_ref, msg_ref, *out_refs):
    row = down_col(128)
    col = lane_row(512)
    lane = lane_row(128)
    pair, g, k, p = row >> 6, (row >> 4) & 3, row & 15, row & 63
    for d in range(4):
        out_ref = out_refs[d]
        tile = ((me_ref[0] ^ d) << 1) | pair
        out_ref[:, 0:256] = mm(ones_where(col == ((k << 5) | (g << 3) | tile)), msg_ref[:, 0:256]).astype(BF)
        got = mm(ones_where(col == ((p << 3) | tile)), msg_ref[:, 256:384])
        rims = jnp.where(lane < 64, got[0:64], pltpu.roll(got[64:128], 64, axis=1))
        pixels = jnp.zeros((16, 128), F32)
        for q in range(8):
            pixels = jnp.where(lane == q, got[q * 16 : q * 16 + 16, 64:65], pixels)
        rest = jnp.zeros((48, 128), F32)
        out_ref[:, 256:384] = jnp.concatenate([rims, pixels, rest], axis=0).astype(BF)


def lay_weights(raw_ref, w_ref, down_ref, down_t_ref, bias_ref):
    raw = jnp.concatenate(
        [
            jnp.concatenate([raw_ref[c, q * 16 : q * 16 + 16, 128 : 128 + n] for c in range(4)], axis=0)
            for q, n in ((0, 256), (1, 256), (2, 128))
        ],
        axis=1,
    )
    e = iota((640, 1), 0)
    i = (e * 7282) >> 16
    tap = e - i * 9
    dy = (tap * 86) >> 8
    to = jnp.where(e < 576, dy * 256 + (tap - dy * 3) * 64 + i, -9999)
    col = lane_row(1536)
    shifted = mm(raw, ones_where(jnp.where(col < 768, col, col - 832) == to)).astype(BF)
    zero = jnp.zeros((64, 256), BF)
    for a in range(2):
        for b in range(2):
            part = shifted[:, b * 768 : b * 768 + 768]
            row = (a * 2 + b) * 64
            w_ref[row : row + 64, :] = jnp.concatenate([zero, part] if a else [part, zero], axis=1)
    down = jnp.zeros((64, 256), F32)
    down_t = jnp.zeros((256, 64), F32)
    for c in range(4):
        mine = raw_ref[c, 0:64, 0:128]
        l = down_col(128)
        to = jnp.where(l < 64, (l & 3) * 64 + c * 16 + (l >> 2), -1)
        down = down + mm(mine, ones_where(lane_row(256) == to))
        l = lane_row(128)
        to = jnp.where(l < 64, (l & 3) * 64 + c * 16 + (l >> 2), -1)
        down_t = down_t + mm_nt(ones_where(down_col(256) == to), mine)
    down_ref[...] = down.astype(BF)
    down_t_ref[...] = down_t.astype(BF)
    bias = jnp.concatenate([raw_ref[c, 32:48, 256:259].astype(F32) for c in range(4)], axis=0)
    bias = (bias[:, 0:1] + bias[:, 1:2]) + bias[:, 2:3]
    bias_ref[...] = jnp.broadcast_to(jnp.concatenate([bias] * 4, axis=0), (256, 128))


def ready_body(me_ref, *refs):
    own_ref, own_raw_ref, first_refs, second_refs = refs[0], refs[1], refs[2:5], refs[5:8]
    win_ref, w_ref, down_ref, down_t_ref, bias_ref, x_ref, raw_ref = refs[8:]
    me = me_ref[0]
    raw_ref[me] = own_raw_ref[...]
    x_ref[me] = own_ref[...]
    for d in range(1, 4):
        first_ref = first_refs[d - 1]
        x_ref[me ^ d, 0:16, :] = first_ref[:, 0:4096]
        x_ref[me ^ d, 16:32, :] = second_refs[d - 1][...]
        for q in range(4):
            raw_ref[me ^ d, q * 16 : q * 16 + 16, :] = first_ref[:, 4096 + q * 384 : 4480 + q * 384]
    lay_weights(raw_ref, w_ref, down_ref, down_t_ref, bias_ref)
    l_in = down_col(512)
    to = (((l_in >> 6) & 1) << 8) | ((l_in & 1) << 7) | ((l_in >> 7) << 5) | ((l_in >> 1) & 31)
    order = ones_where(lane_row(512) == to)
    lane = lane_row(1024)
    v = lane & 31
    for t in range(2):
        x = jnp.concatenate([x_ref[c, t * 16 : t * 16 + 16, :] for c in range(4)], axis=0)
        stack = jnp.concatenate([x[:, q * 512 : q * 512 + 512] for q in range(8)], axis=0)
        split = mm(stack, order)
        cols = []
        for a in range(2):
            even, odd = [
                jnp.concatenate(
                    [split[q * 64 : q * 64 + 64, (a * 2 + b) * 128 : (a * 2 + b) * 128 + 128] for q in range(8)],
                    axis=1,
                )
                for b in range(2)
            ]
            cols.append(
                [
                    jnp.where(v == 0, 0.0, pltpu.roll(odd, 1, axis=1)),
                    even,
                    odd,
                    jnp.where(v == 31, 0.0, pltpu.roll(even, 1023, axis=1)),
                ]
            )
        for cx in range(4):
            top = jnp.where(lane < 32, 0.0, pltpu.roll(cols[1][cx], 32, axis=1))
            low = jnp.where(lane >= 992, 0.0, pltpu.roll(cols[0][cx], 992, axis=1))
            for ry, w in enumerate((top, cols[0][cx], cols[1][cx], low)):
                row = (ry * 4 + cx) * 64
                win_ref[t, row : row + 64, :] = w.astype(BF)


def level_body(me_ref, *refs):
    in_refs, (base_ref, w_ref, down_ref, down_t_ref, bias_ref) = refs[0:4], refs[4:9]
    out_refs, (msg_ref, sum_ref, win_ref, gc_ref) = refs[9:13], refs[13:]
    me = me_ref[0]
    for d in range(4):
        msg_ref[me ^ d] = in_refs[d][...]
    flip = [msg_ref[c, 0:64, 256:384].astype(F32).T.astype(BF) for c in range(4)]

    def strip(k):
        return jnp.concatenate(
            [f[t * 64 + k * 16 : t * 64 + k * 16 + 16, :] for t in range(2) for f in flip], axis=0
        )

    pixels = jnp.concatenate([msg_ref[c, 64:80, 256:384] for c in range(4)], axis=0).astype(F32)
    lane = lane_row(1024)
    v = lane & 31
    pos = down_col(64)
    sides = {}
    for ry in range(4):
        y = ((lane >> 5) << 1) + (ry - 1)
        sides[ry, 0] = mm(strip(1), ones_where(jnp.where(v == 0, 63 - y, -1) == pos)).astype(BF)
        sides[ry, 3] = mm(strip(3), ones_where(jnp.where(v == 31, y, -1) == pos)).astype(BF)
    lane_e = lane_row(512)
    inner = lane_e & 127
    at = ((inner & 31) << 1) + (lane_e >> 7)
    north = jnp.where(inner < 32, at - 1, -1)
    south = jnp.where(inner >= 96, 64 - at, -1)
    ends = mm(strip(0), ones_where(north == pos)) + mm(strip(2), ones_where(south == pos))
    gd = jnp.zeros((64, 256), F32)
    gb = jnp.zeros((256, 1), F32)
    for t in range(2):
        end = ends[t * 64 : t * 64 + 64, :]
        for spot, k in ((0, 0), (96, 1), (384 + 31, 3), (384 + 127, 2)):
            end = jnp.where(lane_e == spot, pixels[:, t * 4 + k : t * 4 + k + 1], end)
        for ry in range(4):
            for cx in range(4):
                row = (ry * 4 + cx) * 64
                w = base_ref[t, row : row + 64, :]
                if (ry, cx) in sides:
                    w = w + sides[ry, cx][t * 64 : t * 64 + 64, :]
                win_ref[t, row : row + 64, :] = w
                edge = end[:, cx * 128 : cx * 128 + 128]
                if ry == 0:
                    fix = jnp.where(lane_row(128) < 64, edge, 0.0).astype(BF)
                    win_ref[t, row : row + 64, 0:128] = w[:, 0:128] + fix
                if ry == 3:
                    fix = jnp.where(lane_row(128) >= 64, edge, 0.0).astype(BF)
                    win_ref[t, row : row + 64, 896:1024] = w[:, 896:1024] + fix
    for t in range(2):
        pre = mm(w_ref[...], win_ref[t]) + bias_ref[:, 0:1]
        sig = 1.0 / (1.0 + jnp.exp(-pre))
        hidden = (pre * sig).astype(BF)
        quarter = mm(down_ref[...], hidden).astype(BF)
        for c in range(4):
            sum_ref[c, t * 16 : t * 16 + 16, :] = quarter[c * 16 : c * 16 + 16, :]
        back = jnp.concatenate(
            [
                jnp.concatenate(
                    [msg_ref[c, t * 64 + g * 16 : t * 64 + g * 16 + 16, 0:256] for c in range(4)], axis=0
                )
                for g in range(4)
            ],
            axis=1,
        )
        grad_hidden = mm(down_t_ref[...], back)
        grad_pre = (grad_hidden * (sig * (1.0 + pre * (1.0 - sig)))).astype(BF)
        gb = gb + jnp.sum(grad_pre.astype(F32), axis=1, keepdims=True)
        gd = gd + mm_nt(back, hidden)
        part = mm_nt(win_ref[t], grad_pre)
        gc_ref[...] = part if t == 0 else gc_ref[...] + part
    rows = []
    for dy in range(3):
        for cx in range(4):
            r0, r1 = (dy * 4 + cx) * 64, ((dy + 1) * 4 + cx) * 64
            rows.append(gc_ref[r0 : r0 + 64, 0:128] + gc_ref[r1 : r1 + 64, 128:256])
    taps = []
    for dy in range(3):
        for dx in range(3):
            taps.append(rows[dy * 4 + dx] + pltpu.roll(rows[dy * 4 + dx + 1], 64, axis=1))
    taps.append(jnp.zeros((64, 128), F32))
    conv = jnp.concatenate(taps, axis=0)
    conv = jnp.concatenate([conv[q * 128 : q * 128 + 128, :].T for q in range(5)], axis=1)[0:64, :]
    kk = down_col(640)
    cc = lane_row(1024)
    i, tap = kk & 63, kk >> 6
    place = ones_where(cc == jnp.where(tap < 9, ((i >> 4) << 8) + (i & 15) * 9 + tap, -1))
    conv = [mm(h, place) for h in halves(conv)]
    kk = down_col(256)
    i, ab = kk & 63, kk >> 6
    place = ones_where(cc == ((i >> 4) << 8) + 144 + (i & 15) * 4 + ab)
    down = [mm(h, place) for h in halves(gd)]
    gb = gb[0:64, :] + gb[64:128, :] + gb[128:192, :] + gb[192:256, :]
    bias = [h.astype(F32) for h in halves(gb)]
    lane16 = lane_row(1024)
    for part in range(2):
        for c in range(4):
            d = jnp.concatenate(
                [down[part][s * 16 : s * 16 + 16, c * 256 : c * 256 + 256] for s in range(4)], axis=1
            )
            both = conv[part][c * 16 : c * 16 + 16, :] + d
            both = jnp.where(lane16 == 208, bias[part][c * 16 : c * 16 + 16, :], both)
            sum_ref[c, 32 + part * 16 : 48 + part * 16, :] = both.astype(BF)
    for d in range(4):
        out_refs[d][...] = sum_ref[me ^ d]


def spread_body(me_ref, *refs):
    in_refs, out_ref, msg_ref = refs[0:4], refs[4], refs[5]
    for d in range(4):
        msg_ref[me_ref[0] ^ d] = in_refs[d][...]
    stack = jnp.concatenate(
        [msg_ref[c, 0:32, g * 256 : g * 256 + 256] for g in range(4) for c in range(4)], axis=0
    )
    row = down_col(512)
    source = (((row >> 3) & 3) << 7) | (((row >> 1) & 3) << 5) | ((row & 1) << 4) | (row >> 5)
    out_ref[:, 0:256] = mm(ones_where(lane_row(512) == source), stack).astype(BF)
    total = jnp.zeros((16, 1024), F32)
    for c in range(4):
        total = total + (msg_ref[c, 32:48, :].astype(F32) + msg_ref[c, 48:64, :].astype(F32))
    parts = [
        h[:, s * 256 + o : s * 256 + o + 128] for h in halves(total) for o in (0, 128) for s in range(4)
    ]
    stack = jnp.concatenate(parts, axis=0)
    r, p = row & 7, row >> 3
    source = jnp.where(r < 4, (r << 6) + p, -1)
    out_ref[:, 256:384] = mm(ones_where(lane_row(256) == source), stack).astype(BF)


def place_body(msg_ref, slot_ref, out_ref):
    quarter = msg_ref[:, 0:256]
    slot = slot_ref[0:1, :].astype(jnp.int32)
    row = down_col(512)
    lane = lane_row(256)
    half = row & 1
    li = down_col(256)
    to = (((li >> 5) & 3) << 6) | (li & 31)
    total = jnp.zeros((512, 256), F32)
    for qc in range(2):
        got = mm(ones_where(slot == ((row >> 1) << 1) + qc), quarter)
        total = total + mm(keep((lane >> 7) == half, got), ones_where(lane == to + qc * 32))
    out_ref[:, 0:256] = total.astype(BF)
    r = down_col(16)
    src = lane_row(512) & 7
    src = jnp.where(src < 4, src & 1, -1)
    summed = mm(ones_where(src == jnp.where(r < 4, r & 1, -2)), msg_ref[:, 256:384])
    high, low = halves(summed)
    both = jnp.where(iota((16, 128), 0) < 2, high.astype(F32), low.astype(F32)).astype(BF)
    r = row & 7
    out_ref[:, 256:384] = mm(ones_where(lane_row(16) == jnp.where(r < 4, r, -1)), both).astype(BF)


def finish_body(msg_ref, coarse_ref, conv_ref, down_ref, bias_ref):
    row = down_col(512)
    col = lane_row(512)
    qr, g, hf, a, k = row >> 8, (row >> 6) & 3, (row >> 5) & 1, (row >> 4) & 1, row & 15
    source = (k << 5) | (g << 3) | (a << 2) | (qr << 1) | hf
    got = mm(ones_where(col == source), msg_ref[:, 0:256]).astype(BF)
    for q in range(16):
        coarse_ref[:, q * 256 : q * 256 + 256] = got[q * 32 : q * 32 + 32, :]

    row = down_col(256)
    got = mm(ones_where(col == ((row & 63) << 3) + (row >> 6)), msg_ref[:, 256:384])
    near = down_col(1024)
    to = jnp.where((near & 255) < 144, (near >> 8) * 144 + (near & 255), -1)
    place = ones_where(lane_row(576) == to)
    lane = lane_row(128)
    shift = ones_where(down_col(128) == jnp.where(lane < 64, lane + 16, -1))
    conv = jnp.zeros((16, 576), F32)
    down = jnp.zeros((64, 128), F32)
    for h in range(2):
        low, high = got[h * 128 : h * 128 + 64, :], got[h * 128 + 64 : h * 128 + 128, :]
        wide = jnp.concatenate(
            [x[s * 16 : s * 16 + 16, :] for s in range(4) for x in (low, high)], axis=1
        )
        conv = conv + mm(wide.astype(BF), place)
        down = down + mm(high.astype(BF), shift)
    conv_ref[...] = conv
    down_ref[...] = down[:, 0:64]
    bias = got[64:80, 80:81] + got[192:208, 80:81]
    bias_ref[...] = jnp.sum(jnp.where(lane_row(16) == down_col(16), bias, 0.0), axis=0, keepdims=True)


def to_peers(parts):
    return [parts[0]] + [
        lax.ppermute(parts[d], "chan", [(i, i ^ d) for i in range(4)]) for d in range(1, 4)
    ]


def on_device(
    features,
    conv_weight,
    conv_bias,
    down_weight,
    cotangent,
    edge_links,
    edge_turns,
    corner_links,
    corner_turns,
    child_slot,
):
    msg_spec = whole(MSG)
    msg = jax.ShapeDtypeStruct(MSG, BF)

    def to_nodes(x):
        return lax.all_to_all(x.reshape(64, 8, 384), "tile", 0, 0, tiled=True).reshape(MSG)

    me = lax.axis_index("chan").astype(jnp.int32).reshape(1)
    scalar = pl.BlockSpec(memory_space=pltpu.SMEM)
    first = jax.ShapeDtypeStruct((16, 5632), BF)
    second = jax.ShapeDtypeStruct((16, 4096), BF)
    pieces, raw, *peers = call(
        send_body,
        (msg, jax.ShapeDtypeStruct((64, 384), BF)) + (first,) * 3 + (second,) * 3,
        (1,),
        [scalar, whole((128, 4096)), whole((32, 4096))]
        + [whole((4, 8))] * 4
        + [whole((1, 8)), whole((16, 576)), whole((1, 16)), whole((64, 64))],
        (msg_spec, whole((64, 384))) + (whole((16, 5632)),) * 3 + (whole((16, 4096)),) * 3,
        flops=10**9,
        moved=2 * 10**6,
    )(
        me,
        *[
            pltpu.with_memory_space_constraint(x, pltpu.HBM)
            for x in (
                features.reshape(128, 4096),
                cotangent.reshape(32, 4096),
                edge_links.T,
                edge_turns.T,
                corner_links.T,
                corner_turns.T,
                child_slot.reshape(1, 8),
                conv_weight,
                conv_bias.reshape(1, 16),
                down_weight,
            )
        ],
    )
    first = to_peers([None] + peers[0:3])[1:]
    second = to_peers([None] + peers[3:6])[1:]
    pieces, first = lax.optimization_barrier((to_nodes(pieces), first))
    picked, slots = call(
        pick_body,
        (msg, jax.ShapeDtypeStruct((8, 512), F32)),
        (1,),
        [msg_spec],
        (msg_spec, whole((8, 512))),
        flops=10**9,
        moved=10**6,
    )(pieces)
    picked = to_nodes(picked)
    own = pl.BlockSpec((32, 4096), lambda i, m: (m[0], 0))
    vmem = pl.BlockSpec(memory_space=pltpu.VMEM)
    ready = pl.pallas_call(
        ready_body,
        out_shape=(
            jax.ShapeDtypeStruct((2, 1024, 1024), BF),
            jax.ShapeDtypeStruct((256, 1024), BF),
            jax.ShapeDtypeStruct((64, 256), BF),
            jax.ShapeDtypeStruct((256, 64), BF),
            jax.ShapeDtypeStruct((256, 128), F32),
        ),
        grid_spec=pltpu.PrefetchScalarGridSpec(
            num_scalar_prefetch=1,
            grid=(1,),
            in_specs=[own, whole((64, 384))] + [whole((16, 5632))] * 3 + [whole((16, 4096))] * 3,
            out_specs=(vmem,) * 5,
            scratch_shapes=(pltpu.VMEM((4, 32, 4096), BF), pltpu.VMEM((4, 64, 384), BF)),
        ),
        compiler_params=pltpu.CompilerParams(vmem_limit_bytes=32 << 20),
        cost_estimate=pl.CostEstimate(flops=10**9, bytes_accessed=4 * 10**6, transcendentals=0),
    )(me, features.reshape(128, 4096), raw, *first, *second)
    group = jax.ShapeDtypeStruct((128, 384), BF)
    picked = call(
        regroup_body,
        (group,) * 4,
        (1,),
        [scalar, msg_spec],
        (whole((128, 384)),) * 4,
        flops=4 * 10**8,
        moved=10**6,
    )(me, picked)
    picked = to_peers(picked)
    local = pl.pallas_call(
        level_body,
        out_shape=(jax.ShapeDtypeStruct((64, 1024), BF),) * 4,
        in_specs=[scalar] + [vmem] * 9,
        out_specs=(vmem,) * 4,
        scratch_shapes=(
            pltpu.VMEM((4, 128, 384), BF),
            pltpu.VMEM((4, 64, 1024), BF),
            pltpu.VMEM((2, 1024, 1024), BF),
            pltpu.VMEM((1024, 256), F32),
        ),
        compiler_params=pltpu.CompilerParams(vmem_limit_bytes=32 << 20),
        cost_estimate=pl.CostEstimate(flops=4 * 10**9, bytes_accessed=4 * 10**6, transcendentals=0),
    )(me, *picked, *ready)
    local = to_peers(local)
    out = call(
        spread_body,
        msg,
        (1,),
        [scalar] + [whole((64, 1024))] * 4,
        msg_spec,
        (pltpu.VMEM((4, 64, 1024), BF),),
        flops=4 * 10**8,
        moved=10**6,
    )(me, *local)
    out = to_nodes(out)
    out = call(place_body, msg, (1,), [msg_spec, whole((8, 512))], msg_spec, flops=5 * 10**8, moved=10**6)(
        out, slots
    )
    out = to_nodes(out)
    coarse, grad_conv, grad_down, grad_bias = call(
        finish_body,
        (
            jax.ShapeDtypeStruct((32, 4096), BF),
            jax.ShapeDtypeStruct((16, 576), F32),
            jax.ShapeDtypeStruct((64, 64), F32),
            jax.ShapeDtypeStruct((1, 16), F32),
        ),
        (1,),
        [msg_spec],
        (
            whole((32, 4096)),
            whole((16, 576)),
            whole((64, 64)),
            whole((1, 16)),
        ),
        flops=4 * 10**8,
        moved=10**6,
    )(out)
    return (coarse.reshape(2, 16, 4096), grad_conv, grad_bias.reshape(16), grad_down)


def solution(mesh):
    in_specs = (
        P("tile", "chan", None),
        P("chan", None),
        P("chan"),
        P(None, "chan"),
        P("tile", "chan", None),
        P("tile", None),
        P("tile", None),
        P("tile", None),
        P("tile", None),
        P("tile"),
    )
    out_specs = (P("tile", "chan", None), P("chan", None), P("chan"), P(None, "chan"))
    return jax.shard_map(
        on_device, mesh=mesh, in_specs=in_specs, out_specs=out_specs, check_vma=False
    )
```

```python
import jax
import jax.numpy as jnp
from jax import lax
from jax.experimental import pallas as pl
from jax.experimental.pallas import tpu as pltpu
from jax.sharding import PartitionSpec as P

BF = jnp.bfloat16
F32 = jnp.float32
NODES = 64
MSG = (NODES * 8, 384)


def iota(shape, dim):
    return lax.broadcasted_iota(jnp.int32, shape, dim)


def down_col(n, start=0):
    return iota((n, 1), 0) + start


def lane_row(n):
    return iota((1, n), 1)


def ones_where(mask):
    return jnp.where(mask, 1.0, 0.0).astype(BF)


def keep(mask, x):
    return jnp.where(mask, x, 0.0).astype(BF)


def mm(a, b):
    return jnp.dot(a, b, preferred_element_type=F32)


def mm_nt(a, b):
    return lax.dot_general(a, b, (((1,), (1,)), ((), ())), preferred_element_type=F32)


def halves(x):
    high = x.astype(BF)
    return high, (x - high.astype(F32)).astype(BF)


def call(body, out_shape, grid, in_specs, out_specs, scratch=(), flops=0, moved=0):
    return pl.pallas_call(
        body,
        out_shape=out_shape,
        grid=grid,
        in_specs=in_specs,
        out_specs=out_specs,
        scratch_shapes=scratch,
        compiler_params=pltpu.CompilerParams(vmem_limit_bytes=48 << 20),
        cost_estimate=pl.CostEstimate(flops=flops, bytes_accessed=moved, transcendentals=0),
    )


def whole(shape):
    return pl.BlockSpec(shape, lambda *i: (0,) * len(shape))


def pack_weights(conv_ref, bias_ref, down_ref, raw_ref):
    zero = jnp.zeros((64, 64), BF)
    lane = lane_row(128)
    bias = jnp.where(lane_row(16) == down_col(16), bias_ref[...], 0.0)
    bias = jnp.sum(bias, axis=1, keepdims=True)
    b0 = bias.astype(BF).astype(F32)
    b1 = (bias - b0).astype(BF).astype(F32)
    b2 = (bias - b0) - b1
    bias = jnp.where(lane == 0, b0, jnp.where(lane == 1, b1, jnp.where(lane == 2, b2, 0.0))).astype(BF)
    raw_ref[:, 0:128] = jnp.concatenate([down_ref[...], zero], axis=1)
    raw_ref[0:16, 128:384] = conv_ref[:, 0:256]
    raw_ref[16:32, 128:384] = conv_ref[:, 256:512]
    raw_ref[32:48, 128:256] = jnp.concatenate([conv_ref[:, 512:576], zero[0:16]], axis=1)
    raw_ref[32:48, 256:384] = bias
    raw_ref[48:64, 128:384] = jnp.zeros((16, 256), BF)


def send_body(
    me_ref,
    feat_ref,
    cot_ref,
    el_ref,
    et_ref,
    cl_ref,
    ct_ref,
    slot_ref,
    conv_ref,
    bias_ref,
    down_ref,
    out_ref,
    raw_ref,
    *peer_refs,
):
    pack_weights(conv_ref, bias_ref, down_ref, raw_ref)
    for d in range(1, 4):
        peer = me_ref[0] ^ d
        first_ref, second_ref = peer_refs[d - 1], peer_refs[d + 2]
        first_ref[:, 0:4096] = feat_ref[pl.ds(pl.multiple_of(peer * 32, 16), 16), :]
        second_ref[...] = feat_ref[pl.ds(pl.multiple_of(peer * 32 + 16, 16), 16), :]
        for q in range(4):
            first_ref[:, 4096 + q * 384 : 4480 + q * 384] = raw_ref[q * 16 : q * 16 + 16, :]

    cot = cot_ref[...]
    stack = jnp.concatenate([cot[:, q * 256 : q * 256 + 256] for q in range(16)], axis=0)
    row = down_col(512)
    k, g, a, qr, hf = row >> 5, (row >> 3) & 3, (row >> 2) & 1, (row >> 1) & 1, row & 1
    source = (qr << 8) | (g << 6) | (hf << 5) | (a << 4) | k
    out_ref[:, 0:256] = mm(ones_where(lane_row(512) == source), stack).astype(BF)

    first = feat_ref[:, 0:128]
    last = feat_ref[:, 3968:4096]
    p = down_col(64)
    lane = lane_row(128)
    rim_n = mm_nt(ones_where(lane == 63 - p), first)
    rim_s = mm_nt(ones_where(lane == 64 + p), last)
    pc = down_col(128)
    pos = pc & 63
    want = jnp.where(pc < 64, pos * 64, (63 - pos) * 64 + 63)
    rim_we = mm_nt(ones_where(lane_row(4096) == want), feat_ref[...])
    cr = down_col(16)
    at_first = jnp.where(cr == 0, 0, jnp.where(cr == 3, 63, -1))
    at_last = jnp.where(cr == 1, 64, jnp.where(cr == 2, 127, -1))
    corners = mm_nt(ones_where(lane == at_first), first) + mm_nt(ones_where(lane == at_last), last)
    tc = down_col(128)
    by_chan = jnp.zeros((16, 128), F32)
    for c in range(4):
        spread = jnp.broadcast_to(corners[c : c + 1, :], (16, 128))
        by_chan = by_chan + mm(keep((lane & 15) == cr, spread), ones_where(lane == (tc >> 4) * 4 + c))

    def over_lanes(x):
        rows = jnp.zeros((x.shape[0], 128), jnp.int32)
        for t in range(8):
            rows = jnp.where((lane & 7) == t, x[:, t : t + 1], rows)
        return rows

    def in_row(x, first_field):
        rows = over_lanes(x)
        side = iota(rows.shape, 0)
        mine = (iota(rows.shape, 1) >> 3) == side + first_field
        return jnp.sum(jnp.where(mine, rows, 0).astype(F32), axis=0, keepdims=True)

    side = iota((4, 8), 0)
    el, cl, slot = el_ref[...], cl_ref[...], slot_ref[...]
    edge = in_row(el >> 3, 0) + in_row((side + 2 + et_ref[...]) & 3, 4) + in_row(el & 7, 8)
    edge = edge + in_row(slot >> 3, 12) + in_row(slot & 7, 13)
    node = over_lanes(jnp.where(cl < 0, 127, cl >> 3)).astype(F32)
    pixel = over_lanes((cl & 7) * 4 + ((side + 2 + ct_ref[...]) & 3)).astype(F32)
    field = lane >> 3
    sub = down_col(16)
    small = jnp.where(sub == 0, edge, 0.0)
    for part in range(4):
        line = jnp.where(field == 14, node[part : part + 1, :], 0.0)
        line = jnp.where(field == 15, pixel[part : part + 1, :], line)
        small = small + jnp.where(sub == part + 1, line, 0.0)
    parts = [rim_n, rim_we[0:64], rim_s, rim_we[64:128], by_chan, small, jnp.zeros((96, 128), F32)]
    stack = jnp.concatenate([x.astype(BF) for x in parts], axis=0)
    r, node = row & 7, row >> 3
    source = jnp.where(r == 4, 256 + (node & 15), jnp.where(r == 5, 272, jnp.where(r == 6, 273 + (node >> 4), -1)))
    source = jnp.where(r < 4, r * 64 + node, source)
    out_ref[:, 256:384] = mm(ones_where(lane_row(384) == source), stack).astype(BF)


def pick_body(msg_ref, out_ref, slot_ref):
    cot = msg_ref[:, 0:256]
    misc = msg_ref[:, 256:384]
    col = lane_row(512)
    lane = lane_row(128)
    sub = down_col(512)
    near = down_col(128)
    base = (sub >> 3) << 3
    both = mm(ones_where((col == base + 5) | (col == base + 6)), misc)
    fields = mm(keep((lane & 7) == (sub & 7), both), ones_where((near >> 3) == lane))
    flip = fields.T
    slot_ref[...] = jnp.broadcast_to(flip[12:13, :] * 8.0 + flip[13:14, :], (8, 512))
    num = fields.astype(jnp.int32)

    def field(f):
        return num[:, f : f + 1]

    slot_row = field(12) * 8 + ((field(13) >> 1) << 1)
    lane2 = lane_row(256)
    fold_r = down_col(256)
    fold = ones_where(lane == (((fold_r >> 6) << 5) | (fold_r & 31)))
    mine = ((lane2 >> 5) & 1) == (field(13) & 1)
    for hf in range(2):
        got = mm(ones_where(col == slot_row + hf), cot)
        out_ref[:, hf * 128 : hf * 128 + 128] = mm(keep(mine, got), fold).astype(BF)
    total = jnp.zeros((512, 128), F32)
    for k in range(4):
        got = mm(ones_where(col == field(k) * 8 + field(4 + k)), misc)
        place = ones_where(lane == k * 16 + (near & 15))
        total = total + mm(keep((lane >> 4) == field(8 + k), got), place)
    got = mm(ones_where(col == field(14) * 8 + 4), misc)
    total = total + mm(keep(lane == field(15), got), ones_where(jnp.broadcast_to(lane == 64, (128, 128))))
    out_ref[:, 256:384] = total.astype(BF)


def regroup_body(me_ref, msg_ref, *out_refs):
    row = down_col(128)
    col = lane_row(512)
    lane = lane_row(128)
    pair, g, k, p = row >> 6, (row >> 4) & 3, row & 15, row & 63
    for d in range(4):
        out_ref = out_refs[d]
        tile = ((me_ref[0] ^ d) << 1) | pair
        out_ref[:, 0:256] = mm(ones_where(col == ((k << 5) | (g << 3) | tile)), msg_ref[:, 0:256]).astype(BF)
        got = mm(ones_where(col == ((p << 3) | tile)), msg_ref[:, 256:384])
        rims = jnp.where(lane < 64, got[0:64], pltpu.roll(got[64:128], 64, axis=1))
        pixels = jnp.zeros((16, 128), F32)
        for q in range(8):
            pixels = jnp.where(lane == q, got[q * 16 : q * 16 + 16, 64:65], pixels)
        rest = jnp.zeros((48, 128), F32)
        out_ref[:, 256:384] = jnp.concatenate([rims, pixels, rest], axis=0).astype(BF)


def lay_weights(raw_ref, w_ref, down_ref, down_t_ref, bias_ref):
    raw = jnp.concatenate(
        [
            jnp.concatenate([raw_ref[c, q * 16 : q * 16 + 16, 128 : 128 + n] for c in range(4)], axis=0)
            for q, n in ((0, 256), (1, 256), (2, 128))
        ],
        axis=1,
    )
    e = iota((640, 1), 0)
    i = (e * 7282) >> 16
    tap = e - i * 9
    dy = (tap * 86) >> 8
    to = jnp.where(e < 576, dy * 256 + (tap - dy * 3) * 64 + i, -9999)
    col = lane_row(1536)
    shifted = mm(raw, ones_where(jnp.where(col < 768, col, col - 832) == to)).astype(BF)
    zero = jnp.zeros((64, 256), BF)
    for a in range(2):
        for b in range(2):
            part = shifted[:, b * 768 : b * 768 + 768]
            row = (a * 2 + b) * 64
            w_ref[row : row + 64, :] = jnp.concatenate([zero, part] if a else [part, zero], axis=1)
    down = jnp.zeros((64, 256), F32)
    down_t = jnp.zeros((256, 64), F32)
    for c in range(4):
        mine = raw_ref[c, 0:64, 0:128]
        l = down_col(128)
        to = jnp.where(l < 64, (l & 3) * 64 + c * 16 + (l >> 2), -1)
        down = down + mm(mine, ones_where(lane_row(256) == to))
        l = lane_row(128)
        to = jnp.where(l < 64, (l & 3) * 64 + c * 16 + (l >> 2), -1)
        down_t = down_t + mm_nt(ones_where(down_col(256) == to), mine)
    down_ref[...] = down.astype(BF)
    down_t_ref[...] = down_t.astype(BF)
    bias = jnp.concatenate([raw_ref[c, 32:48, 256:259].astype(F32) for c in range(4)], axis=0)
    bias = (bias[:, 0:1] + bias[:, 1:2]) + bias[:, 2:3]
    bias_ref[...] = jnp.broadcast_to(jnp.concatenate([bias] * 4, axis=0), (256, 128))


def lay_places(side_ref, end_ref, place_ref):
    lane = lane_row(1024)
    v = lane & 31
    pos = down_col(64)
    for ry in range(4):
        y = ((lane >> 5) << 1) + (ry - 1)
        side_ref[ry] = ones_where(jnp.where(v == 0, 63 - y, -1) == pos)
        side_ref[4 + ry] = ones_where(jnp.where(v == 31, y, -1) == pos)
    lane_e = lane_row(512)
    inner = lane_e & 127
    at = ((inner & 31) << 1) + (lane_e >> 7)
    end_ref[0] = ones_where(jnp.where(inner < 32, at - 1, -1) == pos)
    end_ref[1] = ones_where(jnp.where(inner >= 96, 64 - at, -1) == pos)
    kk = down_col(640)
    i, tap = kk & 63, kk >> 6
    to = jnp.where(tap < 9, ((i >> 4) << 8) + (i & 15) * 9 + tap, -1)
    place_ref[0:640, :] = ones_where(lane == to)
    kk = down_col(256)
    i, ab = kk & 63, kk >> 6
    place_ref[640:896, :] = ones_where(lane == ((i >> 4) << 8) + 144 + (i & 15) * 4 + ab)


def ready_body(me_ref, *refs):
    own_ref, own_raw_ref, first_refs, second_refs = refs[0], refs[1], refs[2:5], refs[5:8]
    win_ref, w_ref, down_ref, down_t_ref, bias_ref = refs[8:13]
    side_ref, end_ref, place_ref, x_ref, raw_ref = refs[13:]
    me = me_ref[0]
    lay_places(side_ref, end_ref, place_ref)
    raw_ref[me] = own_raw_ref[...]
    x_ref[me] = own_ref[...]
    for d in range(1, 4):
        first_ref = first_refs[d - 1]
        x_ref[me ^ d, 0:16, :] = first_ref[:, 0:4096]
        x_ref[me ^ d, 16:32, :] = second_refs[d - 1][...]
        for q in range(4):
            raw_ref[me ^ d, q * 16 : q * 16 + 16, :] = first_ref[:, 4096 + q * 384 : 4480 + q * 384]
    lay_weights(raw_ref, w_ref, down_ref, down_t_ref, bias_ref)
    l_in = down_col(512)
    to = (((l_in >> 6) & 1) << 8) | ((l_in & 1) << 7) | ((l_in >> 7) << 5) | ((l_in >> 1) & 31)
    order = ones_where(lane_row(512) == to)
    lane = lane_row(1024)
    v = lane & 31
    for t in range(2):
        x = jnp.concatenate([x_ref[c, t * 16 : t * 16 + 16, :] for c in range(4)], axis=0)
        stack = jnp.concatenate([x[:, q * 512 : q * 512 + 512] for q in range(8)], axis=0)
        split = mm(stack, order)
        cols = []
        for a in range(2):
            even, odd = [
                jnp.concatenate(
                    [split[q * 64 : q * 64 + 64, (a * 2 + b) * 128 : (a * 2 + b) * 128 + 128] for q in range(8)],
                    axis=1,
                )
                for b in range(2)
            ]
            cols.append(
                [
                    jnp.where(v == 0, 0.0, pltpu.roll(odd, 1, axis=1)),
                    even,
                    odd,
                    jnp.where(v == 31, 0.0, pltpu.roll(even, 1023, axis=1)),
                ]
            )
        for cx in range(4):
            top = jnp.where(lane < 32, 0.0, pltpu.roll(cols[1][cx], 32, axis=1))
            low = jnp.where(lane >= 992, 0.0, pltpu.roll(cols[0][cx], 992, axis=1))
            for ry, w in enumerate((top, cols[0][cx], cols[1][cx], low)):
                row = (ry * 4 + cx) * 64
                win_ref[t, row : row + 64, :] = w.astype(BF)


def level_body(me_ref, *refs):
    in_refs, (base_ref, w_ref, down_ref, down_t_ref, bias_ref, side_ref, end_ref, place_ref) = refs[0:4], refs[4:12]
    out_refs, (msg_ref, sum_ref, win_ref, gc_ref) = refs[12:16], refs[16:]
    me = me_ref[0]
    for d in range(4):
        msg_ref[me ^ d] = in_refs[d][...]
    flip = [msg_ref[c, 0:64, 256:384].astype(F32).T.astype(BF) for c in range(4)]

    def strip(k):
        return jnp.concatenate(
            [f[t * 64 + k * 16 : t * 64 + k * 16 + 16, :] for t in range(2) for f in flip], axis=0
        )

    pixels = jnp.concatenate([msg_ref[c, 64:80, 256:384] for c in range(4)], axis=0).astype(F32)
    sides = {}
    for ry in range(4):
        sides[ry, 0] = mm(strip(1), side_ref[ry]).astype(BF)
        sides[ry, 3] = mm(strip(3), side_ref[4 + ry]).astype(BF)
    lane_e = lane_row(512)
    ends = mm(strip(0), end_ref[0]) + mm(strip(2), end_ref[1])
    gd = jnp.zeros((64, 256), F32)
    gb = jnp.zeros((256, 1), F32)
    for t in range(2):
        end = ends[t * 64 : t * 64 + 64, :]
        for spot, k in ((0, 0), (96, 1), (384 + 31, 3), (384 + 127, 2)):
            end = jnp.where(lane_e == spot, pixels[:, t * 4 + k : t * 4 + k + 1], end)
        for ry in range(4):
            for cx in range(4):
                row = (ry * 4 + cx) * 64
                w = base_ref[t, row : row + 64, :]
                if (ry, cx) in sides:
                    w = w + sides[ry, cx][t * 64 : t * 64 + 64, :]
                win_ref[t, row : row + 64, :] = w
                edge = end[:, cx * 128 : cx * 128 + 128]
                if ry == 0:
                    fix = jnp.where(lane_row(128) < 64, edge, 0.0).astype(BF)
                    win_ref[t, row : row + 64, 0:128] = w[:, 0:128] + fix
                if ry == 3:
                    fix = jnp.where(lane_row(128) >= 64, edge, 0.0).astype(BF)
                    win_ref[t, row : row + 64, 896:1024] = w[:, 896:1024] + fix
    for t in range(2):
        pre = mm(w_ref[...], win_ref[t]) + bias_ref[:, 0:1]
        sig = 1.0 / (1.0 + jnp.exp(-pre))
        hidden = (pre * sig).astype(BF)
        quarter = mm(down_ref[...], hidden).astype(BF)
        for c in range(4):
            sum_ref[c, t * 16 : t * 16 + 16, :] = quarter[c * 16 : c * 16 + 16, :]
        back = jnp.concatenate(
            [
                jnp.concatenate(
                    [msg_ref[c, t * 64 + g * 16 : t * 64 + g * 16 + 16, 0:256] for c in range(4)], axis=0
                )
                for g in range(4)
            ],
            axis=1,
        )
        grad_hidden = mm(down_t_ref[...], back)
        grad_pre = (grad_hidden * (sig * (1.0 + pre * (1.0 - sig)))).astype(BF)
        gb = gb + jnp.sum(grad_pre.astype(F32), axis=1, keepdims=True)
        gd = gd + mm_nt(back, hidden)
        part = mm_nt(win_ref[t], grad_pre)
        gc_ref[...] = part if t == 0 else gc_ref[...] + part
    rows = []
    for dy in range(3):
        for cx in range(4):
            r0, r1 = (dy * 4 + cx) * 64, ((dy + 1) * 4 + cx) * 64
            rows.append(gc_ref[r0 : r0 + 64, 0:128] + gc_ref[r1 : r1 + 64, 128:256])
    taps = []
    for dy in range(3):
        for dx in range(3):
            taps.append(rows[dy * 4 + dx] + pltpu.roll(rows[dy * 4 + dx + 1], 64, axis=1))
    taps.append(jnp.zeros((64, 128), F32))
    conv = jnp.concatenate(taps, axis=0)
    conv = jnp.concatenate([conv[q * 128 : q * 128 + 128, :].T for q in range(5)], axis=1)[0:64, :]
    place = place_ref[0:640, :]
    conv = [mm(h, place) for h in halves(conv)]
    place = place_ref[640:896, :]
    down = [mm(h, place) for h in halves(gd)]
    gb = gb[0:64, :] + gb[64:128, :] + gb[128:192, :] + gb[192:256, :]
    bias = [h.astype(F32) for h in halves(gb)]
    lane16 = lane_row(1024)
    for part in range(2):
        for c in range(4):
            d = jnp.concatenate(
                [down[part][s * 16 : s * 16 + 16, c * 256 : c * 256 + 256] for s in range(4)], axis=1
            )
            both = conv[part][c * 16 : c * 16 + 16, :] + d
            both = jnp.where(lane16 == 208, bias[part][c * 16 : c * 16 + 16, :], both)
            sum_ref[c, 32 + part * 16 : 48 + part * 16, :] = both.astype(BF)
    for d in range(4):
        out_refs[d][...] = sum_ref[me ^ d]


def spread_body(me_ref, *refs):
    in_refs, out_ref, msg_ref = refs[0:4], refs[4], refs[5]
    for d in range(4):
        msg_ref[me_ref[0] ^ d] = in_refs[d][...]
    stack = jnp.concatenate(
        [msg_ref[c, 0:32, g * 256 : g * 256 + 256] for g in range(4) for c in range(4)], axis=0
    )
    row = down_col(512)
    source = (((row >> 3) & 3) << 7) | (((row >> 1) & 3) << 5) | ((row & 1) << 4) | (row >> 5)
    out_ref[:, 0:256] = mm(ones_where(lane_row(512) == source), stack).astype(BF)
    total = jnp.zeros((16, 1024), F32)
    for c in range(4):
        total = total + (msg_ref[c, 32:48, :].astype(F32) + msg_ref[c, 48:64, :].astype(F32))
    parts = [
        h[:, s * 256 + o : s * 256 + o + 128] for h in halves(total) for o in (0, 128) for s in range(4)
    ]
    stack = jnp.concatenate(parts, axis=0)
    r, p = row & 7, row >> 3
    source = jnp.where(r < 4, (r << 6) + p, -1)
    out_ref[:, 256:384] = mm(ones_where(lane_row(256) == source), stack).astype(BF)


def place_body(msg_ref, slot_ref, out_ref):
    quarter = msg_ref[:, 0:256]
    slot = slot_ref[0:1, :].astype(jnp.int32)
    row = down_col(512)
    lane = lane_row(256)
    half = row & 1
    li = down_col(256)
    to = (((li >> 5) & 3) << 6) | (li & 31)
    total = jnp.zeros((512, 256), F32)
    for qc in range(2):
        got = mm(ones_where(slot == ((row >> 1) << 1) + qc), quarter)
        total = total + mm(keep((lane >> 7) == half, got), ones_where(lane == to + qc * 32))
    out_ref[:, 0:256] = total.astype(BF)
    r = down_col(16)
    src = lane_row(512) & 7
    src = jnp.where(src < 4, src & 1, -1)
    summed = mm(ones_where(src == jnp.where(r < 4, r & 1, -2)), msg_ref[:, 256:384])
    high, low = halves(summed)
    both = jnp.where(iota((16, 128), 0) < 2, high.astype(F32), low.astype(F32)).astype(BF)
    r = row & 7
    out_ref[:, 256:384] = mm(ones_where(lane_row(16) == jnp.where(r < 4, r, -1)), both).astype(BF)


def finish_body(msg_ref, coarse_ref, conv_ref, down_ref, bias_ref):
    row = down_col(512)
    col = lane_row(512)
    qr, g, hf, a, k = row >> 8, (row >> 6) & 3, (row >> 5) & 1, (row >> 4) & 1, row & 15
    source = (k << 5) | (g << 3) | (a << 2) | (qr << 1) | hf
    got = mm(ones_where(col == source), msg_ref[:, 0:256]).astype(BF)
    for q in range(16):
        coarse_ref[:, q * 256 : q * 256 + 256] = got[q * 32 : q * 32 + 32, :]

    row = down_col(256)
    got = mm(ones_where(col == ((row & 63) << 3) + (row >> 6)), msg_ref[:, 256:384])
    near = down_col(1024)
    to = jnp.where((near & 255) < 144, (near >> 8) * 144 + (near & 255), -1)
    place = ones_where(lane_row(576) == to)
    lane = lane_row(128)
    shift = ones_where(down_col(128) == jnp.where(lane < 64, lane + 16, -1))
    conv = jnp.zeros((16, 576), F32)
    down = jnp.zeros((64, 128), F32)
    for h in range(2):
        low, high = got[h * 128 : h * 128 + 64, :], got[h * 128 + 64 : h * 128 + 128, :]
        wide = jnp.concatenate(
            [x[s * 16 : s * 16 + 16, :] for s in range(4) for x in (low, high)], axis=1
        )
        conv = conv + mm(wide.astype(BF), place)
        down = down + mm(high.astype(BF), shift)
    conv_ref[...] = conv
    down_ref[...] = down[:, 0:64]
    bias = got[64:80, 80:81] + got[192:208, 80:81]
    bias_ref[...] = jnp.sum(jnp.where(lane_row(16) == down_col(16), bias, 0.0), axis=0, keepdims=True)


def to_peers(parts):
    return [parts[0]] + [
        lax.ppermute(parts[d], "chan", [(i, i ^ d) for i in range(4)]) for d in range(1, 4)
    ]


def on_device(
    features,
    conv_weight,
    conv_bias,
    down_weight,
    cotangent,
    edge_links,
    edge_turns,
    corner_links,
    corner_turns,
    child_slot,
):
    vmem = pl.BlockSpec(memory_space=pltpu.VMEM)
    msg = jax.ShapeDtypeStruct(MSG, BF)

    def to_nodes(x):
        return lax.all_to_all(x.reshape(64, 8, 384), "tile", 0, 0, tiled=True).reshape(MSG)

    me = lax.axis_index("chan").astype(jnp.int32).reshape(1)
    scalar = pl.BlockSpec(memory_space=pltpu.SMEM)
    first = jax.ShapeDtypeStruct((16, 5632), BF)
    second = jax.ShapeDtypeStruct((16, 4096), BF)
    pieces, raw, *peers = call(
        send_body,
        (msg, jax.ShapeDtypeStruct((64, 384), BF)) + (first,) * 3 + (second,) * 3,
        (1,),
        [scalar, whole((128, 4096)), whole((32, 4096))]
        + [whole((4, 8))] * 4
        + [whole((1, 8)), whole((16, 576)), whole((1, 16)), whole((64, 64))],
        (vmem,) * 8,
        flops=10**9,
        moved=2 * 10**6,
    )(
        me,
        *[
            pltpu.with_memory_space_constraint(x, pltpu.HBM)
            for x in (
                features.reshape(128, 4096),
                cotangent.reshape(32, 4096),
                edge_links.T,
                edge_turns.T,
                corner_links.T,
                corner_turns.T,
                child_slot.reshape(1, 8),
                conv_weight,
                conv_bias.reshape(1, 16),
                down_weight,
            )
        ],
    )
    first = to_peers([None] + peers[0:3])[1:]
    second = to_peers([None] + peers[3:6])[1:]
    pieces, first = lax.optimization_barrier((to_nodes(pieces), first))
    picked, slots = call(
        pick_body,
        (msg, jax.ShapeDtypeStruct((8, 512), F32)),
        (1,),
        [vmem],
        (vmem, vmem),
        flops=10**9,
        moved=10**6,
    )(pieces)
    picked = to_nodes(picked)
    own = pl.BlockSpec((32, 4096), lambda i, m: (m[0], 0))
    ready = pl.pallas_call(
        ready_body,
        out_shape=(
            jax.ShapeDtypeStruct((2, 1024, 1024), BF),
            jax.ShapeDtypeStruct((256, 1024), BF),
            jax.ShapeDtypeStruct((64, 256), BF),
            jax.ShapeDtypeStruct((256, 64), BF),
            jax.ShapeDtypeStruct((256, 128), F32),
            jax.ShapeDtypeStruct((8, 64, 1024), BF),
            jax.ShapeDtypeStruct((2, 64, 512), BF),
            jax.ShapeDtypeStruct((896, 1024), BF),
        ),
        grid_spec=pltpu.PrefetchScalarGridSpec(
            num_scalar_prefetch=1,
            grid=(1,),
            in_specs=[own] + [vmem] * 7,
            out_specs=(vmem,) * 8,
            scratch_shapes=(pltpu.VMEM((4, 32, 4096), BF), pltpu.VMEM((4, 64, 384), BF)),
        ),
        compiler_params=pltpu.CompilerParams(vmem_limit_bytes=32 << 20),
        cost_estimate=pl.CostEstimate(flops=10**9, bytes_accessed=4 * 10**6, transcendentals=0),
    )(me, features.reshape(128, 4096), raw, *first, *second)
    group = jax.ShapeDtypeStruct((128, 384), BF)
    picked = call(
        regroup_body,
        (group,) * 4,
        (1,),
        [scalar, vmem],
        (vmem,) * 4,
        flops=4 * 10**8,
        moved=10**6,
    )(me, picked)
    picked = to_peers(picked)
    local = pl.pallas_call(
        level_body,
        out_shape=(jax.ShapeDtypeStruct((64, 1024), BF),) * 4,
        in_specs=[scalar] + [vmem] * 12,
        out_specs=(vmem,) * 4,
        scratch_shapes=(
            pltpu.VMEM((4, 128, 384), BF),
            pltpu.VMEM((4, 64, 1024), BF),
            pltpu.VMEM((2, 1024, 1024), BF),
            pltpu.VMEM((1024, 256), F32),
        ),
        compiler_params=pltpu.CompilerParams(vmem_limit_bytes=32 << 20),
        cost_estimate=pl.CostEstimate(flops=4 * 10**9, bytes_accessed=4 * 10**6, transcendentals=0),
    )(me, *picked, *ready)
    local = to_peers(local)
    out = call(
        spread_body,
        msg,
        (1,),
        [scalar] + [vmem] * 4,
        vmem,
        (pltpu.VMEM((4, 64, 1024), BF),),
        flops=4 * 10**8,
        moved=10**6,
    )(me, *local)
    out = to_nodes(out)
    out = call(place_body, msg, (1,), [vmem, vmem], vmem, flops=5 * 10**8, moved=10**6)(
        out, slots
    )
    out = to_nodes(out)
    coarse, grad_conv, grad_down, grad_bias = call(
        finish_body,
        (
            jax.ShapeDtypeStruct((32, 4096), BF),
            jax.ShapeDtypeStruct((16, 576), F32),
            jax.ShapeDtypeStruct((64, 64), F32),
            jax.ShapeDtypeStruct((1, 16), F32),
        ),
        (1,),
        [vmem],
        (
            whole((32, 4096)),
            whole((16, 576)),
            whole((64, 64)),
            whole((1, 16)),
        ),
        flops=4 * 10**8,
        moved=10**6,
    )(out)
    return (coarse.reshape(2, 16, 4096), grad_conv, grad_bias.reshape(16), grad_down)


def solution(mesh):
    in_specs = (
        P("tile", "chan", None),
        P("chan", None),
        P("chan"),
        P(None, "chan"),
        P("tile", "chan", None),
        P("tile", None),
        P("tile", None),
        P("tile", None),
        P("tile", None),
        P("tile"),
    )
    out_specs = (P("tile", "chan", None), P("chan", None), P("chan"), P(None, "chan"))
    return jax.shard_map(
        on_device, mesh=mesh, in_specs=in_specs, out_specs=out_specs, check_vma=False
    )
```

```python
import jax
import jax.numpy as jnp
from jax import lax
from jax.experimental import pallas as pl
from jax.experimental.pallas import tpu as pltpu
from jax.sharding import PartitionSpec as P

BF = jnp.bfloat16
F32 = jnp.float32
NODES = 64
MSG = (NODES * 8, 384)


def iota(shape, dim):
    return lax.broadcasted_iota(jnp.int32, shape, dim)


def down_col(n, start=0):
    return iota((n, 1), 0) + start


def lane_row(n):
    return iota((1, n), 1)


def ones_where(mask):
    return jnp.where(mask, 1.0, 0.0).astype(BF)


def keep(mask, x):
    return jnp.where(mask, x, 0.0).astype(BF)


def mm(a, b):
    return jnp.dot(a, b, preferred_element_type=F32)


def mm_nt(a, b):
    return lax.dot_general(a, b, (((1,), (1,)), ((), ())), preferred_element_type=F32)


def halves(x):
    high = x.astype(BF)
    return high, (x - high.astype(F32)).astype(BF)


def call(body, out_shape, grid, in_specs, out_specs, scratch=(), flops=0, moved=0):
    return pl.pallas_call(
        body,
        out_shape=out_shape,
        grid=grid,
        in_specs=in_specs,
        out_specs=out_specs,
        scratch_shapes=scratch,
        compiler_params=pltpu.CompilerParams(vmem_limit_bytes=48 << 20),
        cost_estimate=pl.CostEstimate(flops=flops, bytes_accessed=moved, transcendentals=0),
    )


def whole(shape):
    return pl.BlockSpec(shape, lambda *i: (0,) * len(shape))


def pack_weights(conv_ref, bias_ref, down_ref, raw_ref):
    zero = jnp.zeros((64, 64), BF)
    lane = lane_row(128)
    bias = jnp.where(lane_row(16) == down_col(16), bias_ref[...], 0.0)
    bias = jnp.sum(bias, axis=1, keepdims=True)
    b0 = bias.astype(BF).astype(F32)
    b1 = (bias - b0).astype(BF).astype(F32)
    b2 = (bias - b0) - b1
    bias = jnp.where(lane == 0, b0, jnp.where(lane == 1, b1, jnp.where(lane == 2, b2, 0.0))).astype(BF)
    raw_ref[:, 0:128] = jnp.concatenate([down_ref[...], zero], axis=1)
    raw_ref[0:16, 128:384] = conv_ref[:, 0:256]
    raw_ref[16:32, 128:384] = conv_ref[:, 256:512]
    raw_ref[32:48, 128:256] = jnp.concatenate([conv_ref[:, 512:576], zero[0:16]], axis=1)
    raw_ref[32:48, 256:384] = bias
    raw_ref[48:64, 128:384] = jnp.zeros((16, 256), BF)


def send_body(
    me_ref,
    feat_ref,
    cot_ref,
    el_ref,
    et_ref,
    cl_ref,
    ct_ref,
    slot_ref,
    conv_ref,
    bias_ref,
    down_ref,
    out_ref,
    raw_ref,
    *peer_refs,
):
    pack_weights(conv_ref, bias_ref, down_ref, raw_ref)
    for d in range(1, 4):
        peer = me_ref[0] ^ d
        first_ref, second_ref = peer_refs[d - 1], peer_refs[d + 2]
        first_ref[...] = feat_ref[pl.ds(pl.multiple_of(peer * 32, 16), 16), :]
        second_ref[:, 0:4096] = feat_ref[pl.ds(pl.multiple_of(peer * 32 + 16, 16), 16), :]
        for q in range(4):
            second_ref[:, 4096 + q * 384 : 4480 + q * 384] = raw_ref[q * 16 : q * 16 + 16, :]

    cot = cot_ref[...]
    stack = jnp.concatenate([cot[:, q * 256 : q * 256 + 256] for q in range(16)], axis=0)
    row = down_col(512)
    k, g, a, qr, hf = row >> 5, (row >> 3) & 3, (row >> 2) & 1, (row >> 1) & 1, row & 1
    source = (qr << 8) | (g << 6) | (hf << 5) | (a << 4) | k
    out_ref[:, 0:256] = mm(ones_where(lane_row(512) == source), stack).astype(BF)

    first = feat_ref[:, 0:128]
    last = feat_ref[:, 3968:4096]
    p = down_col(64)
    lane = lane_row(128)
    rim_n = mm_nt(ones_where(lane == 63 - p), first)
    rim_s = mm_nt(ones_where(lane == 64 + p), last)
    pc = down_col(128)
    pos = pc & 63
    want = jnp.where(pc < 64, pos * 64, (63 - pos) * 64 + 63)
    rim_we = mm_nt(ones_where(lane_row(4096) == want), feat_ref[...])
    cr = down_col(16)
    at_first = jnp.where(cr == 0, 0, jnp.where(cr == 3, 63, -1))
    at_last = jnp.where(cr == 1, 64, jnp.where(cr == 2, 127, -1))
    corners = mm_nt(ones_where(lane == at_first), first) + mm_nt(ones_where(lane == at_last), last)
    tc = down_col(128)
    by_chan = jnp.zeros((16, 128), F32)
    for c in range(4):
        spread = jnp.broadcast_to(corners[c : c + 1, :], (16, 128))
        by_chan = by_chan + mm(keep((lane & 15) == cr, spread), ones_where(lane == (tc >> 4) * 4 + c))

    def over_lanes(x):
        rows = jnp.zeros((x.shape[0], 128), jnp.int32)
        for t in range(8):
            rows = jnp.where((lane & 7) == t, x[:, t : t + 1], rows)
        return rows

    def in_row(x, first_field):
        rows = over_lanes(x)
        side = iota(rows.shape, 0)
        mine = (iota(rows.shape, 1) >> 3) == side + first_field
        return jnp.sum(jnp.where(mine, rows, 0).astype(F32), axis=0, keepdims=True)

    side = iota((4, 8), 0)
    el, cl, slot = el_ref[...], cl_ref[...], slot_ref[...]
    edge = in_row(el >> 3, 0) + in_row((side + 2 + et_ref[...]) & 3, 4) + in_row(el & 7, 8)
    edge = edge + in_row(slot >> 3, 12) + in_row(slot & 7, 13)
    node = over_lanes(jnp.where(cl < 0, 127, cl >> 3)).astype(F32)
    pixel = over_lanes((cl & 7) * 4 + ((side + 2 + ct_ref[...]) & 3)).astype(F32)
    field = lane >> 3
    sub = down_col(16)
    small = jnp.where(sub == 0, edge, 0.0)
    for part in range(4):
        line = jnp.where(field == 14, node[part : part + 1, :], 0.0)
        line = jnp.where(field == 15, pixel[part : part + 1, :], line)
        small = small + jnp.where(sub == part + 1, line, 0.0)
    parts = [rim_n, rim_we[0:64], rim_s, rim_we[64:128], by_chan, small, jnp.zeros((96, 128), F32)]
    stack = jnp.concatenate([x.astype(BF) for x in parts], axis=0)
    r, node = row & 7, row >> 3
    source = jnp.where(r == 4, 256 + (node & 15), jnp.where(r == 5, 272, jnp.where(r == 6, 273 + (node >> 4), -1)))
    source = jnp.where(r < 4, r * 64 + node, source)
    out_ref[:, 256:384] = mm(ones_where(lane_row(384) == source), stack).astype(BF)


def pick_body(msg_ref, out_ref, slot_ref):
    cot = msg_ref[:, 0:256]
    misc = msg_ref[:, 256:384]
    col = lane_row(512)
    lane = lane_row(128)
    sub = down_col(512)
    near = down_col(128)
    base = (sub >> 3) << 3
    both = mm(ones_where((col == base + 5) | (col == base + 6)), misc)
    fields = mm(keep((lane & 7) == (sub & 7), both), ones_where((near >> 3) == lane))
    flip = fields.T
    slot_ref[...] = jnp.broadcast_to(flip[12:13, :] * 8.0 + flip[13:14, :], (8, 512))
    num = fields.astype(jnp.int32)

    def field(f):
        return num[:, f : f + 1]

    slot_row = field(12) * 8 + ((field(13) >> 1) << 1)
    lane2 = lane_row(256)
    fold_r = down_col(256)
    fold = ones_where(lane == (((fold_r >> 6) << 5) | (fold_r & 31)))
    mine = ((lane2 >> 5) & 1) == (field(13) & 1)
    for hf in range(2):
        got = mm(ones_where(col == slot_row + hf), cot)
        out_ref[:, hf * 128 : hf * 128 + 128] = mm(keep(mine, got), fold).astype(BF)
    total = jnp.zeros((512, 128), F32)
    for k in range(4):
        got = mm(ones_where(col == field(k) * 8 + field(4 + k)), misc)
        place = ones_where(lane == k * 16 + (near & 15))
        total = total + mm(keep((lane >> 4) == field(8 + k), got), place)
    got = mm(ones_where(col == field(14) * 8 + 4), misc)
    total = total + mm(keep(lane == field(15), got), ones_where(jnp.broadcast_to(lane == 64, (128, 128))))
    out_ref[:, 256:384] = total.astype(BF)


def regroup_body(me_ref, msg_ref, *out_refs):
    row = down_col(128)
    col = lane_row(512)
    lane = lane_row(128)
    pair, g, k, p = row >> 6, (row >> 4) & 3, row & 15, row & 63
    for d in range(4):
        out_ref = out_refs[d]
        tile = ((me_ref[0] ^ d) << 1) | pair
        out_ref[:, 0:256] = mm(ones_where(col == ((k << 5) | (g << 3) | tile)), msg_ref[:, 0:256]).astype(BF)
        got = mm(ones_where(col == ((p << 3) | tile)), msg_ref[:, 256:384])
        rims = jnp.where(lane < 64, got[0:64], pltpu.roll(got[64:128], 64, axis=1))
        pixels = jnp.zeros((16, 128), F32)
        for q in range(8):
            pixels = jnp.where(lane == q, got[q * 16 : q * 16 + 16, 64:65], pixels)
        rest = jnp.zeros((48, 128), F32)
        out_ref[:, 256:384] = jnp.concatenate([rims, pixels, rest], axis=0).astype(BF)


def lay_weights(raw_ref, w_ref, down_ref, down_t_ref, bias_ref):
    raw = jnp.concatenate(
        [
            jnp.concatenate([raw_ref[c, q * 16 : q * 16 + 16, 128 : 128 + n] for c in range(4)], axis=0)
            for q, n in ((0, 256), (1, 256), (2, 128))
        ],
        axis=1,
    )
    e = iota((640, 1), 0)
    i = (e * 7282) >> 16
    tap = e - i * 9
    dy = (tap * 86) >> 8
    to = jnp.where(e < 576, dy * 256 + (tap - dy * 3) * 64 + i, -9999)
    col = lane_row(1536)
    shifted = mm(raw, ones_where(jnp.where(col < 768, col, col - 832) == to)).astype(BF)
    zero = jnp.zeros((64, 256), BF)
    for a in range(2):
        for b in range(2):
            part = shifted[:, b * 768 : b * 768 + 768]
            row = (a * 2 + b) * 64
            w_ref[row : row + 64, :] = jnp.concatenate([zero, part] if a else [part, zero], axis=1)
    down = jnp.zeros((64, 256), F32)
    down_t = jnp.zeros((256, 64), F32)
    for c in range(4):
        mine = raw_ref[c, 0:64, 0:128]
        l = down_col(128)
        to = jnp.where(l < 64, (l & 3) * 64 + c * 16 + (l >> 2), -1)
        down = down + mm(mine, ones_where(lane_row(256) == to))
        l = lane_row(128)
        to = jnp.where(l < 64, (l & 3) * 64 + c * 16 + (l >> 2), -1)
        down_t = down_t + mm_nt(ones_where(down_col(256) == to), mine)
    down_ref[...] = down.astype(BF)
    down_t_ref[...] = down_t.astype(BF)
    bias = jnp.concatenate([raw_ref[c, 32:48, 256:259].astype(F32) for c in range(4)], axis=0)
    bias = (bias[:, 0:1] + bias[:, 1:2]) + bias[:, 2:3]
    bias_ref[...] = jnp.broadcast_to(jnp.concatenate([bias] * 4, axis=0), (256, 128))


def lay_places(side_ref, end_ref, conv_place_ref, down_place_ref):
    lane = lane_row(1024)
    v = lane & 31
    pos = down_col(64)
    for ry in range(4):
        y = ((lane >> 5) << 1) + (ry - 1)
        side_ref[ry, 0:64, :] = ones_where(jnp.where(v == 0, 63 - y, -1) == pos)
        side_ref[ry, 64:128, :] = ones_where(jnp.where(v == 31, y, -1) == pos)
    lane_e = lane_row(512)
    inner = lane_e & 127
    at = ((inner & 31) << 1) + (lane_e >> 7)
    end_ref[0:64, :] = ones_where(jnp.where(inner < 32, at - 1, -1) == pos)
    end_ref[64:128, :] = ones_where(jnp.where(inner >= 96, 64 - at, -1) == pos)
    kk = down_col(256)
    to = jnp.where(kk < 144, (kk & 15) * 9 + (kk >> 4), -1)
    conv_place_ref[...] = ones_where(lane_row(256) == to)
    kk = down_col(256)
    i, ab = kk & 63, kk >> 6
    down_place_ref[...] = ones_where(lane == ((i >> 4) << 8) + 144 + (i & 15) * 4 + ab)


def ready_body(me_ref, *refs):
    own_ref, own_raw_ref, first_refs, second_refs = refs[0], refs[1], refs[2:5], refs[5:8]
    win_ref, w_ref, down_ref, down_t_ref, bias_ref = refs[8:13]
    side_ref, end_ref, conv_place_ref, down_place_ref, x_ref, raw_ref = refs[13:]
    me = me_ref[0]
    lay_places(side_ref, end_ref, conv_place_ref, down_place_ref)
    raw_ref[me] = own_raw_ref[...]
    x_ref[me] = own_ref[...]
    for d in range(1, 4):
        second_ref = second_refs[d - 1]
        x_ref[me ^ d, 0:16, :] = first_refs[d - 1][...]
        x_ref[me ^ d, 16:32, :] = second_ref[:, 0:4096]
        for q in range(4):
            raw_ref[me ^ d, q * 16 : q * 16 + 16, :] = second_ref[:, 4096 + q * 384 : 4480 + q * 384]
    lay_weights(raw_ref, w_ref, down_ref, down_t_ref, bias_ref)
    l_in = down_col(512)
    to = (((l_in >> 6) & 1) << 8) | ((l_in & 1) << 7) | ((l_in >> 7) << 5) | ((l_in >> 1) & 31)
    order = ones_where(lane_row(512) == to)
    lane = lane_row(1024)
    v = lane & 31
    for t in range(2):
        x = jnp.concatenate([x_ref[c, t * 16 : t * 16 + 16, :] for c in range(4)], axis=0)
        stack = jnp.concatenate([x[:, q * 512 : q * 512 + 512] for q in range(8)], axis=0)
        split = mm(stack, order)
        cols = []
        for a in range(2):
            even, odd = [
                jnp.concatenate(
                    [split[q * 64 : q * 64 + 64, (a * 2 + b) * 128 : (a * 2 + b) * 128 + 128] for q in range(8)],
                    axis=1,
                )
                for b in range(2)
            ]
            cols.append(
                [
                    jnp.where(v == 0, 0.0, pltpu.roll(odd, 1, axis=1)),
                    even,
                    odd,
                    jnp.where(v == 31, 0.0, pltpu.roll(even, 1023, axis=1)),
                ]
            )
        for cx in range(4):
            top = jnp.where(lane < 32, 0.0, pltpu.roll(cols[1][cx], 32, axis=1))
            low = jnp.where(lane >= 992, 0.0, pltpu.roll(cols[0][cx], 992, axis=1))
            for ry, w in enumerate((top, cols[0][cx], cols[1][cx], low)):
                row = (ry * 4 + cx) * 64
                win_ref[t, row : row + 64, :] = w.astype(BF)


def level_body(me_ref, *refs):
    in_refs, (base_ref, w_ref, down_ref, down_t_ref, bias_ref) = refs[0:4], refs[4:9]
    side_ref, end_ref, conv_place_ref, down_place_ref = refs[9:13]
    out_refs, (msg_ref, sum_ref, win_ref, gc_ref) = refs[13:17], refs[17:]
    me = me_ref[0]
    for d in range(4):
        msg_ref[me ^ d] = in_refs[d][...]
    flip = [msg_ref[c, 0:64, 256:384].astype(F32).T.astype(BF) for c in range(4)]

    def strip(k):
        return jnp.concatenate(
            [f[t * 64 + k * 16 : t * 64 + k * 16 + 16, :] for t in range(2) for f in flip], axis=0
        )

    pixels = jnp.concatenate([msg_ref[c, 64:80, 256:384] for c in range(4)], axis=0).astype(F32)
    sides = {}
    v = lane_row(1024) & 31
    west_east = jnp.concatenate([strip(1), strip(3)], axis=1)
    for ry in range(4):
        both = mm(west_east, side_ref[ry])
        sides[ry, 0] = keep(v == 0, both)
        sides[ry, 3] = keep(v == 31, both)
    lane_e = lane_row(512)
    ends = mm(jnp.concatenate([strip(0), strip(2)], axis=1), end_ref[...])
    gd = jnp.zeros((64, 256), F32)
    gb = jnp.zeros((256, 1), F32)
    for t in range(2):
        end = ends[t * 64 : t * 64 + 64, :]
        for spot, k in ((0, 0), (96, 1), (384 + 31, 3), (384 + 127, 2)):
            end = jnp.where(lane_e == spot, pixels[:, t * 4 + k : t * 4 + k + 1], end)
        for ry in range(4):
            for cx in range(4):
                row = (ry * 4 + cx) * 64
                w = base_ref[t, row : row + 64, :]
                if (ry, cx) in sides:
                    w = w + sides[ry, cx][t * 64 : t * 64 + 64, :]
                win_ref[t, row : row + 64, :] = w
                edge = end[:, cx * 128 : cx * 128 + 128]
                if ry == 0:
                    fix = jnp.where(lane_row(128) < 64, edge, 0.0).astype(BF)
                    win_ref[t, row : row + 64, 0:128] = w[:, 0:128] + fix
                if ry == 3:
                    fix = jnp.where(lane_row(128) >= 64, edge, 0.0).astype(BF)
                    win_ref[t, row : row + 64, 896:1024] = w[:, 896:1024] + fix
    for t in range(2):
        pre = mm(w_ref[...], win_ref[t]) + bias_ref[:, 0:1]
        sig = 1.0 / (1.0 + jnp.exp(-pre))
        hidden = (pre * sig).astype(BF)
        quarter = mm(down_ref[...], hidden).astype(BF)
        for c in range(4):
            sum_ref[c, t * 16 : t * 16 + 16, :] = quarter[c * 16 : c * 16 + 16, :]
        back = jnp.concatenate(
            [
                jnp.concatenate(
                    [msg_ref[c, t * 64 + g * 16 : t * 64 + g * 16 + 16, 0:256] for c in range(4)], axis=0
                )
                for g in range(4)
            ],
            axis=1,
        )
        grad_hidden = mm(down_t_ref[...], back)
        grad_pre = (grad_hidden * (sig * (1.0 + pre * (1.0 - sig)))).astype(BF)
        gb = gb + jnp.sum(grad_pre.astype(F32), axis=1, keepdims=True)
        gd = gd + mm_nt(back, hidden)
        part = mm_nt(win_ref[t], grad_pre)
        gc_ref[...] = part if t == 0 else gc_ref[...] + part
    rows = []
    for dy in range(3):
        for cx in range(4):
            r0, r1 = (dy * 4 + cx) * 64, ((dy + 1) * 4 + cx) * 64
            rows.append(gc_ref[r0 : r0 + 64, 0:128] + gc_ref[r1 : r1 + 64, 128:256])
    taps = []
    for dy in range(3):
        for dx in range(3):
            taps.append(rows[dy * 4 + dx] + pltpu.roll(rows[dy * 4 + dx + 1], 64, axis=1))
    groups = []
    for q in range(4):
        rows = jnp.concatenate(
            [tap[q * 16 : q * 16 + 16, :] for tap in taps] + [jnp.zeros((112, 128), F32)], axis=0
        )
        groups.append(jnp.concatenate([rows[0:128].T, rows[128:256].T], axis=1)[0:64, :])
    conv = mm(jnp.concatenate(halves(jnp.concatenate(groups, axis=0)), axis=0), conv_place_ref[...])
    down = mm(jnp.concatenate(halves(gd), axis=0), down_place_ref[...])
    gb = gb[0:64, :] + gb[64:128, :] + gb[128:192, :] + gb[192:256, :]
    bias = [h.astype(F32) for h in halves(gb)]
    lane16 = lane_row(1024)
    for part in range(2):
        for c in range(4):
            both = jnp.concatenate(
                [
                    conv[part * 256 + q * 64 + c * 16 : part * 256 + q * 64 + c * 16 + 16, :]
                    + down[part * 64 + q * 16 : part * 64 + q * 16 + 16, c * 256 : c * 256 + 256]
                    for q in range(4)
                ],
                axis=1,
            )
            both = jnp.where(lane16 == 208, bias[part][c * 16 : c * 16 + 16, :], both)
            sum_ref[c, 32 + part * 16 : 48 + part * 16, :] = both.astype(BF)
    for d in range(4):
        out_refs[d][...] = sum_ref[me ^ d]


def spread_body(me_ref, *refs):
    in_refs, out_ref, msg_ref = refs[0:4], refs[4], refs[5]
    for d in range(4):
        msg_ref[me_ref[0] ^ d] = in_refs[d][...]
    stack = jnp.concatenate(
        [msg_ref[c, 0:32, g * 256 : g * 256 + 256] for g in range(4) for c in range(4)], axis=0
    )
    row = down_col(512)
    source = (((row >> 3) & 3) << 7) | (((row >> 1) & 3) << 5) | ((row & 1) << 4) | (row >> 5)
    out_ref[:, 0:256] = mm(ones_where(lane_row(512) == source), stack).astype(BF)
    total = jnp.zeros((16, 1024), F32)
    for c in range(4):
        total = total + (msg_ref[c, 32:48, :].astype(F32) + msg_ref[c, 48:64, :].astype(F32))
    parts = [
        h[:, s * 256 + o : s * 256 + o + 128] for h in halves(total) for o in (0, 128) for s in range(4)
    ]
    stack = jnp.concatenate(parts, axis=0)
    r, p = row & 7, row >> 3
    source = jnp.where(r < 4, (r << 6) + p, -1)
    out_ref[:, 256:384] = mm(ones_where(lane_row(256) == source), stack).astype(BF)


def place_body(msg_ref, slot_ref, out_ref):
    quarter = msg_ref[:, 0:256]
    slot = slot_ref[0:1, :].astype(jnp.int32)
    row = down_col(512)
    lane = lane_row(256)
    half = row & 1
    li = down_col(256)
    to = (((li >> 5) & 3) << 6) | (li & 31)
    total = jnp.zeros((512, 256), F32)
    for qc in range(2):
        got = mm(ones_where(slot == ((row >> 1) << 1) + qc), quarter)
        total = total + mm(keep((lane >> 7) == half, got), ones_where(lane == to + qc * 32))
    out_ref[:, 0:256] = total.astype(BF)
    r = down_col(16)
    src = lane_row(512) & 7
    src = jnp.where(src < 4, src & 1, -1)
    summed = mm(ones_where(src == jnp.where(r < 4, r & 1, -2)), msg_ref[:, 256:384])
    high, low = halves(summed)
    both = jnp.where(iota((16, 128), 0) < 2, high.astype(F32), low.astype(F32)).astype(BF)
    r = row & 7
    out_ref[:, 256:384] = mm(ones_where(lane_row(16) == jnp.where(r < 4, r, -1)), both).astype(BF)


def finish_body(msg_ref, coarse_ref, conv_ref, down_ref, bias_ref):
    row = down_col(512)
    col = lane_row(512)
    qr, g, hf, a, k = row >> 8, (row >> 6) & 3, (row >> 5) & 1, (row >> 4) & 1, row & 15
    source = (k << 5) | (g << 3) | (a << 2) | (qr << 1) | hf
    got = mm(ones_where(col == source), msg_ref[:, 0:256]).astype(BF)
    for q in range(16):
        coarse_ref[:, q * 256 : q * 256 + 256] = got[q * 32 : q * 32 + 32, :]

    row = down_col(256)
    got = mm(ones_where(col == ((row & 63) << 3) + (row >> 6)), msg_ref[:, 256:384])
    near = down_col(1024)
    to = jnp.where((near & 255) < 144, (near >> 8) * 144 + (near & 255), -1)
    place = ones_where(lane_row(576) == to)
    lane = lane_row(128)
    shift = ones_where(down_col(128) == jnp.where(lane < 64, lane + 16, -1))
    conv = jnp.zeros((16, 576), F32)
    down = jnp.zeros((64, 128), F32)
    for h in range(2):
        low, high = got[h * 128 : h * 128 + 64, :], got[h * 128 + 64 : h * 128 + 128, :]
        wide = jnp.concatenate(
            [x[s * 16 : s * 16 + 16, :] for s in range(4) for x in (low, high)], axis=1
        )
        conv = conv + mm(wide.astype(BF), place)
        down = down + mm(high.astype(BF), shift)
    conv_ref[...] = conv
    down_ref[...] = down[:, 0:64]
    bias = got[64:80, 80:81] + got[192:208, 80:81]
    bias_ref[...] = jnp.sum(jnp.where(lane_row(16) == down_col(16), bias, 0.0), axis=0, keepdims=True)


def to_peers(parts):
    return [parts[0]] + [
        lax.ppermute(parts[d], "chan", [(i, i ^ d) for i in range(4)]) for d in range(1, 4)
    ]


def on_device(
    features,
    conv_weight,
    conv_bias,
    down_weight,
    cotangent,
    edge_links,
    edge_turns,
    corner_links,
    corner_turns,
    child_slot,
):
    vmem = pl.BlockSpec(memory_space=pltpu.VMEM)
    msg = jax.ShapeDtypeStruct(MSG, BF)

    def to_nodes(x):
        return lax.all_to_all(x.reshape(64, 8, 384), "tile", 0, 0, tiled=True).reshape(MSG)

    me = lax.axis_index("chan").astype(jnp.int32).reshape(1)
    scalar = pl.BlockSpec(memory_space=pltpu.SMEM)
    first = jax.ShapeDtypeStruct((16, 4096), BF)
    second = jax.ShapeDtypeStruct((16, 5632), BF)
    pieces, raw, *peers = call(
        send_body,
        (msg, jax.ShapeDtypeStruct((64, 384), BF)) + (first,) * 3 + (second,) * 3,
        (1,),
        [scalar, whole((128, 4096)), whole((32, 4096))]
        + [whole((4, 8))] * 4
        + [whole((1, 8)), whole((16, 576)), whole((1, 16)), whole((64, 64))],
        (vmem,) * 8,
        flops=10**9,
        moved=2 * 10**6,
    )(
        me,
        *[
            pltpu.with_memory_space_constraint(x, pltpu.HBM)
            for x in (
                features.reshape(128, 4096),
                cotangent.reshape(32, 4096),
                edge_links.T,
                edge_turns.T,
                corner_links.T,
                corner_turns.T,
                child_slot.reshape(1, 8),
                conv_weight,
                conv_bias.reshape(1, 16),
                down_weight,
            )
        ],
    )
    first = to_peers([None] + peers[0:3])[1:]
    second = to_peers([None] + peers[3:6])[1:]
    pieces, first = lax.optimization_barrier((to_nodes(pieces), first))
    picked, slots = call(
        pick_body,
        (msg, jax.ShapeDtypeStruct((8, 512), F32)),
        (1,),
        [vmem],
        (vmem, vmem),
        flops=10**9,
        moved=10**6,
    )(pieces)
    picked = to_nodes(picked)
    own = pl.BlockSpec((32, 4096), lambda i, m: (m[0], 0))
    ready = pl.pallas_call(
        ready_body,
        out_shape=(
            jax.ShapeDtypeStruct((2, 1024, 1024), BF),
            jax.ShapeDtypeStruct((256, 1024), BF),
            jax.ShapeDtypeStruct((64, 256), BF),
            jax.ShapeDtypeStruct((256, 64), BF),
            jax.ShapeDtypeStruct((256, 128), F32),
            jax.ShapeDtypeStruct((4, 128, 1024), BF),
            jax.ShapeDtypeStruct((128, 512), BF),
            jax.ShapeDtypeStruct((256, 256), BF),
            jax.ShapeDtypeStruct((256, 1024), BF),
        ),
        grid_spec=pltpu.PrefetchScalarGridSpec(
            num_scalar_prefetch=1,
            grid=(1,),
            in_specs=[own] + [vmem] * 7,
            out_specs=(vmem,) * 9,
            scratch_shapes=(pltpu.VMEM((4, 32, 4096), BF), pltpu.VMEM((4, 64, 384), BF)),
        ),
        compiler_params=pltpu.CompilerParams(vmem_limit_bytes=32 << 20),
        cost_estimate=pl.CostEstimate(flops=10**9, bytes_accessed=4 * 10**6, transcendentals=0),
    )(me, features.reshape(128, 4096), raw, *first, *second)
    group = jax.ShapeDtypeStruct((128, 384), BF)
    picked = call(
        regroup_body,
        (group,) * 4,
        (1,),
        [scalar, vmem],
        (vmem,) * 4,
        flops=4 * 10**8,
        moved=10**6,
    )(me, picked)
    picked = to_peers(picked)
    local = pl.pallas_call(
        level_body,
        out_shape=(jax.ShapeDtypeStruct((64, 1024), BF),) * 4,
        in_specs=[scalar] + [vmem] * 13,
        out_specs=(vmem,) * 4,
        scratch_shapes=(
            pltpu.VMEM((4, 128, 384), BF),
            pltpu.VMEM((4, 64, 1024), BF),
            pltpu.VMEM((2, 1024, 1024), BF),
            pltpu.VMEM((1024, 256), F32),
        ),
        compiler_params=pltpu.CompilerParams(vmem_limit_bytes=32 << 20),
        cost_estimate=pl.CostEstimate(flops=4 * 10**9, bytes_accessed=4 * 10**6, transcendentals=0),
    )(me, *picked, *ready)
    local = to_peers(local)
    out = call(
        spread_body,
        msg,
        (1,),
        [scalar] + [vmem] * 4,
        vmem,
        (pltpu.VMEM((4, 64, 1024), BF),),
        flops=4 * 10**8,
        moved=10**6,
    )(me, *local)
    out = to_nodes(out)
    out = call(place_body, msg, (1,), [vmem, vmem], vmem, flops=5 * 10**8, moved=10**6)(
        out, slots
    )
    out = to_nodes(out)
    coarse, grad_conv, grad_down, grad_bias = call(
        finish_body,
        (
            jax.ShapeDtypeStruct((32, 4096), BF),
            jax.ShapeDtypeStruct((16, 576), F32),
            jax.ShapeDtypeStruct((64, 64), F32),
            jax.ShapeDtypeStruct((1, 16), F32),
        ),
        (1,),
        [vmem],
        (
            whole((32, 4096)),
            whole((16, 576)),
            whole((64, 64)),
            whole((1, 16)),
        ),
        flops=4 * 10**8,
        moved=10**6,
    )(out)
    return (coarse.reshape(2, 16, 4096), grad_conv, grad_bias.reshape(16), grad_down)


def solution(mesh):
    in_specs = (
        P("tile", "chan", None),
        P("chan", None),
        P("chan"),
        P(None, "chan"),
        P("tile", "chan", None),
        P("tile", None),
        P("tile", None),
        P("tile", None),
        P("tile", None),
        P("tile"),
    )
    out_specs = (P("tile", "chan", None), P("chan", None), P("chan"), P(None, "chan"))
    return jax.shard_map(
        on_device, mesh=mesh, in_specs=in_specs, out_specs=out_specs, check_vma=False
    )
```

```python
import jax
import jax.numpy as jnp
from jax import lax
from jax.experimental import pallas as pl
from jax.experimental.pallas import tpu as pltpu
from jax.sharding import PartitionSpec as P

BF = jnp.bfloat16
F32 = jnp.float32
NODES = 64
MSG = (NODES * 8, 384)


def iota(shape, dim):
    return lax.broadcasted_iota(jnp.int32, shape, dim)


def down_col(n, start=0):
    return iota((n, 1), 0) + start


def lane_row(n):
    return iota((1, n), 1)


def ones_where(mask):
    return jnp.where(mask, 1.0, 0.0).astype(BF)


def keep(mask, x):
    return jnp.where(mask, x, 0.0).astype(BF)


def mm(a, b):
    return jnp.dot(a, b, preferred_element_type=F32)


def mm_nt(a, b):
    return lax.dot_general(a, b, (((1,), (1,)), ((), ())), preferred_element_type=F32)


def halves(x):
    high = x.astype(BF)
    return high, (x - high.astype(F32)).astype(BF)


def call(body, out_shape, grid, in_specs, out_specs, scratch=(), flops=0, moved=0):
    return pl.pallas_call(
        body,
        out_shape=out_shape,
        grid=grid,
        in_specs=in_specs,
        out_specs=out_specs,
        scratch_shapes=scratch,
        compiler_params=pltpu.CompilerParams(vmem_limit_bytes=48 << 20),
        cost_estimate=pl.CostEstimate(flops=flops, bytes_accessed=moved, transcendentals=0),
    )


def whole(shape):
    return pl.BlockSpec(shape, lambda *i: (0,) * len(shape))


def pack_weights(conv_ref, bias_ref, down_ref, raw_ref):
    zero = jnp.zeros((64, 64), BF)
    lane = lane_row(128)
    bias = jnp.where(lane_row(16) == down_col(16), bias_ref[...], 0.0)
    bias = jnp.sum(bias, axis=1, keepdims=True)
    b0 = bias.astype(BF).astype(F32)
    b1 = (bias - b0).astype(BF).astype(F32)
    b2 = (bias - b0) - b1
    bias = jnp.where(lane == 0, b0, jnp.where(lane == 1, b1, jnp.where(lane == 2, b2, 0.0))).astype(BF)
    raw_ref[:, 0:128] = jnp.concatenate([down_ref[...], zero], axis=1)
    raw_ref[0:16, 128:384] = conv_ref[:, 0:256]
    raw_ref[16:32, 128:384] = conv_ref[:, 256:512]
    raw_ref[32:48, 128:256] = jnp.concatenate([conv_ref[:, 512:576], zero[0:16]], axis=1)
    raw_ref[32:48, 256:384] = bias
    raw_ref[48:64, 128:384] = jnp.zeros((16, 256), BF)


def send_body(
    me_ref,
    feat_ref,
    cot_ref,
    el_ref,
    et_ref,
    cl_ref,
    ct_ref,
    slot_ref,
    conv_ref,
    bias_ref,
    down_ref,
    out_ref,
    raw_ref,
    *peer_refs,
):
    pack_weights(conv_ref, bias_ref, down_ref, raw_ref)
    for d in range(1, 4):
        peer = me_ref[0] ^ d
        first_ref, second_ref = peer_refs[d - 1], peer_refs[d + 2]
        first_ref[...] = feat_ref[pl.ds(pl.multiple_of(peer * 32, 16), 16), :]
        second_ref[:, 0:4096] = feat_ref[pl.ds(pl.multiple_of(peer * 32 + 16, 16), 16), :]
        for q in range(4):
            second_ref[:, 4096 + q * 384 : 4480 + q * 384] = raw_ref[q * 16 : q * 16 + 16, :]

    cot = cot_ref[...]
    stack = jnp.concatenate([cot[:, q * 256 : q * 256 + 256] for q in range(16)], axis=0)
    row = down_col(512)
    k, g, a, qr, hf = row >> 5, (row >> 3) & 3, (row >> 2) & 1, (row >> 1) & 1, row & 1
    source = (qr << 8) | (g << 6) | (hf << 5) | (a << 4) | k
    out_ref[:, 0:256] = mm(ones_where(lane_row(512) == source), stack).astype(BF)

    first = feat_ref[:, 0:128]
    last = feat_ref[:, 3968:4096]
    p = down_col(64)
    lane = lane_row(128)
    rim_n = mm_nt(ones_where(lane == 63 - p), first)
    rim_s = mm_nt(ones_where(lane == 64 + p), last)
    pc = down_col(128)
    pos = pc & 63
    want = jnp.where(pc < 64, pos * 64, (63 - pos) * 64 + 63)
    rim_we = mm_nt(ones_where(lane_row(4096) == want), feat_ref[...])
    cr = down_col(16)
    at_first = jnp.where(cr == 0, 0, jnp.where(cr == 3, 63, -1))
    at_last = jnp.where(cr == 1, 64, jnp.where(cr == 2, 127, -1))
    corners = mm_nt(ones_where(lane == at_first), first) + mm_nt(ones_where(lane == at_last), last)
    tc = down_col(128)
    by_chan = jnp.zeros((16, 128), F32)
    for c in range(4):
        spread = jnp.broadcast_to(corners[c : c + 1, :], (16, 128))
        by_chan = by_chan + mm(keep((lane & 15) == cr, spread), ones_where(lane == (tc >> 4) * 4 + c))

    def over_lanes(x):
        rows = jnp.zeros((x.shape[0], 128), jnp.int32)
        for t in range(8):
            rows = jnp.where((lane & 7) == t, x[:, t : t + 1], rows)
        return rows

    def in_row(x, first_field):
        rows = over_lanes(x)
        side = iota(rows.shape, 0)
        mine = (iota(rows.shape, 1) >> 3) == side + first_field
        return jnp.sum(jnp.where(mine, rows, 0).astype(F32), axis=0, keepdims=True)

    side = iota((4, 8), 0)
    el, cl, slot = el_ref[...], cl_ref[...], slot_ref[...]
    edge = in_row(el >> 3, 0) + in_row((side + 2 + et_ref[...]) & 3, 4) + in_row(el & 7, 8)
    edge = edge + in_row(slot >> 3, 12) + in_row(slot & 7, 13)
    node = over_lanes(jnp.where(cl < 0, 127, cl >> 3)).astype(F32)
    pixel = over_lanes((cl & 7) * 4 + ((side + 2 + ct_ref[...]) & 3)).astype(F32)
    field = lane >> 3
    sub = down_col(16)
    small = jnp.where(sub == 0, edge, 0.0)
    for part in range(4):
        line = jnp.where(field == 14, node[part : part + 1, :], 0.0)
        line = jnp.where(field == 15, pixel[part : part + 1, :], line)
        small = small + jnp.where(sub == part + 1, line, 0.0)
    parts = [rim_n, rim_we[0:64], rim_s, rim_we[64:128], by_chan, small, jnp.zeros((96, 128), F32)]
    stack = jnp.concatenate([x.astype(BF) for x in parts], axis=0)
    r, node = row & 7, row >> 3
    source = jnp.where(r == 4, 256 + (node & 15), jnp.where(r == 5, 272, jnp.where(r == 6, 273 + (node >> 4), -1)))
    source = jnp.where(r < 4, r * 64 + node, source)
    out_ref[:, 256:384] = mm(ones_where(lane_row(384) == source), stack).astype(BF)


def pick_body(msg_ref, out_ref, slot_ref):
    cot = msg_ref[:, 0:256]
    misc = msg_ref[:, 256:384]
    col = lane_row(512)
    lane = lane_row(128)
    sub = down_col(512)
    near = down_col(128)
    base = (sub >> 3) << 3
    both = mm(ones_where((col == base + 5) | (col == base + 6)), misc)
    fields = mm(keep((lane & 7) == (sub & 7), both), ones_where((near >> 3) == lane))
    flip = fields.T
    slot_ref[...] = jnp.broadcast_to(flip[12:13, :] * 8.0 + flip[13:14, :], (8, 512))
    num = fields.astype(jnp.int32)

    def field(f):
        return num[:, f : f + 1]

    slot_row = field(12) * 8 + ((field(13) >> 1) << 1)
    lane2 = lane_row(256)
    fold_r = down_col(256)
    fold = ones_where(lane == (((fold_r >> 6) << 5) | (fold_r & 31)))
    mine = ((lane2 >> 5) & 1) == (field(13) & 1)
    for hf in range(2):
        got = mm(ones_where(col == slot_row + hf), cot)
        out_ref[:, hf * 128 : hf * 128 + 128] = mm(keep(mine, got), fold).astype(BF)
    total = jnp.zeros((512, 128), F32)
    for k in range(4):
        got = mm(ones_where(col == field(k) * 8 + field(4 + k)), misc)
        place = ones_where(lane == k * 16 + (near & 15))
        total = total + mm(keep((lane >> 4) == field(8 + k), got), place)
    got = mm(ones_where(col == field(14) * 8 + 4), misc)
    total = total + mm(keep(lane == field(15), got), ones_where(jnp.broadcast_to(lane == 64, (128, 128))))
    out_ref[:, 256:384] = total.astype(BF)


def regroup_body(me_ref, msg_ref, *out_refs):
    row = down_col(128)
    col = lane_row(512)
    lane = lane_row(128)
    pair, g, k, p = row >> 6, (row >> 4) & 3, row & 15, row & 63
    for d in range(4):
        out_ref = out_refs[d]
        tile = ((me_ref[0] ^ d) << 1) | pair
        out_ref[:, 0:256] = mm(ones_where(col == ((k << 5) | (g << 3) | tile)), msg_ref[:, 0:256]).astype(BF)
        got = mm(ones_where(col == ((p << 3) | tile)), msg_ref[:, 256:384])
        rims = jnp.where(lane < 64, got[0:64], pltpu.roll(got[64:128], 64, axis=1))
        pixels = jnp.zeros((16, 128), F32)
        for q in range(8):
            pixels = jnp.where(lane == q, got[q * 16 : q * 16 + 16, 64:65], pixels)
        rest = jnp.zeros((48, 128), F32)
        out_ref[:, 256:384] = jnp.concatenate([rims, pixels, rest], axis=0).astype(BF)


def lay_weights(raw_ref, w_ref, down_ref, down_t_ref, bias_ref):
    raw = jnp.concatenate(
        [
            jnp.concatenate([raw_ref[c, q * 16 : q * 16 + 16, 128 : 128 + n] for c in range(4)], axis=0)
            for q, n in ((0, 256), (1, 256), (2, 128))
        ],
        axis=1,
    )
    e = iota((640, 1), 0)
    i = (e * 7282) >> 16
    tap = e - i * 9
    dy = (tap * 86) >> 8
    to = jnp.where(e < 576, dy * 256 + (tap - dy * 3) * 64 + i, -9999)
    col = lane_row(1536)
    shifted = mm(raw, ones_where(jnp.where(col < 768, col, col - 832) == to)).astype(BF)
    zero = jnp.zeros((64, 256), BF)
    for a in range(2):
        for b in range(2):
            part = shifted[:, b * 768 : b * 768 + 768]
            row = (a * 2 + b) * 64
            w_ref[row : row + 64, :] = jnp.concatenate([zero, part] if a else [part, zero], axis=1)
    down = jnp.zeros((64, 256), F32)
    down_t = jnp.zeros((256, 64), F32)
    for c in range(4):
        mine = raw_ref[c, 0:64, 0:128]
        l = down_col(128)
        to = jnp.where(l < 64, (l & 3) * 64 + c * 16 + (l >> 2), -1)
        down = down + mm(mine, ones_where(lane_row(256) == to))
        l = lane_row(128)
        to = jnp.where(l < 64, (l & 3) * 64 + c * 16 + (l >> 2), -1)
        down_t = down_t + mm_nt(ones_where(down_col(256) == to), mine)
    down_ref[...] = down.astype(BF)
    down_t_ref[...] = down_t.astype(BF)
    bias = jnp.concatenate([raw_ref[c, 32:48, 256:259].astype(F32) for c in range(4)], axis=0)
    bias = (bias[:, 0:1] + bias[:, 1:2]) + bias[:, 2:3]
    bias_ref[...] = jnp.broadcast_to(jnp.concatenate([bias] * 4, axis=0), (256, 128))


def lay_places(side_ref, end_ref, conv_place_ref, down_place_ref):
    lane = lane_row(1024)
    v = lane & 31
    pos = down_col(64)
    for ry in range(4):
        y = ((lane >> 5) << 1) + (ry - 1)
        side_ref[ry, 0:64, :] = ones_where(jnp.where(v == 0, 63 - y, -1) == pos)
        side_ref[ry, 64:128, :] = ones_where(jnp.where(v == 31, y, -1) == pos)
    lane_e = lane_row(512)
    inner = lane_e & 127
    at = ((inner & 31) << 1) + (lane_e >> 7)
    end_ref[0:64, :] = ones_where(jnp.where(inner < 32, at - 1, -1) == pos)
    end_ref[64:128, :] = ones_where(jnp.where(inner >= 96, 64 - at, -1) == pos)
    kk = down_col(256)
    to = jnp.where(kk < 144, (kk & 15) * 9 + (kk >> 4), -1)
    conv_place_ref[...] = ones_where(lane_row(256) == to)
    kk = down_col(256)
    i, ab = kk & 63, kk >> 6
    down_place_ref[...] = ones_where(lane == ((i >> 4) << 8) + 144 + (i & 15) * 4 + ab)


def ready_body(me_ref, *refs):
    own_ref, own_raw_ref, first_refs, second_refs = refs[0], refs[1], refs[2:5], refs[5:8]
    win_ref, w_ref, down_ref, down_t_ref, bias_ref = refs[8:13]
    side_ref, end_ref, conv_place_ref, down_place_ref, x_ref, raw_ref = refs[13:]
    me = me_ref[0]
    lay_places(side_ref, end_ref, conv_place_ref, down_place_ref)
    raw_ref[me] = own_raw_ref[...]
    x_ref[me] = own_ref[...]
    for d in range(1, 4):
        second_ref = second_refs[d - 1]
        x_ref[me ^ d, 0:16, :] = first_refs[d - 1][...]
        x_ref[me ^ d, 16:32, :] = second_ref[:, 0:4096]
        for q in range(4):
            raw_ref[me ^ d, q * 16 : q * 16 + 16, :] = second_ref[:, 4096 + q * 384 : 4480 + q * 384]
    lay_weights(raw_ref, w_ref, down_ref, down_t_ref, bias_ref)
    l_in = down_col(512)
    to = (((l_in >> 6) & 1) << 8) | ((l_in & 1) << 7) | ((l_in >> 7) << 5) | ((l_in >> 1) & 31)
    order = ones_where(lane_row(512) == to)
    lane = lane_row(1024)
    v = lane & 31
    for t in range(2):
        x = jnp.concatenate([x_ref[c, t * 16 : t * 16 + 16, :] for c in range(4)], axis=0)
        stack = jnp.concatenate([x[:, q * 512 : q * 512 + 512] for q in range(8)], axis=0)
        split = mm(stack, order)
        cols = []
        for a in range(2):
            even, odd = [
                jnp.concatenate(
                    [split[q * 64 : q * 64 + 64, (a * 2 + b) * 128 : (a * 2 + b) * 128 + 128] for q in range(8)],
                    axis=1,
                )
                for b in range(2)
            ]
            cols.append(
                [
                    jnp.where(v == 0, 0.0, pltpu.roll(odd, 1, axis=1)),
                    even,
                    odd,
                    jnp.where(v == 31, 0.0, pltpu.roll(even, 1023, axis=1)),
                ]
            )
        for cx in range(4):
            top = jnp.where(lane < 32, 0.0, pltpu.roll(cols[1][cx], 32, axis=1))
            low = jnp.where(lane >= 992, 0.0, pltpu.roll(cols[0][cx], 992, axis=1))
            for ry, w in enumerate((top, cols[0][cx], cols[1][cx], low)):
                row = (ry * 4 + cx) * 64
                win_ref[t, row : row + 64, :] = w.astype(BF)


def level_body(me_ref, *refs):
    in_refs, (base_ref, w_ref, down_ref, down_t_ref, bias_ref) = refs[0:4], refs[4:9]
    side_ref, end_ref, conv_place_ref, down_place_ref = refs[9:13]
    out_refs, (msg_ref, sum_ref, win_ref, gc_ref) = refs[13:17], refs[17:]
    me = me_ref[0]
    for d in range(4):
        msg_ref[me ^ d] = in_refs[d][...]
    flip = [msg_ref[c, 0:64, 256:384].astype(F32).T.astype(BF) for c in range(4)]

    def strip(k):
        return jnp.concatenate(
            [f[t * 64 + k * 16 : t * 64 + k * 16 + 16, :] for t in range(2) for f in flip], axis=0
        )

    pixels = jnp.concatenate([msg_ref[c, 64:80, 256:384] for c in range(4)], axis=0).astype(F32)
    sides = {}
    v = lane_row(1024) & 31
    west_east = jnp.concatenate([strip(1), strip(3)], axis=1)
    for ry in range(4):
        both = mm(west_east, side_ref[ry])
        sides[ry, 0] = keep(v == 0, both)
        sides[ry, 3] = keep(v == 31, both)
    lane_e = lane_row(512)
    ends = mm(jnp.concatenate([strip(0), strip(2)], axis=1), end_ref[...])
    gd = jnp.zeros((64, 256), F32)
    gb = jnp.zeros((256, 1), F32)
    for t in range(2):
        end = ends[t * 64 : t * 64 + 64, :]
        for spot, k in ((0, 0), (96, 1), (384 + 31, 3), (384 + 127, 2)):
            end = jnp.where(lane_e == spot, pixels[:, t * 4 + k : t * 4 + k + 1], end)
        for ry in range(4):
            for cx in range(4):
                row = (ry * 4 + cx) * 64
                w = base_ref[t, row : row + 64, :]
                if (ry, cx) in sides:
                    w = w + sides[ry, cx][t * 64 : t * 64 + 64, :]
                win_ref[t, row : row + 64, :] = w
                edge = end[:, cx * 128 : cx * 128 + 128]
                if ry == 0:
                    fix = jnp.where(lane_row(128) < 64, edge, 0.0).astype(BF)
                    win_ref[t, row : row + 64, 0:128] = w[:, 0:128] + fix
                if ry == 3:
                    fix = jnp.where(lane_row(128) >= 64, edge, 0.0).astype(BF)
                    win_ref[t, row : row + 64, 896:1024] = w[:, 896:1024] + fix
    for t in range(2):
        pre = mm(w_ref[...], win_ref[t]) + bias_ref[:, 0:1]
        sig = 1.0 / (1.0 + jnp.exp(-pre))
        hidden = (pre * sig).astype(BF)
        quarter = mm(down_ref[...], hidden).astype(BF)
        for c in range(4):
            sum_ref[c, t * 16 : t * 16 + 16, :] = quarter[c * 16 : c * 16 + 16, :]
        back = jnp.concatenate(
            [
                jnp.concatenate(
                    [msg_ref[c, t * 64 + g * 16 : t * 64 + g * 16 + 16, 0:256] for c in range(4)], axis=0
                )
                for g in range(4)
            ],
            axis=1,
        )
        grad_hidden = mm(down_t_ref[...], back)
        grad_pre = (grad_hidden * (sig * (1.0 + pre * (1.0 - sig)))).astype(BF)
        gb = gb + jnp.sum(grad_pre.astype(F32), axis=1, keepdims=True)
        gd = gd + mm_nt(back, hidden)
        part = mm_nt(win_ref[t], grad_pre)
        gc_ref[...] = part if t == 0 else gc_ref[...] + part
    rows = []
    for dy in range(3):
        for cx in range(4):
            r0, r1 = (dy * 4 + cx) * 64, ((dy + 1) * 4 + cx) * 64
            rows.append(gc_ref[r0 : r0 + 64, 0:128] + gc_ref[r1 : r1 + 64, 128:256])
    taps = []
    for dy in range(3):
        for dx in range(3):
            taps.append(rows[dy * 4 + dx] + pltpu.roll(rows[dy * 4 + dx + 1], 64, axis=1))
    groups = []
    for q in range(4):
        rows = jnp.concatenate(
            [tap[q * 16 : q * 16 + 16, :] for tap in taps] + [jnp.zeros((112, 128), F32)], axis=0
        )
        groups.append(jnp.concatenate([rows[0:128].T, rows[128:256].T], axis=1)[0:64, :])
    conv = mm(jnp.concatenate(halves(jnp.concatenate(groups, axis=0)), axis=0), conv_place_ref[...])
    down = mm(jnp.concatenate(halves(gd), axis=0), down_place_ref[...])
    gb = gb[0:64, :] + gb[64:128, :] + gb[128:192, :] + gb[192:256, :]
    bias = [h.astype(F32) for h in halves(gb)]
    lane16 = lane_row(1024)
    for part in range(2):
        for c in range(4):
            both = jnp.concatenate(
                [
                    conv[part * 256 + q * 64 + c * 16 : part * 256 + q * 64 + c * 16 + 16, :]
                    + down[part * 64 + q * 16 : part * 64 + q * 16 + 16, c * 256 : c * 256 + 256]
                    for q in range(4)
                ],
                axis=1,
            )
            both = jnp.where(lane16 == 208, bias[part][c * 16 : c * 16 + 16, :], both)
            sum_ref[c, 32 + part * 16 : 48 + part * 16, :] = both.astype(BF)
    for d in range(4):
        out_refs[d][...] = sum_ref[me ^ d]


def spread_body(me_ref, *refs):
    in_refs, out_ref, msg_ref = refs[0:4], refs[4], refs[5]
    for d in range(4):
        msg_ref[me_ref[0] ^ d] = in_refs[d][...]
    stack = jnp.concatenate(
        [msg_ref[c, 0:32, g * 256 : g * 256 + 256] for g in range(4) for c in range(4)], axis=0
    )
    row = down_col(512)
    source = (((row >> 3) & 3) << 7) | (((row >> 1) & 3) << 5) | ((row & 1) << 4) | (row >> 5)
    out_ref[:, 0:256] = mm(ones_where(lane_row(512) == source), stack).astype(BF)
    total = jnp.zeros((16, 1024), F32)
    for c in range(4):
        total = total + (msg_ref[c, 32:48, :].astype(F32) + msg_ref[c, 48:64, :].astype(F32))
    parts = [
        h[:, s * 256 + o : s * 256 + o + 128] for h in halves(total) for o in (0, 128) for s in range(4)
    ]
    stack = jnp.concatenate(parts, axis=0)
    r, p = row & 7, row >> 3
    source = jnp.where(r < 4, (r << 6) + p, -1)
    out_ref[:, 256:384] = mm(ones_where(lane_row(256) == source), stack).astype(BF)


def place_body(msg_ref, slot_ref, out_ref):
    quarter = msg_ref[:, 0:256]
    slot = slot_ref[0:1, :].astype(jnp.int32)
    row = down_col(512)
    lane = lane_row(256)
    half = row & 1
    li = down_col(256)
    to = (((li >> 5) & 3) << 6) | (li & 31)
    total = jnp.zeros((512, 256), F32)
    for qc in range(2):
        got = mm(ones_where(slot == ((row >> 1) << 1) + qc), quarter)
        total = total + mm(keep((lane >> 7) == half, got), ones_where(lane == to + qc * 32))
    out_ref[:, 0:256] = total.astype(BF)
    r = down_col(16)
    src = lane_row(512) & 7
    src = jnp.where(src < 4, src & 1, -1)
    summed = mm(ones_where(src == jnp.where(r < 4, r & 1, -2)), msg_ref[:, 256:384])
    high, low = halves(summed)
    both = jnp.where(iota((16, 128), 0) < 2, high.astype(F32), low.astype(F32)).astype(BF)
    r = row & 7
    out_ref[:, 256:384] = mm(ones_where(lane_row(16) == jnp.where(r < 4, r, -1)), both).astype(BF)


def finish_body(msg_ref, coarse_ref, conv_ref, down_ref, bias_ref):
    row = down_col(512)
    col = lane_row(512)
    qr, g, hf, a, k = row >> 8, (row >> 6) & 3, (row >> 5) & 1, (row >> 4) & 1, row & 15
    source = (k << 5) | (g << 3) | (a << 2) | (qr << 1) | hf
    got = mm(ones_where(col == source), msg_ref[:, 0:256]).astype(BF)
    for q in range(16):
        coarse_ref[:, q * 256 : q * 256 + 256] = got[q * 32 : q * 32 + 32, :]

    row = down_col(256)
    got = mm(ones_where(col == ((row & 63) << 3) + (row >> 6)), msg_ref[:, 256:384])
    value = jnp.concatenate([got[0:64] + got[128:192], got[64:128] + got[192:256]], axis=1)
    head = jnp.where(lane_row(256) < 144, value, 0.0)
    pad = jnp.zeros((16, 384), F32)
    conv = jnp.zeros((16, 640), F32)
    for q in range(4):
        part = jnp.concatenate([head[q * 16 : q * 16 + 16, :], pad], axis=1)
        conv = conv + (pltpu.roll(part, q * 144, axis=1) if q else part)
    conv_ref[...] = conv[:, 0:576]
    down_ref[...] = pltpu.roll(value, 112, axis=1)[:, 0:64]
    bias = value[0:16, 208:209]
    bias_ref[...] = jnp.sum(jnp.where(lane_row(16) == down_col(16), bias, 0.0), axis=0, keepdims=True)


def to_peers(parts):
    return [parts[0]] + [
        lax.ppermute(parts[d], "chan", [(i, i ^ d) for i in range(4)]) for d in range(1, 4)
    ]


def on_device(
    features,
    conv_weight,
    conv_bias,
    down_weight,
    cotangent,
    edge_links,
    edge_turns,
    corner_links,
    corner_turns,
    child_slot,
):
    vmem = pl.BlockSpec(memory_space=pltpu.VMEM)
    msg = jax.ShapeDtypeStruct(MSG, BF)

    def to_nodes(x):
        return lax.all_to_all(x.reshape(64, 8, 384), "tile", 0, 0, tiled=True).reshape(MSG)

    me = lax.axis_index("chan").astype(jnp.int32).reshape(1)
    scalar = pl.BlockSpec(memory_space=pltpu.SMEM)
    first = jax.ShapeDtypeStruct((16, 4096), BF)
    second = jax.ShapeDtypeStruct((16, 5632), BF)
    pieces, raw, *peers = call(
        send_body,
        (msg, jax.ShapeDtypeStruct((64, 384), BF)) + (first,) * 3 + (second,) * 3,
        (1,),
        [scalar, whole((128, 4096)), whole((32, 4096))]
        + [whole((4, 8))] * 4
        + [whole((1, 8)), whole((16, 576)), whole((1, 16)), whole((64, 64))],
        (vmem,) * 8,
        flops=10**9,
        moved=2 * 10**6,
    )(
        me,
        *[
            pltpu.with_memory_space_constraint(x, pltpu.HBM)
            for x in (
                features.reshape(128, 4096),
                cotangent.reshape(32, 4096),
                edge_links.T,
                edge_turns.T,
                corner_links.T,
                corner_turns.T,
                child_slot.reshape(1, 8),
                conv_weight,
                conv_bias.reshape(1, 16),
                down_weight,
            )
        ],
    )
    first = to_peers([None] + peers[0:3])[1:]
    second = to_peers([None] + peers[3:6])[1:]
    pieces, first = lax.optimization_barrier((to_nodes(pieces), first))
    picked, slots = call(
        pick_body,
        (msg, jax.ShapeDtypeStruct((8, 512), F32)),
        (1,),
        [vmem],
        (vmem, vmem),
        flops=10**9,
        moved=10**6,
    )(pieces)
    picked = to_nodes(picked)
    own = pl.BlockSpec((32, 4096), lambda i, m: (m[0], 0))
    ready = pl.pallas_call(
        ready_body,
        out_shape=(
            jax.ShapeDtypeStruct((2, 1024, 1024), BF),
            jax.ShapeDtypeStruct((256, 1024), BF),
            jax.ShapeDtypeStruct((64, 256), BF),
            jax.ShapeDtypeStruct((256, 64), BF),
            jax.ShapeDtypeStruct((256, 128), F32),
            jax.ShapeDtypeStruct((4, 128, 1024), BF),
            jax.ShapeDtypeStruct((128, 512), BF),
            jax.ShapeDtypeStruct((256, 256), BF),
            jax.ShapeDtypeStruct((256, 1024), BF),
        ),
        grid_spec=pltpu.PrefetchScalarGridSpec(
            num_scalar_prefetch=1,
            grid=(1,),
            in_specs=[own] + [vmem] * 7,
            out_specs=(vmem,) * 9,
            scratch_shapes=(pltpu.VMEM((4, 32, 4096), BF), pltpu.VMEM((4, 64, 384), BF)),
        ),
        compiler_params=pltpu.CompilerParams(vmem_limit_bytes=32 << 20),
        cost_estimate=pl.CostEstimate(flops=10**9, bytes_accessed=4 * 10**6, transcendentals=0),
    )(me, features.reshape(128, 4096), raw, *first, *second)
    group = jax.ShapeDtypeStruct((128, 384), BF)
    picked = call(
        regroup_body,
        (group,) * 4,
        (1,),
        [scalar, vmem],
        (vmem,) * 4,
        flops=4 * 10**8,
        moved=10**6,
    )(me, picked)
    picked = to_peers(picked)
    local = pl.pallas_call(
        level_body,
        out_shape=(jax.ShapeDtypeStruct((64, 1024), BF),) * 4,
        in_specs=[scalar] + [vmem] * 13,
        out_specs=(vmem,) * 4,
        scratch_shapes=(
            pltpu.VMEM((4, 128, 384), BF),
            pltpu.VMEM((4, 64, 1024), BF),
            pltpu.VMEM((2, 1024, 1024), BF),
            pltpu.VMEM((1024, 256), F32),
        ),
        compiler_params=pltpu.CompilerParams(vmem_limit_bytes=32 << 20),
        cost_estimate=pl.CostEstimate(flops=4 * 10**9, bytes_accessed=4 * 10**6, transcendentals=0),
    )(me, *picked, *ready)
    local = to_peers(local)
    out = call(
        spread_body,
        msg,
        (1,),
        [scalar] + [vmem] * 4,
        vmem,
        (pltpu.VMEM((4, 64, 1024), BF),),
        flops=4 * 10**8,
        moved=10**6,
    )(me, *local)
    out = to_nodes(out)
    out = call(place_body, msg, (1,), [vmem, vmem], vmem, flops=5 * 10**8, moved=10**6)(
        out, slots
    )
    out = to_nodes(out)
    coarse, grad_conv, grad_down, grad_bias = call(
        finish_body,
        (
            jax.ShapeDtypeStruct((32, 4096), BF),
            jax.ShapeDtypeStruct((16, 576), F32),
            jax.ShapeDtypeStruct((64, 64), F32),
            jax.ShapeDtypeStruct((1, 16), F32),
        ),
        (1,),
        [vmem],
        (
            whole((32, 4096)),
            whole((16, 576)),
            whole((64, 64)),
            whole((1, 16)),
        ),
        flops=4 * 10**8,
        moved=10**6,
    )(out)
    return (coarse.reshape(2, 16, 4096), grad_conv, grad_bias.reshape(16), grad_down)


def solution(mesh):
    in_specs = (
        P("tile", "chan", None),
        P("chan", None),
        P("chan"),
        P(None, "chan"),
        P("tile", "chan", None),
        P("tile", None),
        P("tile", None),
        P("tile", None),
        P("tile", None),
        P("tile"),
    )
    out_specs = (P("tile", "chan", None), P("chan", None), P("chan"), P(None, "chan"))
    return jax.shard_map(
        on_device, mesh=mesh, in_specs=in_specs, out_specs=out_specs, check_vma=False
    )
```

```python
import jax
import jax.numpy as jnp
from jax import lax
from jax.experimental import pallas as pl
from jax.experimental.pallas import tpu as pltpu
from jax.sharding import PartitionSpec as P

BF = jnp.bfloat16
F32 = jnp.float32
NODES = 64
MSG = (NODES * 8, 384)


def iota(shape, dim):
    return lax.broadcasted_iota(jnp.int32, shape, dim)


def down_col(n, start=0):
    return iota((n, 1), 0) + start


def lane_row(n):
    return iota((1, n), 1)


def ones_where(mask):
    return jnp.where(mask, 1.0, 0.0).astype(BF)


def keep(mask, x):
    return jnp.where(mask, x, 0.0).astype(BF)


def mm(a, b):
    return jnp.dot(a, b, preferred_element_type=F32)


def mm_nt(a, b):
    return lax.dot_general(a, b, (((1,), (1,)), ((), ())), preferred_element_type=F32)


def halves(x):
    high = x.astype(BF)
    return high, (x - high.astype(F32)).astype(BF)


def call(body, out_shape, grid, in_specs, out_specs, scratch=(), flops=0, moved=0):
    return pl.pallas_call(
        body,
        out_shape=out_shape,
        grid=grid,
        in_specs=in_specs,
        out_specs=out_specs,
        scratch_shapes=scratch,
        compiler_params=pltpu.CompilerParams(vmem_limit_bytes=48 << 20),
        cost_estimate=pl.CostEstimate(flops=flops, bytes_accessed=moved, transcendentals=0),
    )


def whole(shape):
    return pl.BlockSpec(shape, lambda *i: (0,) * len(shape))


def pack_weights(conv_ref, bias_ref, down_ref, raw_ref):
    zero = jnp.zeros((64, 64), BF)
    lane = lane_row(128)
    bias = jnp.where(lane_row(16) == down_col(16), bias_ref[...], 0.0)
    bias = jnp.sum(bias, axis=1, keepdims=True)
    b0 = bias.astype(BF).astype(F32)
    b1 = (bias - b0).astype(BF).astype(F32)
    b2 = (bias - b0) - b1
    bias = jnp.where(lane == 0, b0, jnp.where(lane == 1, b1, jnp.where(lane == 2, b2, 0.0))).astype(BF)
    raw_ref[:, 0:128] = jnp.concatenate([down_ref[...], zero], axis=1)
    raw_ref[0:16, 128:384] = conv_ref[:, 0:256]
    raw_ref[16:32, 128:384] = conv_ref[:, 256:512]
    raw_ref[32:48, 128:256] = jnp.concatenate([conv_ref[:, 512:576], zero[0:16]], axis=1)
    raw_ref[32:48, 256:384] = bias
    raw_ref[48:64, 128:384] = jnp.zeros((16, 256), BF)


def send_body(
    me_ref,
    all_ref,
    cot_ref,
    el_ref,
    et_ref,
    cl_ref,
    ct_ref,
    slot_ref,
    conv_ref,
    bias_ref,
    down_ref,
    out_ref,
    raw_ref,
    *more_refs,
):
    peer_refs, (feat_ref, sems) = more_refs[0:6], more_refs[6:]
    copies = [pltpu.make_async_copy(all_ref, feat_ref, sems.at[0])]
    for d in range(1, 4):
        peer = me_ref[0] ^ d
        first = all_ref.at[pl.ds(pl.multiple_of(peer * 32, 16), 16), :]
        second = all_ref.at[pl.ds(pl.multiple_of(peer * 32 + 16, 16), 16), :]
        copies.append(pltpu.make_async_copy(first, peer_refs[d - 1], sems.at[d]))
        copies.append(pltpu.make_async_copy(second, peer_refs[d + 2].at[:, 0:4096], sems.at[d + 3]))
    for copy in copies:
        copy.start()
    pack_weights(conv_ref, bias_ref, down_ref, raw_ref)
    cot = cot_ref[...]
    stack = jnp.concatenate([cot[:, q * 256 : q * 256 + 256] for q in range(16)], axis=0)
    row = down_col(512)
    k, g, a, qr, hf = row >> 5, (row >> 3) & 3, (row >> 2) & 1, (row >> 1) & 1, row & 1
    source = (qr << 8) | (g << 6) | (hf << 5) | (a << 4) | k
    out_ref[:, 0:256] = mm(ones_where(lane_row(512) == source), stack).astype(BF)

    copies[0].wait()
    first = feat_ref[:, 0:128]
    last = feat_ref[:, 3968:4096]
    p = down_col(64)
    lane = lane_row(128)
    rim_n = mm_nt(ones_where(lane == 63 - p), first)
    rim_s = mm_nt(ones_where(lane == 64 + p), last)
    pc = down_col(128)
    pos = pc & 63
    want = jnp.where(pc < 64, pos * 64, (63 - pos) * 64 + 63)
    rim_we = mm_nt(ones_where(lane_row(4096) == want), feat_ref[...])
    cr = down_col(16)
    at_first = jnp.where(cr == 0, 0, jnp.where(cr == 3, 63, -1))
    at_last = jnp.where(cr == 1, 64, jnp.where(cr == 2, 127, -1))
    corners = mm_nt(ones_where(lane == at_first), first) + mm_nt(ones_where(lane == at_last), last)
    tc = down_col(128)
    by_chan = jnp.zeros((16, 128), F32)
    for c in range(4):
        spread = jnp.broadcast_to(corners[c : c + 1, :], (16, 128))
        by_chan = by_chan + mm(keep((lane & 15) == cr, spread), ones_where(lane == (tc >> 4) * 4 + c))

    def over_lanes(x):
        rows = jnp.zeros((x.shape[0], 128), jnp.int32)
        for t in range(8):
            rows = jnp.where((lane & 7) == t, x[:, t : t + 1], rows)
        return rows

    def in_row(x, first_field):
        rows = over_lanes(x)
        side = iota(rows.shape, 0)
        mine = (iota(rows.shape, 1) >> 3) == side + first_field
        return jnp.sum(jnp.where(mine, rows, 0).astype(F32), axis=0, keepdims=True)

    side = iota((4, 8), 0)
    el, cl, slot = el_ref[...], cl_ref[...], slot_ref[...]
    edge = in_row(el >> 3, 0) + in_row((side + 2 + et_ref[...]) & 3, 4) + in_row(el & 7, 8)
    edge = edge + in_row(slot >> 3, 12) + in_row(slot & 7, 13)
    node = over_lanes(jnp.where(cl < 0, 127, cl >> 3)).astype(F32)
    pixel = over_lanes((cl & 7) * 4 + ((side + 2 + ct_ref[...]) & 3)).astype(F32)
    field = lane >> 3
    sub = down_col(16)
    small = jnp.where(sub == 0, edge, 0.0)
    for part in range(4):
        line = jnp.where(field == 14, node[part : part + 1, :], 0.0)
        line = jnp.where(field == 15, pixel[part : part + 1, :], line)
        small = small + jnp.where(sub == part + 1, line, 0.0)
    parts = [rim_n, rim_we[0:64], rim_s, rim_we[64:128], by_chan, small, jnp.zeros((96, 128), F32)]
    stack = jnp.concatenate([x.astype(BF) for x in parts], axis=0)
    r, node = row & 7, row >> 3
    source = jnp.where(r == 4, 256 + (node & 15), jnp.where(r == 5, 272, jnp.where(r == 6, 273 + (node >> 4), -1)))
    source = jnp.where(r < 4, r * 64 + node, source)
    out_ref[:, 256:384] = mm(ones_where(lane_row(384) == source), stack).astype(BF)
    for copy in copies[1:]:
        copy.wait()
    for d in range(1, 4):
        for q in range(4):
            peer_refs[d + 2][:, 4096 + q * 384 : 4480 + q * 384] = raw_ref[q * 16 : q * 16 + 16, :]


def pick_body(msg_ref, out_ref, slot_ref):
    cot = msg_ref[:, 0:256]
    misc = msg_ref[:, 256:384]
    col = lane_row(512)
    lane = lane_row(128)
    sub = down_col(512)
    near = down_col(128)
    base = (sub >> 3) << 3
    both = mm(ones_where((col == base + 5) | (col == base + 6)), misc)
    fields = mm(keep((lane & 7) == (sub & 7), both), ones_where((near >> 3) == lane))
    flip = fields.T
    slot_ref[...] = jnp.broadcast_to(flip[12:13, :] * 8.0 + flip[13:14, :], (8, 512))
    num = fields.astype(jnp.int32)

    def field(f):
        return num[:, f : f + 1]

    slot_row = field(12) * 8 + ((field(13) >> 1) << 1)
    lane2 = lane_row(256)
    fold_r = down_col(256)
    fold = ones_where(lane == (((fold_r >> 6) << 5) | (fold_r & 31)))
    mine = ((lane2 >> 5) & 1) == (field(13) & 1)
    for hf in range(2):
        got = mm(ones_where(col == slot_row + hf), cot)
        out_ref[:, hf * 128 : hf * 128 + 128] = mm(keep(mine, got), fold).astype(BF)
    total = jnp.zeros((512, 128), F32)
    for k in range(4):
        got = mm(ones_where(col == field(k) * 8 + field(4 + k)), misc)
        place = ones_where(lane == k * 16 + (near & 15))
        total = total + mm(keep((lane >> 4) == field(8 + k), got), place)
    got = mm(ones_where(col == field(14) * 8 + 4), misc)
    total = total + mm(keep(lane == field(15), got), ones_where(jnp.broadcast_to(lane == 64, (128, 128))))
    out_ref[:, 256:384] = total.astype(BF)


def regroup_body(me_ref, msg_ref, *out_refs):
    row = down_col(128)
    col = lane_row(512)
    lane = lane_row(128)
    pair, g, k, p = row >> 6, (row >> 4) & 3, row & 15, row & 63
    for d in range(4):
        out_ref = out_refs[d]
        tile = ((me_ref[0] ^ d) << 1) | pair
        out_ref[:, 0:256] = mm(ones_where(col == ((k << 5) | (g << 3) | tile)), msg_ref[:, 0:256]).astype(BF)
        got = mm(ones_where(col == ((p << 3) | tile)), msg_ref[:, 256:384])
        rims = jnp.where(lane < 64, got[0:64], pltpu.roll(got[64:128], 64, axis=1))
        pixels = jnp.zeros((16, 128), F32)
        for q in range(8):
            pixels = jnp.where(lane == q, got[q * 16 : q * 16 + 16, 64:65], pixels)
        rest = jnp.zeros((48, 128), F32)
        out_ref[:, 256:384] = jnp.concatenate([rims, pixels, rest], axis=0).astype(BF)


def lay_weights(raw_ref, w_ref, down_ref, down_t_ref, bias_ref):
    raw = jnp.concatenate(
        [
            jnp.concatenate([raw_ref[c, q * 16 : q * 16 + 16, 128 : 128 + n] for c in range(4)], axis=0)
            for q, n in ((0, 256), (1, 256), (2, 128))
        ],
        axis=1,
    )
    e = iota((640, 1), 0)
    i = (e * 7282) >> 16
    tap = e - i * 9
    dy = (tap * 86) >> 8
    to = jnp.where(e < 576, dy * 256 + (tap - dy * 3) * 64 + i, -9999)
    col = lane_row(1536)
    shifted = mm(raw, ones_where(jnp.where(col < 768, col, col - 832) == to)).astype(BF)
    zero = jnp.zeros((64, 256), BF)
    for a in range(2):
        for b in range(2):
            part = shifted[:, b * 768 : b * 768 + 768]
            row = (a * 2 + b) * 64
            w_ref[row : row + 64, :] = jnp.concatenate([zero, part] if a else [part, zero], axis=1)
    down = jnp.zeros((64, 256), F32)
    down_t = jnp.zeros((256, 64), F32)
    for c in range(4):
        mine = raw_ref[c, 0:64, 0:128]
        l = down_col(128)
        to = jnp.where(l < 64, (l & 3) * 64 + c * 16 + (l >> 2), -1)
        down = down + mm(mine, ones_where(lane_row(256) == to))
        l = lane_row(128)
        to = jnp.where(l < 64, (l & 3) * 64 + c * 16 + (l >> 2), -1)
        down_t = down_t + mm_nt(ones_where(down_col(256) == to), mine)
    down_ref[...] = down.astype(BF)
    down_t_ref[...] = down_t.astype(BF)
    bias = jnp.concatenate([raw_ref[c, 32:48, 256:259].astype(F32) for c in range(4)], axis=0)
    bias = (bias[:, 0:1] + bias[:, 1:2]) + bias[:, 2:3]
    bias_ref[...] = jnp.broadcast_to(jnp.concatenate([bias] * 4, axis=0), (256, 128))


def lay_places(side_ref, end_ref, conv_place_ref, down_place_ref):
    lane = lane_row(1024)
    v = lane & 31
    pos = down_col(64)
    for ry in range(4):
        y = ((lane >> 5) << 1) + (ry - 1)
        side_ref[ry, 0:64, :] = ones_where(jnp.where(v == 0, 63 - y, -1) == pos)
        side_ref[ry, 64:128, :] = ones_where(jnp.where(v == 31, y, -1) == pos)
    lane_e = lane_row(512)
    inner = lane_e & 127
    at = ((inner & 31) << 1) + (lane_e >> 7)
    end_ref[0:64, :] = ones_where(jnp.where(inner < 32, at - 1, -1) == pos)
    end_ref[64:128, :] = ones_where(jnp.where(inner >= 96, 64 - at, -1) == pos)
    kk = down_col(256)
    to = jnp.where(kk < 144, (kk & 15) * 9 + (kk >> 4), -1)
    conv_place_ref[...] = ones_where(lane_row(256) == to)
    kk = down_col(256)
    i, ab = kk & 63, kk >> 6
    down_place_ref[...] = ones_where(lane == ((i >> 4) << 8) + 144 + (i & 15) * 4 + ab)


def ready_body(me_ref, *refs):
    own_ref, own_raw_ref, first_refs, second_refs = refs[0], refs[1], refs[2:5], refs[5:8]
    win_ref, w_ref, down_ref, down_t_ref, bias_ref = refs[8:13]
    side_ref, end_ref, conv_place_ref, down_place_ref, x_ref, raw_ref = refs[13:]
    me = me_ref[0]
    lay_places(side_ref, end_ref, conv_place_ref, down_place_ref)
    raw_ref[me] = own_raw_ref[...]
    x_ref[me] = own_ref[...]
    for d in range(1, 4):
        second_ref = second_refs[d - 1]
        x_ref[me ^ d, 0:16, :] = first_refs[d - 1][...]
        x_ref[me ^ d, 16:32, :] = second_ref[:, 0:4096]
        for q in range(4):
            raw_ref[me ^ d, q * 16 : q * 16 + 16, :] = second_ref[:, 4096 + q * 384 : 4480 + q * 384]
    lay_weights(raw_ref, w_ref, down_ref, down_t_ref, bias_ref)
    l_in = down_col(512)
    to = (((l_in >> 6) & 1) << 8) | ((l_in & 1) << 7) | ((l_in >> 7) << 5) | ((l_in >> 1) & 31)
    order = ones_where(lane_row(512) == to)
    lane = lane_row(1024)
    v = lane & 31
    for t in range(2):
        x = jnp.concatenate([x_ref[c, t * 16 : t * 16 + 16, :] for c in range(4)], axis=0)
        stack = jnp.concatenate([x[:, q * 512 : q * 512 + 512] for q in range(8)], axis=0)
        split = mm(stack, order)
        cols = []
        for a in range(2):
            even, odd = [
                jnp.concatenate(
                    [split[q * 64 : q * 64 + 64, (a * 2 + b) * 128 : (a * 2 + b) * 128 + 128] for q in range(8)],
                    axis=1,
                )
                for b in range(2)
            ]
            cols.append(
                [
                    jnp.where(v == 0, 0.0, pltpu.roll(odd, 1, axis=1)),
                    even,
                    odd,
                    jnp.where(v == 31, 0.0, pltpu.roll(even, 1023, axis=1)),
                ]
            )
        for cx in range(4):
            top = jnp.where(lane < 32, 0.0, pltpu.roll(cols[1][cx], 32, axis=1))
            low = jnp.where(lane >= 992, 0.0, pltpu.roll(cols[0][cx], 992, axis=1))
            for ry, w in enumerate((top, cols[0][cx], cols[1][cx], low)):
                row = (ry * 4 + cx) * 64
                win_ref[t, row : row + 64, :] = w.astype(BF)


def level_body(me_ref, *refs):
    in_refs, (base_ref, w_ref, down_ref, down_t_ref, bias_ref) = refs[0:4], refs[4:9]
    side_ref, end_ref, conv_place_ref, down_place_ref = refs[9:13]
    out_refs, (msg_ref, sum_ref, win_ref, gc_ref) = refs[13:17], refs[17:]
    me = me_ref[0]
    for d in range(4):
        msg_ref[me ^ d] = in_refs[d][...]
    flip = [msg_ref[c, 0:64, 256:384].astype(F32).T.astype(BF) for c in range(4)]

    def strip(k):
        return jnp.concatenate(
            [f[t * 64 + k * 16 : t * 64 + k * 16 + 16, :] for t in range(2) for f in flip], axis=0
        )

    pixels = jnp.concatenate([msg_ref[c, 64:80, 256:384] for c in range(4)], axis=0).astype(F32)
    sides = {}
    v = lane_row(1024) & 31
    west_east = jnp.concatenate([strip(1), strip(3)], axis=1)
    for ry in range(4):
        both = mm(west_east, side_ref[ry])
        sides[ry, 0] = keep(v == 0, both)
        sides[ry, 3] = keep(v == 31, both)
    lane_e = lane_row(512)
    ends = mm(jnp.concatenate([strip(0), strip(2)], axis=1), end_ref[...])
    gd = jnp.zeros((64, 256), F32)
    gb = jnp.zeros((256, 1), F32)
    for t in range(2):
        end = ends[t * 64 : t * 64 + 64, :]
        for spot, k in ((0, 0), (96, 1), (384 + 31, 3), (384 + 127, 2)):
            end = jnp.where(lane_e == spot, pixels[:, t * 4 + k : t * 4 + k + 1], end)
        for ry in range(4):
            for cx in range(4):
                row = (ry * 4 + cx) * 64
                w = base_ref[t, row : row + 64, :]
                if (ry, cx) in sides:
                    w = w + sides[ry, cx][t * 64 : t * 64 + 64, :]
                win_ref[t, row : row + 64, :] = w
                edge = end[:, cx * 128 : cx * 128 + 128]
                if ry == 0:
                    fix = jnp.where(lane_row(128) < 64, edge, 0.0).astype(BF)
                    win_ref[t, row : row + 64, 0:128] = w[:, 0:128] + fix
                if ry == 3:
                    fix = jnp.where(lane_row(128) >= 64, edge, 0.0).astype(BF)
                    win_ref[t, row : row + 64, 896:1024] = w[:, 896:1024] + fix
    for t in range(2):
        pre = mm(w_ref[...], win_ref[t]) + bias_ref[:, 0:1]
        sig = 1.0 / (1.0 + jnp.exp(-pre))
        hidden = (pre * sig).astype(BF)
        quarter = mm(down_ref[...], hidden).astype(BF)
        for c in range(4):
            sum_ref[c, t * 16 : t * 16 + 16, :] = quarter[c * 16 : c * 16 + 16, :]
        back = jnp.concatenate(
            [
                jnp.concatenate(
                    [msg_ref[c, t * 64 + g * 16 : t * 64 + g * 16 + 16, 0:256] for c in range(4)], axis=0
                )
                for g in range(4)
            ],
            axis=1,
        )
        grad_hidden = mm(down_t_ref[...], back)
        grad_pre = (grad_hidden * (sig * (1.0 + pre * (1.0 - sig)))).astype(BF)
        gb = gb + jnp.sum(grad_pre.astype(F32), axis=1, keepdims=True)
        gd = gd + mm_nt(back, hidden)
        part = mm_nt(win_ref[t], grad_pre)
        gc_ref[...] = part if t == 0 else gc_ref[...] + part
    rows = []
    for dy in range(3):
        for cx in range(4):
            r0, r1 = (dy * 4 + cx) * 64, ((dy + 1) * 4 + cx) * 64
            rows.append(gc_ref[r0 : r0 + 64, 0:128] + gc_ref[r1 : r1 + 64, 128:256])
    taps = []
    for dy in range(3):
        for dx in range(3):
            taps.append(rows[dy * 4 + dx] + pltpu.roll(rows[dy * 4 + dx + 1], 64, axis=1))
    groups = []
    for q in range(4):
        rows = jnp.concatenate(
            [tap[q * 16 : q * 16 + 16, :] for tap in taps] + [jnp.zeros((112, 128), F32)], axis=0
        )
        groups.append(jnp.concatenate([rows[0:128].T, rows[128:256].T], axis=1)[0:64, :])
    conv = mm(jnp.concatenate(halves(jnp.concatenate(groups, axis=0)), axis=0), conv_place_ref[...])
    down = mm(jnp.concatenate(halves(gd), axis=0), down_place_ref[...])
    gb = gb[0:64, :] + gb[64:128, :] + gb[128:192, :] + gb[192:256, :]
    bias = [h.astype(F32) for h in halves(gb)]
    lane16 = lane_row(1024)
    for part in range(2):
        for c in range(4):
            both = jnp.concatenate(
                [
                    conv[part * 256 + q * 64 + c * 16 : part * 256 + q * 64 + c * 16 + 16, :]
                    + down[part * 64 + q * 16 : part * 64 + q * 16 + 16, c * 256 : c * 256 + 256]
                    for q in range(4)
                ],
                axis=1,
            )
            both = jnp.where(lane16 == 208, bias[part][c * 16 : c * 16 + 16, :], both)
            sum_ref[c, 32 + part * 16 : 48 + part * 16, :] = both.astype(BF)
    for d in range(4):
        out_refs[d][...] = sum_ref[me ^ d]


def spread_body(me_ref, *refs):
    in_refs, out_ref, msg_ref = refs[0:4], refs[4], refs[5]
    for d in range(4):
        msg_ref[me_ref[0] ^ d] = in_refs[d][...]
    stack = jnp.concatenate(
        [msg_ref[c, 0:32, g * 256 : g * 256 + 256] for g in range(4) for c in range(4)], axis=0
    )
    row = down_col(512)
    source = (((row >> 3) & 3) << 7) | (((row >> 1) & 3) << 5) | ((row & 1) << 4) | (row >> 5)
    out_ref[:, 0:256] = mm(ones_where(lane_row(512) == source), stack).astype(BF)
    total = jnp.zeros((16, 1024), F32)
    for c in range(4):
        total = total + (msg_ref[c, 32:48, :].astype(F32) + msg_ref[c, 48:64, :].astype(F32))
    parts = [
        h[:, s * 256 + o : s * 256 + o + 128] for h in halves(total) for o in (0, 128) for s in range(4)
    ]
    stack = jnp.concatenate(parts, axis=0)
    r, p = row & 7, row >> 3
    source = jnp.where(r < 4, (r << 6) + p, -1)
    out_ref[:, 256:384] = mm(ones_where(lane_row(256) == source), stack).astype(BF)


def place_body(msg_ref, slot_ref, out_ref):
    quarter = msg_ref[:, 0:256]
    slot = slot_ref[0:1, :].astype(jnp.int32)
    row = down_col(512)
    lane = lane_row(256)
    half = row & 1
    li = down_col(256)
    to = (((li >> 5) & 3) << 6) | (li & 31)
    total = jnp.zeros((512, 256), F32)
    for qc in range(2):
        got = mm(ones_where(slot == ((row >> 1) << 1) + qc), quarter)
        total = total + mm(keep((lane >> 7) == half, got), ones_where(lane == to + qc * 32))
    out_ref[:, 0:256] = total.astype(BF)
    r = down_col(16)
    src = lane_row(512) & 7
    src = jnp.where(src < 4, src & 1, -1)
    summed = mm(ones_where(src == jnp.where(r < 4, r & 1, -2)), msg_ref[:, 256:384])
    high, low = halves(summed)
    both = jnp.where(iota((16, 128), 0) < 2, high.astype(F32), low.astype(F32)).astype(BF)
    r = row & 7
    out_ref[:, 256:384] = mm(ones_where(lane_row(16) == jnp.where(r < 4, r, -1)), both).astype(BF)


def finish_body(msg_ref, coarse_ref, conv_ref, down_ref, bias_ref):
    row = down_col(512)
    col = lane_row(512)
    qr, g, hf, a, k = row >> 8, (row >> 6) & 3, (row >> 5) & 1, (row >> 4) & 1, row & 15
    source = (k << 5) | (g << 3) | (a << 2) | (qr << 1) | hf
    got = mm(ones_where(col == source), msg_ref[:, 0:256]).astype(BF)
    for q in range(16):
        coarse_ref[:, q * 256 : q * 256 + 256] = got[q * 32 : q * 32 + 32, :]

    row = down_col(256)
    got = mm(ones_where(col == ((row & 63) << 3) + (row >> 6)), msg_ref[:, 256:384])
    value = jnp.concatenate([got[0:64] + got[128:192], got[64:128] + got[192:256]], axis=1)
    head = jnp.where(lane_row(256) < 144, value, 0.0)
    pad = jnp.zeros((16, 384), F32)
    conv = jnp.zeros((16, 640), F32)
    for q in range(4):
        part = jnp.concatenate([head[q * 16 : q * 16 + 16, :], pad], axis=1)
        conv = conv + (pltpu.roll(part, q * 144, axis=1) if q else part)
    conv_ref[...] = conv[:, 0:576]
    down_ref[...] = pltpu.roll(value, 112, axis=1)[:, 0:64]
    bias = value[0:16, 208:209]
    bias_ref[...] = jnp.sum(jnp.where(lane_row(16) == down_col(16), bias, 0.0), axis=0, keepdims=True)


def to_peers(parts):
    return [parts[0]] + [
        lax.ppermute(parts[d], "chan", [(i, i ^ d) for i in range(4)]) for d in range(1, 4)
    ]


def on_device(
    features,
    conv_weight,
    conv_bias,
    down_weight,
    cotangent,
    edge_links,
    edge_turns,
    corner_links,
    corner_turns,
    child_slot,
):
    vmem = pl.BlockSpec(memory_space=pltpu.VMEM)
    msg = jax.ShapeDtypeStruct(MSG, BF)

    def to_nodes(x):
        return lax.all_to_all(x.reshape(64, 8, 384), "tile", 0, 0, tiled=True).reshape(MSG)

    me = lax.axis_index("chan").astype(jnp.int32).reshape(1)
    scalar = pl.BlockSpec(memory_space=pltpu.SMEM)
    first = jax.ShapeDtypeStruct((16, 4096), BF)
    second = jax.ShapeDtypeStruct((16, 5632), BF)
    pieces, raw, *peers = call(
        send_body,
        (msg, jax.ShapeDtypeStruct((64, 384), BF)) + (first,) * 3 + (second,) * 3,
        (1,),
        [scalar, pl.BlockSpec(memory_space=pl.ANY), whole((32, 4096))]
        + [whole((4, 8))] * 4
        + [whole((1, 8)), whole((16, 576)), whole((1, 16)), whole((64, 64))],
        (vmem,) * 8,
        (pltpu.VMEM((128, 4096), BF), pltpu.SemaphoreType.DMA((7,))),
        flops=10**9,
        moved=2 * 10**6,
    )(
        me,
        *[
            pltpu.with_memory_space_constraint(x, pltpu.HBM)
            for x in (
                features.reshape(128, 4096),
                cotangent.reshape(32, 4096),
                edge_links.T,
                edge_turns.T,
                corner_links.T,
                corner_turns.T,
                child_slot.reshape(1, 8),
                conv_weight,
                conv_bias.reshape(1, 16),
                down_weight,
            )
        ],
    )
    first = to_peers([None] + peers[0:3])[1:]
    second = to_peers([None] + peers[3:6])[1:]
    pieces, first = lax.optimization_barrier((to_nodes(pieces), first))
    picked, slots = call(
        pick_body,
        (msg, jax.ShapeDtypeStruct((8, 512), F32)),
        (1,),
        [vmem],
        (vmem, vmem),
        flops=10**9,
        moved=10**6,
    )(pieces)
    picked = to_nodes(picked)
    own = pl.BlockSpec((32, 4096), lambda i, m: (m[0], 0))
    ready = pl.pallas_call(
        ready_body,
        out_shape=(
            jax.ShapeDtypeStruct((2, 1024, 1024), BF),
            jax.ShapeDtypeStruct((256, 1024), BF),
            jax.ShapeDtypeStruct((64, 256), BF),
            jax.ShapeDtypeStruct((256, 64), BF),
            jax.ShapeDtypeStruct((256, 128), F32),
            jax.ShapeDtypeStruct((4, 128, 1024), BF),
            jax.ShapeDtypeStruct((128, 512), BF),
            jax.ShapeDtypeStruct((256, 256), BF),
            jax.ShapeDtypeStruct((256, 1024), BF),
        ),
        grid_spec=pltpu.PrefetchScalarGridSpec(
            num_scalar_prefetch=1,
            grid=(1,),
            in_specs=[own] + [vmem] * 7,
            out_specs=(vmem,) * 9,
            scratch_shapes=(pltpu.VMEM((4, 32, 4096), BF), pltpu.VMEM((4, 64, 384), BF)),
        ),
        compiler_params=pltpu.CompilerParams(vmem_limit_bytes=32 << 20),
        cost_estimate=pl.CostEstimate(flops=10**9, bytes_accessed=4 * 10**6, transcendentals=0),
    )(me, features.reshape(128, 4096), raw, *first, *second)
    group = jax.ShapeDtypeStruct((128, 384), BF)
    picked = call(
        regroup_body,
        (group,) * 4,
        (1,),
        [scalar, vmem],
        (vmem,) * 4,
        flops=4 * 10**8,
        moved=10**6,
    )(me, picked)
    picked = to_peers(picked)
    local = pl.pallas_call(
        level_body,
        out_shape=(jax.ShapeDtypeStruct((64, 1024), BF),) * 4,
        in_specs=[scalar] + [vmem] * 13,
        out_specs=(vmem,) * 4,
        scratch_shapes=(
            pltpu.VMEM((4, 128, 384), BF),
            pltpu.VMEM((4, 64, 1024), BF),
            pltpu.VMEM((2, 1024, 1024), BF),
            pltpu.VMEM((1024, 256), F32),
        ),
        compiler_params=pltpu.CompilerParams(vmem_limit_bytes=32 << 20),
        cost_estimate=pl.CostEstimate(flops=4 * 10**9, bytes_accessed=4 * 10**6, transcendentals=0),
    )(me, *picked, *ready)
    local = to_peers(local)
    out = call(
        spread_body,
        msg,
        (1,),
        [scalar] + [vmem] * 4,
        vmem,
        (pltpu.VMEM((4, 64, 1024), BF),),
        flops=4 * 10**8,
        moved=10**6,
    )(me, *local)
    out = to_nodes(out)
    out = call(place_body, msg, (1,), [vmem, vmem], vmem, flops=5 * 10**8, moved=10**6)(
        out, slots
    )
    out = to_nodes(out)
    coarse, grad_conv, grad_down, grad_bias = call(
        finish_body,
        (
            jax.ShapeDtypeStruct((32, 4096), BF),
            jax.ShapeDtypeStruct((16, 576), F32),
            jax.ShapeDtypeStruct((64, 64), F32),
            jax.ShapeDtypeStruct((1, 16), F32),
        ),
        (1,),
        [vmem],
        (
            whole((32, 4096)),
            whole((16, 576)),
            whole((64, 64)),
            whole((1, 16)),
        ),
        flops=4 * 10**8,
        moved=10**6,
    )(out)
    return (coarse.reshape(2, 16, 4096), grad_conv, grad_bias.reshape(16), grad_down)


def solution(mesh):
    in_specs = (
        P("tile", "chan", None),
        P("chan", None),
        P("chan"),
        P(None, "chan"),
        P("tile", "chan", None),
        P("tile", None),
        P("tile", None),
        P("tile", None),
        P("tile", None),
        P("tile"),
    )
    out_specs = (P("tile", "chan", None), P("chan", None), P("chan"), P(None, "chan"))
    return jax.shard_map(
        on_device, mesh=mesh, in_specs=in_specs, out_specs=out_specs, check_vma=False
    )
```

```python
import jax
import jax.numpy as jnp
from jax import lax
from jax.experimental import pallas as pl
from jax.experimental.pallas import tpu as pltpu
from jax.sharding import PartitionSpec as P

BF = jnp.bfloat16
F32 = jnp.float32
NODES = 64
MSG = (NODES * 8, 384)


def iota(shape, dim):
    return lax.broadcasted_iota(jnp.int32, shape, dim)


def down_col(n, start=0):
    return iota((n, 1), 0) + start


def lane_row(n):
    return iota((1, n), 1)


def ones_where(mask):
    return jnp.where(mask, 1.0, 0.0).astype(BF)


def keep(mask, x):
    return jnp.where(mask, x, 0.0).astype(BF)


def mm(a, b):
    return jnp.dot(a, b, preferred_element_type=F32)


def mm_nt(a, b):
    return lax.dot_general(a, b, (((1,), (1,)), ((), ())), preferred_element_type=F32)


def halves(x):
    high = x.astype(BF)
    return high, (x - high.astype(F32)).astype(BF)


def call(body, out_shape, grid, in_specs, out_specs, scratch=(), flops=0, moved=0):
    return pl.pallas_call(
        body,
        out_shape=out_shape,
        grid=grid,
        in_specs=in_specs,
        out_specs=out_specs,
        scratch_shapes=scratch,
        compiler_params=pltpu.CompilerParams(vmem_limit_bytes=48 << 20),
        cost_estimate=pl.CostEstimate(flops=flops, bytes_accessed=moved, transcendentals=0),
    )


def whole(shape):
    return pl.BlockSpec(shape, lambda *i: (0,) * len(shape))


def pack_weights(conv_ref, bias_ref, down_ref, raw_ref):
    zero = jnp.zeros((64, 64), BF)
    lane = lane_row(128)
    bias = jnp.where(lane_row(16) == down_col(16), bias_ref[...], 0.0)
    bias = jnp.sum(bias, axis=1, keepdims=True)
    b0 = bias.astype(BF).astype(F32)
    b1 = (bias - b0).astype(BF).astype(F32)
    b2 = (bias - b0) - b1
    bias = jnp.where(lane == 0, b0, jnp.where(lane == 1, b1, jnp.where(lane == 2, b2, 0.0))).astype(BF)
    raw_ref[:, 0:128] = jnp.concatenate([down_ref[...], zero], axis=1)
    raw_ref[0:16, 128:384] = conv_ref[:, 0:256]
    raw_ref[16:32, 128:384] = conv_ref[:, 256:512]
    raw_ref[32:48, 128:256] = jnp.concatenate([conv_ref[:, 512:576], zero[0:16]], axis=1)
    raw_ref[32:48, 256:384] = bias
    raw_ref[48:64, 128:384] = jnp.zeros((16, 256), BF)


def send_body(
    me_ref,
    all_ref,
    cot_ref,
    el_ref,
    et_ref,
    cl_ref,
    ct_ref,
    slot_ref,
    conv_ref,
    bias_ref,
    down_ref,
    out_ref,
    raw_ref,
    *more_refs,
):
    peer_refs, (feat_ref, sems) = more_refs[0:6], more_refs[6:]
    copy = pltpu.make_async_copy(all_ref, feat_ref, sems.at[0])
    copy.start()
    pack_weights(conv_ref, bias_ref, down_ref, raw_ref)
    cot = cot_ref[...]
    stack = jnp.concatenate([cot[:, q * 256 : q * 256 + 256] for q in range(16)], axis=0)
    row = down_col(512)
    k, g, a, qr, hf = row >> 5, (row >> 3) & 3, (row >> 2) & 1, (row >> 1) & 1, row & 1
    source = (qr << 8) | (g << 6) | (hf << 5) | (a << 4) | k
    out_ref[:, 0:256] = mm(ones_where(lane_row(512) == source), stack).astype(BF)

    copy.wait()
    for d in range(1, 4):
        peer = me_ref[0] ^ d
        first_ref, second_ref = peer_refs[d - 1], peer_refs[d + 2]
        first_ref[...] = feat_ref[pl.ds(pl.multiple_of(peer * 32, 16), 16), :]
        second_ref[:, 0:4096] = feat_ref[pl.ds(pl.multiple_of(peer * 32 + 16, 16), 16), :]
        for q in range(4):
            second_ref[:, 4096 + q * 384 : 4480 + q * 384] = raw_ref[q * 16 : q * 16 + 16, :]
    first = feat_ref[:, 0:128]
    last = feat_ref[:, 3968:4096]
    p = down_col(64)
    lane = lane_row(128)
    rim_n = mm_nt(ones_where(lane == 63 - p), first)
    rim_s = mm_nt(ones_where(lane == 64 + p), last)
    pc = down_col(128)
    pos = pc & 63
    want = jnp.where(pc < 64, pos * 64, (63 - pos) * 64 + 63)
    rim_we = mm_nt(ones_where(lane_row(4096) == want), feat_ref[...])
    cr = down_col(16)
    at_first = jnp.where(cr == 0, 0, jnp.where(cr == 3, 63, -1))
    at_last = jnp.where(cr == 1, 64, jnp.where(cr == 2, 127, -1))
    corners = mm_nt(ones_where(lane == at_first), first) + mm_nt(ones_where(lane == at_last), last)
    tc = down_col(128)
    by_chan = jnp.zeros((16, 128), F32)
    for c in range(4):
        spread = jnp.broadcast_to(corners[c : c + 1, :], (16, 128))
        by_chan = by_chan + mm(keep((lane & 15) == cr, spread), ones_where(lane == (tc >> 4) * 4 + c))

    def over_lanes(x):
        rows = jnp.zeros((x.shape[0], 128), jnp.int32)
        for t in range(8):
            rows = jnp.where((lane & 7) == t, x[:, t : t + 1], rows)
        return rows

    def in_row(x, first_field):
        rows = over_lanes(x)
        side = iota(rows.shape, 0)
        mine = (iota(rows.shape, 1) >> 3) == side + first_field
        return jnp.sum(jnp.where(mine, rows, 0).astype(F32), axis=0, keepdims=True)

    side = iota((4, 8), 0)
    el, cl, slot = el_ref[...], cl_ref[...], slot_ref[...]
    edge = in_row(el >> 3, 0) + in_row((side + 2 + et_ref[...]) & 3, 4) + in_row(el & 7, 8)
    edge = edge + in_row(slot >> 3, 12) + in_row(slot & 7, 13)
    node = over_lanes(jnp.where(cl < 0, 127, cl >> 3)).astype(F32)
    pixel = over_lanes((cl & 7) * 4 + ((side + 2 + ct_ref[...]) & 3)).astype(F32)
    field = lane >> 3
    sub = down_col(16)
    small = jnp.where(sub == 0, edge, 0.0)
    for part in range(4):
        line = jnp.where(field == 14, node[part : part + 1, :], 0.0)
        line = jnp.where(field == 15, pixel[part : part + 1, :], line)
        small = small + jnp.where(sub == part + 1, line, 0.0)
    parts = [rim_n, rim_we[0:64], rim_s, rim_we[64:128], by_chan, small, jnp.zeros((96, 128), F32)]
    stack = jnp.concatenate([x.astype(BF) for x in parts], axis=0)
    r, node = row & 7, row >> 3
    source = jnp.where(r == 4, 256 + (node & 15), jnp.where(r == 5, 272, jnp.where(r == 6, 273 + (node >> 4), -1)))
    source = jnp.where(r < 4, r * 64 + node, source)
    out_ref[:, 256:384] = mm(ones_where(lane_row(384) == source), stack).astype(BF)


def pick_body(msg_ref, out_ref, slot_ref):
    cot = msg_ref[:, 0:256]
    misc = msg_ref[:, 256:384]
    col = lane_row(512)
    lane = lane_row(128)
    sub = down_col(512)
    near = down_col(128)
    base = (sub >> 3) << 3
    both = mm(ones_where((col == base + 5) | (col == base + 6)), misc)
    fields = mm(keep((lane & 7) == (sub & 7), both), ones_where((near >> 3) == lane))
    flip = fields.T
    slot_ref[...] = jnp.broadcast_to(flip[12:13, :] * 8.0 + flip[13:14, :], (8, 512))
    num = fields.astype(jnp.int32)

    def field(f):
        return num[:, f : f + 1]

    slot_row = field(12) * 8 + ((field(13) >> 1) << 1)
    lane2 = lane_row(256)
    fold_r = down_col(256)
    fold = ones_where(lane == (((fold_r >> 6) << 5) | (fold_r & 31)))
    mine = ((lane2 >> 5) & 1) == (field(13) & 1)
    for hf in range(2):
        got = mm(ones_where(col == slot_row + hf), cot)
        out_ref[:, hf * 128 : hf * 128 + 128] = mm(keep(mine, got), fold).astype(BF)
    total = jnp.zeros((512, 128), F32)
    for k in range(4):
        got = mm(ones_where(col == field(k) * 8 + field(4 + k)), misc)
        place = ones_where(lane == k * 16 + (near & 15))
        total = total + mm(keep((lane >> 4) == field(8 + k), got), place)
    got = mm(ones_where(col == field(14) * 8 + 4), misc)
    total = total + mm(keep(lane == field(15), got), ones_where(jnp.broadcast_to(lane == 64, (128, 128))))
    out_ref[:, 256:384] = total.astype(BF)


def regroup_body(me_ref, msg_ref, *out_refs):
    row = down_col(128)
    col = lane_row(512)
    lane = lane_row(128)
    pair, g, k, p = row >> 6, (row >> 4) & 3, row & 15, row & 63
    for d in range(4):
        out_ref = out_refs[d]
        tile = ((me_ref[0] ^ d) << 1) | pair
        out_ref[:, 0:256] = mm(ones_where(col == ((k << 5) | (g << 3) | tile)), msg_ref[:, 0:256]).astype(BF)
        got = mm(ones_where(col == ((p << 3) | tile)), msg_ref[:, 256:384])
        rims = jnp.where(lane < 64, got[0:64], pltpu.roll(got[64:128], 64, axis=1))
        pixels = jnp.zeros((16, 128), F32)
        for q in range(8):
            pixels = jnp.where(lane == q, got[q * 16 : q * 16 + 16, 64:65], pixels)
        rest = jnp.zeros((48, 128), F32)
        out_ref[:, 256:384] = jnp.concatenate([rims, pixels, rest], axis=0).astype(BF)


def lay_weights(raw_ref, w_ref, down_ref, down_t_ref, bias_ref):
    raw = jnp.concatenate(
        [
            jnp.concatenate([raw_ref[c, q * 16 : q * 16 + 16, 128 : 128 + n] for c in range(4)], axis=0)
            for q, n in ((0, 256), (1, 256), (2, 128))
        ],
        axis=1,
    )
    e = iota((640, 1), 0)
    i = (e * 7282) >> 16
    tap = e - i * 9
    dy = (tap * 86) >> 8
    to = jnp.where(e < 576, dy * 256 + (tap - dy * 3) * 64 + i, -9999)
    col = lane_row(1536)
    shifted = mm(raw, ones_where(jnp.where(col < 768, col, col - 832) == to)).astype(BF)
    zero = jnp.zeros((64, 256), BF)
    for a in range(2):
        for b in range(2):
            part = shifted[:, b * 768 : b * 768 + 768]
            row = (a * 2 + b) * 64
            w_ref[row : row + 64, :] = jnp.concatenate([zero, part] if a else [part, zero], axis=1)
    down = jnp.zeros((64, 256), F32)
    down_t = jnp.zeros((256, 64), F32)
    for c in range(4):
        mine = raw_ref[c, 0:64, 0:128]
        l = down_col(128)
        to = jnp.where(l < 64, (l & 3) * 64 + c * 16 + (l >> 2), -1)
        down = down + mm(mine, ones_where(lane_row(256) == to))
        l = lane_row(128)
        to = jnp.where(l < 64, (l & 3) * 64 + c * 16 + (l >> 2), -1)
        down_t = down_t + mm_nt(ones_where(down_col(256) == to), mine)
    down_ref[...] = down.astype(BF)
    down_t_ref[...] = down_t.astype(BF)
    bias = jnp.concatenate([raw_ref[c, 32:48, 256:259].astype(F32) for c in range(4)], axis=0)
    bias = (bias[:, 0:1] + bias[:, 1:2]) + bias[:, 2:3]
    bias_ref[...] = jnp.broadcast_to(jnp.concatenate([bias] * 4, axis=0), (256, 128))


def lay_places(side_ref, end_ref, conv_place_ref, down_place_ref):
    lane = lane_row(1024)
    v = lane & 31
    pos = down_col(64)
    for ry in range(4):
        y = ((lane >> 5) << 1) + (ry - 1)
        side_ref[ry, 0:64, :] = ones_where(jnp.where(v == 0, 63 - y, -1) == pos)
        side_ref[ry, 64:128, :] = ones_where(jnp.where(v == 31, y, -1) == pos)
    lane_e = lane_row(512)
    inner = lane_e & 127
    at = ((inner & 31) << 1) + (lane_e >> 7)
    end_ref[0:64, :] = ones_where(jnp.where(inner < 32, at - 1, -1) == pos)
    end_ref[64:128, :] = ones_where(jnp.where(inner >= 96, 64 - at, -1) == pos)
    kk = down_col(256)
    to = jnp.where(kk < 144, (kk & 15) * 9 + (kk >> 4), -1)
    conv_place_ref[...] = ones_where(lane_row(256) == to)
    kk = down_col(256)
    i, ab = kk & 63, kk >> 6
    down_place_ref[...] = ones_where(lane == ((i >> 4) << 8) + 144 + (i & 15) * 4 + ab)


def ready_body(me_ref, *refs):
    own_ref, own_raw_ref, first_refs, second_refs = refs[0], refs[1], refs[2:5], refs[5:8]
    win_ref, w_ref, down_ref, down_t_ref, bias_ref = refs[8:13]
    side_ref, end_ref, conv_place_ref, down_place_ref, x_ref, raw_ref = refs[13:]
    me = me_ref[0]
    lay_places(side_ref, end_ref, conv_place_ref, down_place_ref)
    raw_ref[me] = own_raw_ref[...]
    x_ref[me] = own_ref[...]
    for d in range(1, 4):
        second_ref = second_refs[d - 1]
        x_ref[me ^ d, 0:16, :] = first_refs[d - 1][...]
        x_ref[me ^ d, 16:32, :] = second_ref[:, 0:4096]
        for q in range(4):
            raw_ref[me ^ d, q * 16 : q * 16 + 16, :] = second_ref[:, 4096 + q * 384 : 4480 + q * 384]
    lay_weights(raw_ref, w_ref, down_ref, down_t_ref, bias_ref)
    l_in = down_col(512)
    to = (((l_in >> 6) & 1) << 8) | ((l_in & 1) << 7) | ((l_in >> 7) << 5) | ((l_in >> 1) & 31)
    order = ones_where(lane_row(512) == to)
    lane = lane_row(1024)
    v = lane & 31
    for t in range(2):
        x = jnp.concatenate([x_ref[c, t * 16 : t * 16 + 16, :] for c in range(4)], axis=0)
        stack = jnp.concatenate([x[:, q * 512 : q * 512 + 512] for q in range(8)], axis=0)
        split = mm(stack, order)
        cols = []
        for a in range(2):
            even, odd = [
                jnp.concatenate(
                    [split[q * 64 : q * 64 + 64, (a * 2 + b) * 128 : (a * 2 + b) * 128 + 128] for q in range(8)],
                    axis=1,
                )
                for b in range(2)
            ]
            cols.append(
                [
                    jnp.where(v == 0, 0.0, pltpu.roll(odd, 1, axis=1)),
                    even,
                    odd,
                    jnp.where(v == 31, 0.0, pltpu.roll(even, 1023, axis=1)),
                ]
            )
        for cx in range(4):
            top = jnp.where(lane < 32, 0.0, pltpu.roll(cols[1][cx], 32, axis=1))
            low = jnp.where(lane >= 992, 0.0, pltpu.roll(cols[0][cx], 992, axis=1))
            for ry, w in enumerate((top, cols[0][cx], cols[1][cx], low)):
                row = (ry * 4 + cx) * 64
                win_ref[t, row : row + 64, :] = w.astype(BF)


def level_body(me_ref, *refs):
    in_refs, (base_ref, w_ref, down_ref, down_t_ref, bias_ref) = refs[0:4], refs[4:9]
    side_ref, end_ref, conv_place_ref, down_place_ref = refs[9:13]
    out_refs, (msg_ref, sum_ref, win_ref, gc_ref) = refs[13:17], refs[17:]
    me = me_ref[0]
    for d in range(4):
        msg_ref[me ^ d] = in_refs[d][...]
    flip = [msg_ref[c, 0:64, 256:384].astype(F32).T.astype(BF) for c in range(4)]

    def strip(k):
        return jnp.concatenate(
            [f[t * 64 + k * 16 : t * 64 + k * 16 + 16, :] for t in range(2) for f in flip], axis=0
        )

    pixels = jnp.concatenate([msg_ref[c, 64:80, 256:384] for c in range(4)], axis=0).astype(F32)
    sides = {}
    v = lane_row(1024) & 31
    west_east = jnp.concatenate([strip(1), strip(3)], axis=1)
    for ry in range(4):
        both = mm(west_east, side_ref[ry])
        sides[ry, 0] = keep(v == 0, both)
        sides[ry, 3] = keep(v == 31, both)
    lane_e = lane_row(512)
    ends = mm(jnp.concatenate([strip(0), strip(2)], axis=1), end_ref[...])
    gd = jnp.zeros((64, 256), F32)
    gb = jnp.zeros((256, 1), F32)
    for t in range(2):
        end = ends[t * 64 : t * 64 + 64, :]
        for spot, k in ((0, 0), (96, 1), (384 + 31, 3), (384 + 127, 2)):
            end = jnp.where(lane_e == spot, pixels[:, t * 4 + k : t * 4 + k + 1], end)
        for ry in range(4):
            for cx in range(4):
                row = (ry * 4 + cx) * 64
                w = base_ref[t, row : row + 64, :]
                if (ry, cx) in sides:
                    w = w + sides[ry, cx][t * 64 : t * 64 + 64, :]
                win_ref[t, row : row + 64, :] = w
                edge = end[:, cx * 128 : cx * 128 + 128]
                if ry == 0:
                    fix = jnp.where(lane_row(128) < 64, edge, 0.0).astype(BF)
                    win_ref[t, row : row + 64, 0:128] = w[:, 0:128] + fix
                if ry == 3:
                    fix = jnp.where(lane_row(128) >= 64, edge, 0.0).astype(BF)
                    win_ref[t, row : row + 64, 896:1024] = w[:, 896:1024] + fix
    for t in range(2):
        pre = mm(w_ref[...], win_ref[t]) + bias_ref[:, 0:1]
        sig = 1.0 / (1.0 + jnp.exp(-pre))
        hidden = (pre * sig).astype(BF)
        quarter = mm(down_ref[...], hidden).astype(BF)
        for c in range(4):
            sum_ref[c, t * 16 : t * 16 + 16, :] = quarter[c * 16 : c * 16 + 16, :]
        back = jnp.concatenate(
            [
                jnp.concatenate(
                    [msg_ref[c, t * 64 + g * 16 : t * 64 + g * 16 + 16, 0:256] for c in range(4)], axis=0
                )
                for g in range(4)
            ],
            axis=1,
        )
        grad_hidden = mm(down_t_ref[...], back)
        grad_pre = (grad_hidden * (sig * (1.0 + pre * (1.0 - sig)))).astype(BF)
        gb = gb + jnp.sum(grad_pre.astype(F32), axis=1, keepdims=True)
        gd = gd + mm_nt(back, hidden)
        part = mm_nt(win_ref[t], grad_pre)
        gc_ref[...] = part if t == 0 else gc_ref[...] + part
    rows = []
    for dy in range(3):
        for cx in range(4):
            r0, r1 = (dy * 4 + cx) * 64, ((dy + 1) * 4 + cx) * 64
            rows.append(gc_ref[r0 : r0 + 64, 0:128] + gc_ref[r1 : r1 + 64, 128:256])
    taps = []
    for dy in range(3):
        for dx in range(3):
            taps.append(rows[dy * 4 + dx] + pltpu.roll(rows[dy * 4 + dx + 1], 64, axis=1))
    groups = []
    for q in range(4):
        rows = jnp.concatenate(
            [tap[q * 16 : q * 16 + 16, :] for tap in taps] + [jnp.zeros((112, 128), F32)], axis=0
        )
        groups.append(jnp.concatenate([rows[0:128].T, rows[128:256].T], axis=1)[0:64, :])
    conv = mm(jnp.concatenate(halves(jnp.concatenate(groups, axis=0)), axis=0), conv_place_ref[...])
    down = mm(jnp.concatenate(halves(gd), axis=0), down_place_ref[...])
    gb = gb[0:64, :] + gb[64:128, :] + gb[128:192, :] + gb[192:256, :]
    bias = [h.astype(F32) for h in halves(gb)]
    lane16 = lane_row(1024)
    for part in range(2):
        for c in range(4):
            both = jnp.concatenate(
                [
                    conv[part * 256 + q * 64 + c * 16 : part * 256 + q * 64 + c * 16 + 16, :]
                    + down[part * 64 + q * 16 : part * 64 + q * 16 + 16, c * 256 : c * 256 + 256]
                    for q in range(4)
                ],
                axis=1,
            )
            both = jnp.where(lane16 == 208, bias[part][c * 16 : c * 16 + 16, :], both)
            sum_ref[c, 32 + part * 16 : 48 + part * 16, :] = both.astype(BF)
    for d in range(4):
        out_refs[d][...] = sum_ref[me ^ d]


def spread_body(me_ref, *refs):
    in_refs, out_ref, msg_ref = refs[0:4], refs[4], refs[5]
    for d in range(4):
        msg_ref[me_ref[0] ^ d] = in_refs[d][...]
    stack = jnp.concatenate(
        [msg_ref[c, 0:32, g * 256 : g * 256 + 256] for g in range(4) for c in range(4)], axis=0
    )
    row = down_col(512)
    source = (((row >> 3) & 3) << 7) | (((row >> 1) & 3) << 5) | ((row & 1) << 4) | (row >> 5)
    out_ref[:, 0:256] = mm(ones_where(lane_row(512) == source), stack).astype(BF)
    total = jnp.zeros((16, 1024), F32)
    for c in range(4):
        total = total + (msg_ref[c, 32:48, :].astype(F32) + msg_ref[c, 48:64, :].astype(F32))
    parts = [
        h[:, s * 256 + o : s * 256 + o + 128] for h in halves(total) for o in (0, 128) for s in range(4)
    ]
    stack = jnp.concatenate(parts, axis=0)
    r, p = row & 7, row >> 3
    source = jnp.where(r < 4, (r << 6) + p, -1)
    out_ref[:, 256:384] = mm(ones_where(lane_row(256) == source), stack).astype(BF)


def place_body(msg_ref, slot_ref, out_ref):
    quarter = msg_ref[:, 0:256]
    slot = slot_ref[0:1, :].astype(jnp.int32)
    row = down_col(512)
    lane = lane_row(256)
    half = row & 1
    li = down_col(256)
    to = (((li >> 5) & 3) << 6) | (li & 31)
    total = jnp.zeros((512, 256), F32)
    for qc in range(2):
        got = mm(ones_where(slot == ((row >> 1) << 1) + qc), quarter)
        total = total + mm(keep((lane >> 7) == half, got), ones_where(lane == to + qc * 32))
    out_ref[:, 0:256] = total.astype(BF)
    r = down_col(16)
    src = lane_row(512) & 7
    src = jnp.where(src < 4, src & 1, -1)
    summed = mm(ones_where(src == jnp.where(r < 4, r & 1, -2)), msg_ref[:, 256:384])
    high, low = halves(summed)
    both = jnp.where(iota((16, 128), 0) < 2, high.astype(F32), low.astype(F32)).astype(BF)
    r = row & 7
    out_ref[:, 256:384] = mm(ones_where(lane_row(16) == jnp.where(r < 4, r, -1)), both).astype(BF)


def finish_body(msg_ref, coarse_ref, conv_ref, down_ref, bias_ref):
    row = down_col(512)
    col = lane_row(512)
    qr, g, hf, a, k = row >> 8, (row >> 6) & 3, (row >> 5) & 1, (row >> 4) & 1, row & 15
    source = (k << 5) | (g << 3) | (a << 2) | (qr << 1) | hf
    got = mm(ones_where(col == source), msg_ref[:, 0:256]).astype(BF)
    for q in range(16):
        coarse_ref[:, q * 256 : q * 256 + 256] = got[q * 32 : q * 32 + 32, :]

    row = down_col(256)
    got = mm(ones_where(col == ((row & 63) << 3) + (row >> 6)), msg_ref[:, 256:384])
    value = jnp.concatenate([got[0:64] + got[128:192], got[64:128] + got[192:256]], axis=1)
    head = jnp.where(lane_row(256) < 144, value, 0.0)
    pad = jnp.zeros((16, 384), F32)
    conv = jnp.zeros((16, 640), F32)
    for q in range(4):
        part = jnp.concatenate([head[q * 16 : q * 16 + 16, :], pad], axis=1)
        conv = conv + (pltpu.roll(part, q * 144, axis=1) if q else part)
    conv_ref[...] = conv[:, 0:576]
    down_ref[...] = pltpu.roll(value, 112, axis=1)[:, 0:64]
    bias = value[0:16, 208:209]
    bias_ref[...] = jnp.sum(jnp.where(lane_row(16) == down_col(16), bias, 0.0), axis=0, keepdims=True)


def to_peers(parts):
    return [parts[0]] + [
        lax.ppermute(parts[d], "chan", [(i, i ^ d) for i in range(4)]) for d in range(1, 4)
    ]


def on_device(
    features,
    conv_weight,
    conv_bias,
    down_weight,
    cotangent,
    edge_links,
    edge_turns,
    corner_links,
    corner_turns,
    child_slot,
):
    vmem = pl.BlockSpec(memory_space=pltpu.VMEM)
    msg = jax.ShapeDtypeStruct(MSG, BF)

    def to_nodes(x):
        return lax.all_to_all(x.reshape(64, 8, 384), "tile", 0, 0, tiled=True).reshape(MSG)

    me = lax.axis_index("chan").astype(jnp.int32).reshape(1)
    scalar = pl.BlockSpec(memory_space=pltpu.SMEM)
    first = jax.ShapeDtypeStruct((16, 4096), BF)
    second = jax.ShapeDtypeStruct((16, 5632), BF)
    pieces, raw, *peers = call(
        send_body,
        (msg, jax.ShapeDtypeStruct((64, 384), BF)) + (first,) * 3 + (second,) * 3,
        (1,),
        [scalar, pl.BlockSpec(memory_space=pl.ANY), whole((32, 4096))]
        + [whole((4, 8))] * 4
        + [whole((1, 8)), whole((16, 576)), whole((1, 16)), whole((64, 64))],
        (vmem,) * 8,
        (pltpu.VMEM((128, 4096), BF), pltpu.SemaphoreType.DMA((1,))),
        flops=10**9,
        moved=2 * 10**6,
    )(
        me,
        *[
            pltpu.with_memory_space_constraint(x, pltpu.HBM)
            for x in (
                features.reshape(128, 4096),
                cotangent.reshape(32, 4096),
                edge_links.T,
                edge_turns.T,
                corner_links.T,
                corner_turns.T,
                child_slot.reshape(1, 8),
                conv_weight,
                conv_bias.reshape(1, 16),
                down_weight,
            )
        ],
    )
    first = to_peers([None] + peers[0:3])[1:]
    second = to_peers([None] + peers[3:6])[1:]
    pieces, first = lax.optimization_barrier((to_nodes(pieces), first))
    picked, slots = call(
        pick_body,
        (msg, jax.ShapeDtypeStruct((8, 512), F32)),
        (1,),
        [vmem],
        (vmem, vmem),
        flops=10**9,
        moved=10**6,
    )(pieces)
    picked = to_nodes(picked)
    own = pl.BlockSpec((32, 4096), lambda i, m: (m[0], 0))
    ready = pl.pallas_call(
        ready_body,
        out_shape=(
            jax.ShapeDtypeStruct((2, 1024, 1024), BF),
            jax.ShapeDtypeStruct((256, 1024), BF),
            jax.ShapeDtypeStruct((64, 256), BF),
            jax.ShapeDtypeStruct((256, 64), BF),
            jax.ShapeDtypeStruct((256, 128), F32),
            jax.ShapeDtypeStruct((4, 128, 1024), BF),
            jax.ShapeDtypeStruct((128, 512), BF),
            jax.ShapeDtypeStruct((256, 256), BF),
            jax.ShapeDtypeStruct((256, 1024), BF),
        ),
        grid_spec=pltpu.PrefetchScalarGridSpec(
            num_scalar_prefetch=1,
            grid=(1,),
            in_specs=[own] + [vmem] * 7,
            out_specs=(vmem,) * 9,
            scratch_shapes=(pltpu.VMEM((4, 32, 4096), BF), pltpu.VMEM((4, 64, 384), BF)),
        ),
        compiler_params=pltpu.CompilerParams(vmem_limit_bytes=32 << 20),
        cost_estimate=pl.CostEstimate(flops=10**9, bytes_accessed=4 * 10**6, transcendentals=0),
    )(me, features.reshape(128, 4096), raw, *first, *second)
    group = jax.ShapeDtypeStruct((128, 384), BF)
    picked = call(
        regroup_body,
        (group,) * 4,
        (1,),
        [scalar, vmem],
        (vmem,) * 4,
        flops=4 * 10**8,
        moved=10**6,
    )(me, picked)
    picked = to_peers(picked)
    local = pl.pallas_call(
        level_body,
        out_shape=(jax.ShapeDtypeStruct((64, 1024), BF),) * 4,
        in_specs=[scalar] + [vmem] * 13,
        out_specs=(vmem,) * 4,
        scratch_shapes=(
            pltpu.VMEM((4, 128, 384), BF),
            pltpu.VMEM((4, 64, 1024), BF),
            pltpu.VMEM((2, 1024, 1024), BF),
            pltpu.VMEM((1024, 256), F32),
        ),
        compiler_params=pltpu.CompilerParams(vmem_limit_bytes=32 << 20),
        cost_estimate=pl.CostEstimate(flops=4 * 10**9, bytes_accessed=4 * 10**6, transcendentals=0),
    )(me, *picked, *ready)
    local = to_peers(local)
    out = call(
        spread_body,
        msg,
        (1,),
        [scalar] + [vmem] * 4,
        vmem,
        (pltpu.VMEM((4, 64, 1024), BF),),
        flops=4 * 10**8,
        moved=10**6,
    )(me, *local)
    out = to_nodes(out)
    out = call(place_body, msg, (1,), [vmem, vmem], vmem, flops=5 * 10**8, moved=10**6)(
        out, slots
    )
    out = to_nodes(out)
    coarse, grad_conv, grad_down, grad_bias = call(
        finish_body,
        (
            jax.ShapeDtypeStruct((32, 4096), BF),
            jax.ShapeDtypeStruct((16, 576), F32),
            jax.ShapeDtypeStruct((64, 64), F32),
            jax.ShapeDtypeStruct((1, 16), F32),
        ),
        (1,),
        [vmem],
        (
            whole((32, 4096)),
            whole((16, 576)),
            whole((64, 64)),
            whole((1, 16)),
        ),
        flops=4 * 10**8,
        moved=10**6,
    )(out)
    return (coarse.reshape(2, 16, 4096), grad_conv, grad_bias.reshape(16), grad_down)


def solution(mesh):
    in_specs = (
        P("tile", "chan", None),
        P("chan", None),
        P("chan"),
        P(None, "chan"),
        P("tile", "chan", None),
        P("tile", None),
        P("tile", None),
        P("tile", None),
        P("tile", None),
        P("tile"),
    )
    out_specs = (P("tile", "chan", None), P("chan", None), P("chan"), P(None, "chan"))
    return jax.shard_map(
        on_device, mesh=mesh, in_specs=in_specs, out_specs=out_specs, check_vma=False
    )
```
